32 devices in a mesh: dp: 16 (over z, x, core), tensor: 2 (over y).
Axes of the slice: x: 2, y: 2, z: 4, core: 2. Of those that a mesh axis runs over, the one named last changes fastest.
Arguments:
- latents: bfloat16 [16384, 1536], P('dp'), may hold values from -6 to 6
- cotangent: bfloat16 [16384, 1536], P('dp'), may hold values from -8 to 8
- caption: bfloat16 [16, 256, 4096], P('dp'), may hold values from -6 to 6
- caption_lens: int32 [16], P('dp'), may hold values from 8 to 256, as said below
- patch_row: int32 [16, 1024], P('dp'), may hold values from 0 to 63, as said below
- patch_col: int32 [16, 1024], P('dp'), may hold values from 0 to 63, as said below
- timestep: int32 [16], P('dp'), may hold values from 0 to 999
- query_proj: bfloat16 [1536, 1536], P('dp', 'tensor'), may hold values from -0.15625 to 0.15625
- key_proj: bfloat16 [1536, 1536], P('dp', 'tensor'), may hold values from -0.15625 to 0.15625
- value_proj: bfloat16 [1536, 1536], P('dp', 'tensor'), may hold values from -0.15625 to 0.15625
- output_proj: bfloat16 [1536, 1536], P('tensor', 'dp'), may hold values from -0.625 to 0.625
- textkey_proj: bfloat16 [4096, 1536], P('dp', 'tensor'), may hold values from -0.09375 to 0.09375
- textval_proj: bfloat16 [4096, 1536], P('dp', 'tensor'), may hold values from -0.09375 to 0.09375
- gate_proj: bfloat16 [1536, 4096], P('dp', 'tensor'), may hold values from -0.15625 to 0.15625
- up_proj: bfloat16 [1536, 4096], P('dp', 'tensor'), may hold values from -0.15625 to 0.15625
- down_proj: bfloat16 [4096, 1536], P('tensor', 'dp'), may hold values from -0.09375 to 0.09375
- modulation: bfloat16 [1024, 6144], P('dp', 'tensor'), may hold values from -0.375 to 0.375
- attn_gain: bfloat16 [1536], P('dp'), may hold values from 0.5 to 1.5
- ffn_gain: bfloat16 [1536], P('dp'), may hold values from 0.5 to 1.5
- query_gain: bfloat16 [64], P('dp'), may hold values from 0.59765625 to 1.59375
- key_gain: bfloat16 [64], P('dp'), may hold values from 0.59765625 to 1.59375
- textkey_gain: bfloat16 [64], P('dp'), may hold values from 0.59765625 to 1.59375
- cross_gate: bfloat16 [24], P('tensor'), may hold values from -2.5 to 2.5
Outputs:
- output: bfloat16 [16384, 1536], P('dp')
- grad_latents: bfloat16 [16384, 1536], P('dp')
- grad_caption: bfloat16 [16, 256, 4096], P('dp', None, 'tensor')
- grad_embed: float32 [16, 1024], P('dp', 'tensor')
- grad_query: float32 [1536, 1536], P('dp', 'tensor')
- grad_key: float32 [1536, 1536], P('dp', 'tensor')
- grad_value: float32 [1536, 1536], P('dp', 'tensor')
- grad_output: float32 [1536, 1536], P('tensor', 'dp')
- grad_textkey: float32 [4096, 1536], P('dp', 'tensor')
- grad_textval: float32 [4096, 1536], P('dp', 'tensor')
- grad_gate: float32 [1536, 4096], P('dp', 'tensor')
- grad_up: float32 [1536, 4096], P('dp', 'tensor')
- grad_down: float32 [4096, 1536], P('tensor', 'dp')
- grad_modul: float32 [1024, 6144], P('dp', 'tensor')
- grad_attngain: float32 [1536], P('dp')
- grad_ffngain: float32 [1536], P('dp')
- grad_qgain: float32 [64], P('dp')
- grad_kgain: float32 [64], P('dp')
- grad_tkgain: float32 [64], P('dp')
- grad_xgate: float32 [24], P('tensor')
The draws below stay inside these ranges and needn't reach their ends.
Inputs may be any that keep to these rules, and one draw needn't show every extreme that they name: `caption_lens`: at least one image uses all 256 caption slots. `patch_row`: each image's 1024 patches form a grid of H rows and 1024 / H columns in row-major order, H one of 16, 32, 64; patch_col gives the column in the same grid. `patch_col`: the column in the grid that patch_row describes.
All inputs are finite; a program needn't handle non-finite values.
Results may differ from the reference program's by a relative error of at most 0.04.
Values may be sent and summed in bfloat16 or wider, within the bound.
No kernel may reach another device: no remote copies, remote signals or barrier semaphores. Data moves between devices by JAX's collectives and lax.ppermute only.
A program may use at most 448 MiB of HBM per device.

```python
import math
import jax
import jax.numpy as jnp
from jax import lax

D = 1536
HEADS = 24
HD = 64
FF = 4096
CAP = 4096
TDIM = 1024
CAPLEN = 256
SIDE = 32
SEQ = 1024
IMAGES = 16
TOKENS = 16384
N_TENSOR = 2


def draw_caption_lens(key, part):
    drawn_lens = jax.random.randint(jax.random.fold_in(key, 11), (IMAGES,), 8, CAPLEN + 1)
    longest = jax.random.randint(jax.random.fold_in(key, 12), (), 0, IMAGES)
    return jnp.where(jnp.arange(IMAGES) == longest, CAPLEN, drawn_lens).astype(jnp.int32)


def patch_grid(key):
    choose = jax.random.randint(jax.random.fold_in(key, 21), (IMAGES,), 0, 3)
    tallest = jax.random.randint(jax.random.fold_in(key, 22), (), 0, IMAGES)
    offset = jax.random.randint(jax.random.fold_in(key, 23), (), 1, IMAGES)
    widest = (tallest + offset) % IMAGES
    index_img = jnp.arange(IMAGES)
    choose = jnp.where(index_img == tallest, 2, jnp.where(index_img == widest, 0, choose))
    height = jnp.where(choose == 0, SIDE // 2, jnp.where(choose == 1, SIDE, 2 * SIDE))
    across = SEQ // height
    position = jnp.arange(SEQ)[None, :]
    return ((position // across[:, None]).astype(jnp.int32), (position % across[:, None]).astype(jnp.int32))


def draw_patch_row(key, part):
    return patch_grid(key)[0]


def draw_patch_col(key, part):
    return patch_grid(key)[1]


def plant(array, key, smallest, largest):
    extent = array.shape
    spot = [jax.random.randint(jax.random.fold_in(key, axis), (), 0, extent[axis]) for axis in range(len(extent))]
    array = array.at[tuple(spot)].set(smallest)
    longest = extent.index(max(extent))
    spot[longest] = (spot[longest] + 1) % extent[longest]
    return array.at[tuple(spot)].set(largest)


def raised(array, key, source, target, blocks, factor):
    def block_of(axis_at):
        return (jnp.arange(array.shape[axis_at]) // (array.shape[axis_at] // blocks)).reshape((-1,) + (1,) * (array.ndim - 1 - axis_at))

    first = jax.random.permutation(key, blocks)[block_of(target)]
    other_side = (block_of(target) + blocks // 2) % blocks
    return jnp.where((block_of(source) == first) | (block_of(source) == other_side), factor * array, array)


def levels(own_key, extent, pieces, low, top_value):
    gain = 1.0
    for axis_at, blocks in pieces:
        draws = jax.random.uniform(jax.random.fold_in(jax.random.fold_in(own_key, 6), axis_at), (blocks,), jnp.float32, low / len(pieces), top_value / len(pieces))
        gain = gain * jnp.repeat(jnp.exp(draws), extent[axis_at] // blocks).reshape((-1,) + (1,) * (len(extent) - 1 - axis_at))
    return gain


def centred(stream_key, extent, scale, bound, shards=(), kind=jnp.bfloat16):
    array = scale * jax.random.normal(stream_key, extent, jnp.float32)
    if shards:
        array = array * levels(stream_key, extent, shards, -0.22, 0.18)
    return jnp.clip(array, -bound, bound).astype(kind)


def bell_draw_with(key, dims, width, bound, split, heavy, held_as=jnp.bfloat16):
    values = width * jax.random.normal(key, dims, jnp.float32)
    if split:
        values = values * levels(key, dims, split, -0.22, 0.18)
    return jnp.clip(raised(values, jax.random.fold_in(key, 3), *heavy), -bound, bound).astype(held_as)


def setup_inputs(seed: int = 0) -> dict:
    streams_of = jax.random.split(jax.random.key(seed), 24)
    latents = centred(streams_of[0], (TOKENS, D), 1.0, 6.0, ((0, 16),))
    cotangent = bell_draw_with(streams_of[1], (TOKENS, D), 1.0, 8.0, ((0, 16),), (0, 1, 16, 2.0))
    caption = centred(streams_of[2], (IMAGES, CAPLEN, CAP), 1.0, 6.0, ((0, 16),))
    caption_lens = draw_caption_lens(jax.random.fold_in(streams_of[23], 71), 0)
    patch_row = draw_patch_row(jax.random.fold_in(streams_of[23], 71), 0)
    patch_col = draw_patch_col(jax.random.fold_in(streams_of[23], 71), 0)
    timestep = plant(jax.random.randint(streams_of[6], (IMAGES,), 0, 1000), jax.random.fold_in(streams_of[6], 1), 0, 999).astype(jnp.int32)
    query_proj = centred(streams_of[7], (D, D), D ** -0.5, 0.15625, ((0, 16), (1, 2)))
    key_proj = centred(streams_of[8], (D, D), D ** -0.5, 0.15625, ((0, 16), (1, 2)))
    value_proj = centred(streams_of[9], (D, D), D ** -0.5, 0.15625, ((0, 16), (1, 2)))
    output_proj = centred(streams_of[10], (D, D), (D // 16) ** -0.5, 0.625, ((0, 2), (1, 16)))
    textkey_proj = centred(streams_of[11], (CAP, D), CAP ** -0.5, 0.09375, ((0, 16), (1, 2)))
    textval_proj = centred(streams_of[12], (CAP, D), CAP ** -0.5, 0.09375, ((0, 16), (1, 2)))
    gate_proj = centred(streams_of[13], (D, FF), D ** -0.5, 0.15625, ((0, 16), (1, 2)))
    up_proj = centred(streams_of[14], (D, FF), D ** -0.5, 0.15625, ((0, 16), (1, 2)))
    down_proj = centred(streams_of[15], (FF, D), FF ** -0.5, 0.09375, ((0, 2), (1, 16)))
    modulation = centred(streams_of[16], (TDIM, 4 * D), (TDIM // 4) ** -0.5, 0.375, ((0, 16), (1, 2)))
    attn_gain = jnp.clip(0.5 + 1.0 * jax.random.uniform(streams_of[17], (D,), jnp.float32) ** levels(streams_of[17], (D,), ((0, 16),), -0.2, 0.2), 0.5, 1.5).astype(jnp.bfloat16)
    ffn_gain = jnp.clip(0.5 + 1.0 * jax.random.uniform(streams_of[18], (D,), jnp.float32) ** levels(streams_of[18], (D,), ((0, 16),), -0.2, 0.2), 0.5, 1.5).astype(jnp.bfloat16)
    query_gain = jnp.clip(0.59765625 + 0.99609375 * jax.random.uniform(streams_of[19], (HD,), jnp.float32) ** levels(streams_of[19], (HD,), ((0, 16),), -0.2, 0.2), 0.59765625, 1.59375).astype(jnp.bfloat16)
    key_gain = jnp.clip(0.59765625 + 0.99609375 * jax.random.uniform(streams_of[20], (HD,), jnp.float32) ** levels(streams_of[20], (HD,), ((0, 16),), -0.2, 0.2), 0.59765625, 1.59375).astype(jnp.bfloat16)
    textkey_gain = jnp.clip(0.59765625 + 0.99609375 * jax.random.uniform(streams_of[21], (HD,), jnp.float32) ** levels(streams_of[21], (HD,), ((0, 16),), -0.2, 0.2), 0.59765625, 1.59375).astype(jnp.bfloat16)
    cross_gate = centred(streams_of[22], (HEADS,), 0.8, 2.5, ((0, 2),))
    return {"latents": latents, "cotangent": cotangent, "caption": caption, "caption_lens": caption_lens, "patch_row": patch_row, "patch_col": patch_col, "timestep": timestep, "query_proj": query_proj, "key_proj": key_proj, "value_proj": value_proj, "output_proj": output_proj, "textkey_proj": textkey_proj, "textval_proj": textval_proj, "gate_proj": gate_proj, "up_proj": up_proj, "down_proj": down_proj, "modulation": modulation, "attn_gain": attn_gain, "ffn_gain": ffn_gain, "query_gain": query_gain, "key_gain": key_gain, "textkey_gain": textkey_gain, "cross_gate": cross_gate}


@jax.custom_vjp
def low(v):
    return lax.optimization_barrier(v.astype(jnp.bfloat16)).astype(jnp.float32)

@jax.custom_vjp
def low_back(v):
    return v

def low_keep(v):
    return (low(v), None)

def low_pass(kept, grad):
    return (grad,)

def back_keep(v):
    return (v, None)

def back_low(kept, grad):
    return (low(grad),)
low.defvjp(low_keep, low_pass)
low_back.defvjp(back_keep, back_low)
EPSILON = 1e-06
HIGHEST = lax.Precision.HIGHEST

def matmul(left, right):
    return jnp.dot(left, right, precision=HIGHEST, preferred_element_type=jnp.float32)

def inv_rms(values):
    return lax.rsqrt(lax.optimization_barrier(jnp.mean(values * values, axis=-1, keepdims=True)) + EPSILON)

def rotary(values, row_pos, col_pos, direction):
    quarter = values.shape[-1] // 4
    frequency = jnp.exp(-math.log(10000.0) * jnp.arange(quarter, dtype=jnp.float32) / quarter)
    angles = jnp.concatenate([row_pos.astype(jnp.float32)[:, None] * frequency, col_pos.astype(jnp.float32)[:, None] * frequency], axis=1)[:, None, :]
    cosine = jnp.cos(angles)
    sine_part = direction * jnp.sin(angles)
    first_half = values[..., :2 * quarter]
    second = values[..., 2 * quarter:]
    return jnp.concatenate([first_half * cosine - second * sine_part, first_half * sine_part + second * cosine], axis=-1)

def time_embed(step_vals, embed_width):
    half_width = embed_width // 2
    frequency = jnp.exp(-math.log(10000.0) * jnp.arange(half_width, dtype=jnp.float32) / half_width)
    phases = step_vals.astype(jnp.float32)[:, None] * frequency
    return jnp.concatenate([jnp.cos(phases), jnp.sin(phases)], axis=1)

def softmax_rows(scores):
    row_max = lax.optimization_barrier(jnp.max(scores, axis=-1, keepdims=True))
    exp_scores = jnp.exp(scores - row_max)
    return exp_scores / lax.optimization_barrier(jnp.sum(exp_scores, axis=-1, keepdims=True))

def shard_sum(left, right, groups):
    row_count = left.shape[0]
    inner = right.shape[0] // groups
    parts = jnp.einsum('rgc,gcd->grd', left.reshape(row_count, groups, inner), right.reshape(groups, inner, right.shape[1]), precision=HIGHEST)
    return low_back(lax.optimization_barrier(jnp.sum(low(parts), axis=0)))

def one_layer(params, image_in, caption_in, mod_row, cap_count, row_pos, col_pos):
    query_proj, key_proj, value_proj, output_proj, textkey_proj, textval_proj, gate_proj, up_proj, down_proj, modulation, attn_gain, ffn_gain, query_gain, key_gain, textkey_gain, cross_gate = params
    length, model_dim = image_in.shape
    head_dim = query_gain.shape[0]
    heads_all = model_dim // head_dim
    scale_one = mod_row[0:model_dim]
    gate_one = jnp.tanh(mod_row[model_dim:2 * model_dim])
    scale_two = mod_row[2 * model_dim:3 * model_dim]
    gate_two = jnp.tanh(mod_row[3 * model_dim:4 * model_dim])
    normed_one = image_in * inv_rms(image_in)
    attn_in = low(normed_one * attn_gain * (1.0 + scale_one))
    query_raw = low_back(matmul(attn_in, query_proj)).reshape(length, heads_all, head_dim)
    key_raw = low_back(matmul(attn_in, key_proj)).reshape(length, heads_all, head_dim)
    values_in = low_back(low(matmul(attn_in, value_proj))).reshape(length, heads_all, head_dim)
    query_in = low_back(low(rotary(query_raw * inv_rms(query_raw) * query_gain, row_pos, col_pos, 1.0)))
    key_in = low_back(low(rotary(key_raw * inv_rms(key_raw) * key_gain, row_pos, col_pos, 1.0)))
    text_raw = low_back(matmul(caption_in, textkey_proj)).reshape(CAPLEN, heads_all, head_dim)
    tkeys_in = low_back(low(text_raw * inv_rms(text_raw) * textkey_gain))
    tvals_in = low_back(low(matmul(caption_in, textval_proj))).reshape(CAPLEN, heads_all, head_dim)
    scaling = head_dim ** (-0.5)
    scores = low_back(jnp.einsum('qhd,khd->hqk', query_in, key_in, precision=HIGHEST) * scaling)
    own_out = jnp.einsum('hqk,khd->qhd', low(softmax_rows(scores)), values_in, precision=HIGHEST)
    keep_mask = jnp.arange(CAPLEN) < cap_count
    cross_scores = low_back(jnp.einsum('qhd,khd->hqk', query_in, tkeys_in, precision=HIGHEST) * scaling)
    cross_scores = jnp.where(keep_mask[None, None, :], cross_scores, -1e+30)
    cross_out = low_back(jnp.einsum('hqk,khd->qhd', low(softmax_rows(cross_scores)), tvals_in, precision=HIGHEST))
    mixed_heads = low_back(low(own_out + jnp.tanh(cross_gate)[:, None] * cross_out)).reshape(length, model_dim)
    attn_out = shard_sum(mixed_heads, output_proj, N_TENSOR)
    residual = image_in + gate_one * attn_out
    ffn_in = low(residual * inv_rms(residual) * ffn_gain * (1.0 + scale_two))
    gate_pre = low_back(matmul(ffn_in, gate_proj))
    up_pre = low_back(matmul(ffn_in, up_proj))
    hidden = low(gate_pre * jax.nn.sigmoid(gate_pre) * up_pre)
    ffn_out = shard_sum(hidden, down_proj, N_TENSOR)
    return residual + gate_two * ffn_out

def reference(latents, cotangent, caption, caption_lens, patch_row, patch_col, timestep, query_proj, key_proj, value_proj, output_proj, textkey_proj, textval_proj, gate_proj, up_proj, down_proj, modulation, attn_gain, ffn_gain, query_gain, key_gain, textkey_gain, cross_gate):
    params = tuple((weight.astype(jnp.float32) for weight in (query_proj, key_proj, value_proj, output_proj, textkey_proj, textval_proj, gate_proj, up_proj, down_proj, modulation, attn_gain, ffn_gain, query_gain, key_gain, textkey_gain, cross_gate)))
    image_all = latents.astype(jnp.float32).reshape(IMAGES, SEQ, D)
    caption_all = caption.astype(jnp.float32)
    embedding = time_embed(timestep, TDIM)

    def forward(image_set, caption_set, embed_in, weights):
        cond = low(embed_in * jax.nn.sigmoid(embed_in))
        mod_all = low_back(matmul(cond, weights[9]))

        def per_image(item_in):
            return one_layer(weights, *item_in)
        return lax.map(jax.checkpoint(per_image), (image_set, caption_set, mod_all, caption_lens, patch_row, patch_col))
    result, pullback = jax.vjp(forward, image_all, caption_all, embedding, params)
    grad_image, grad_text, grad_embed, grads = pullback(cotangent.astype(jnp.float32).reshape(IMAGES, SEQ, D))
    return (result.reshape(TOKENS, D).astype(jnp.bfloat16), grad_image.reshape(TOKENS, D).astype(jnp.bfloat16), grad_text.astype(jnp.bfloat16), grad_embed, grads[0], grads[1], grads[2], grads[3], grads[4], grads[5], grads[6], grads[7], grads[8], grads[9], grads[10], grads[11], grads[12], grads[13], grads[14], grads[15])
```

```python
import functools
import math

import jax
import jax.numpy as jnp
from jax import lax
from jax.experimental import pallas as pl
from jax.experimental.pallas import tpu as pltpu
from jax.sharding import PartitionSpec as P

EPSILON = 1e-06


def inv_rms(values):
    return lax.rsqrt(jnp.mean(values * values, axis=-1, keepdims=True) + EPSILON)


def time_embed(step_vals, embed_width):
    half_width = embed_width // 2
    frequency = jnp.exp(-math.log(10000.0) * jnp.arange(half_width, dtype=jnp.float32) / half_width)
    phases = step_vals.astype(jnp.float32)[:, None] * frequency
    return jnp.concatenate([jnp.cos(phases), jnp.sin(phases)], axis=1)


def norm_back(grad_hat, normed, factor):
    return factor * (grad_hat - normed * jnp.mean(grad_hat * normed, axis=-1, keepdims=True))


LANES = 128


def lane_ids(rows):
    return lax.broadcasted_iota(jnp.int32, (rows, LANES), 1)


def pair_matrix(same, half):
    row = lax.broadcasted_iota(jnp.int32, (LANES, LANES), 0) // half
    col = lax.broadcasted_iota(jnp.int32, (LANES, LANES), 1) // half
    return jnp.where((row == col) == same, 1.0, 0.0).astype(jnp.bfloat16)


def head_sums(values, matrix):
    high = values.astype(jnp.bfloat16)
    low = (values - high.astype(jnp.float32)).astype(jnp.bfloat16)
    return jnp.dot(high, matrix, preferred_element_type=jnp.float32) + jnp.dot(
        low, matrix, preferred_element_type=jnp.float32
    )


def swap_quarters(values, half):
    rows = values.shape[0]
    first = lane_ids(rows) % half < half // 2
    return jnp.where(
        first,
        pltpu.roll(values, LANES - half // 2, 1),
        pltpu.roll(values, half // 2, 1),
    )


def nt_dot(left, right):
    return lax.dot_general(
        left, right, (((1,), (1,)), ((), ())), preferred_element_type=jnp.float32
    )


def tn_dot(left, right):
    return lax.dot_general(
        left, right, (((0,), (0,)), ((), ())), preferred_element_type=jnp.float32
    )


def attend_kernel(
    half,
    block,
    len_ref,
    raw_ref,
    text_ref,
    cos_ref,
    sin_ref,
    gain_ref,
    tanh_ref,
    mixed_ref,
    qkv_ref,
    tkv_ref,
    own_ref,
    cross_ref,
    lse_ref,
):
    f32, bf16 = jnp.float32, jnp.bfloat16
    rows = raw_ref.shape[0]
    matrix = pair_matrix(True, half)

    def hat(raw):
        return raw * lax.rsqrt(head_sums(raw * raw, matrix) * (1.0 / half) + EPSILON)

    def turned(raw, gain):
        value = hat(raw) * gain
        return (value * cos_ref[...] + swap_quarters(value, half) * sin_ref[...]).astype(bf16)

    query = turned(raw_ref[:, :LANES], gain_ref[0:1])
    key = turned(raw_ref[:, LANES : 2 * LANES], gain_ref[1:2])
    value = raw_ref[:, 2 * LANES :].astype(bf16)
    tkey = (hat(text_ref[:, :LANES]) * gain_ref[2:3]).astype(bf16)
    tval = text_ref[:, LANES:].astype(bf16)
    qkv_ref[:, :LANES] = query
    qkv_ref[:, LANES : 2 * LANES] = key
    qkv_ref[:, 2 * LANES :] = value
    tkv_ref[:, :LANES] = tkey
    tkv_ref[:, LANES:] = tval
    one = jnp.ones((), bf16)
    zero = jnp.zeros((), bf16)

    def pick(a, b):
        return jnp.where(lane_ids(a.shape[0]) < half, a, b)

    def fill(a, fillers, first):
        other = jnp.full(a.shape, fillers, bf16)
        return pick(a, other) if first else pick(other, a)

    value_ones = [fill(value, one, True), fill(value, one, False)]
    tval_ones = [fill(tval, one, True), fill(tval, one, False)]
    keep = lax.broadcasted_iota(jnp.int32, (block, tkey.shape[0]), 1) < len_ref[0]

    def step(i, _):
        here = pl.ds(pl.multiple_of(i * block, block), block)
        q_blk = qkv_ref[here, :LANES] * jnp.asarray(half**-0.5, bf16)
        outs = []
        texts = []
        for head in range(2):
            q_one = fill(q_blk, zero, head == 0)
            e_self = jnp.exp(nt_dot(q_one, key)).astype(bf16)
            outs.append(jnp.dot(e_self, value_ones[head], preferred_element_type=f32))
            e_text = jnp.where(keep, jnp.exp(nt_dot(q_one, tkey)), 0.0).astype(bf16)
            texts.append(jnp.dot(e_text, tval_ones[head], preferred_element_type=f32))
        for n, (a, b) in enumerate((outs, texts)):
            total = pick(b, a)
            lse_ref[here, n * LANES : (n + 1) * LANES] = jnp.log(total)
            res = pick(a, b) / pltpu.roll(total, half, 1)
            if n == 0:
                own = res
                own_ref[here, :] = res
            else:
                cross_ref[here, :] = res
                mixed_ref[here, :] = (own + tanh_ref[0:1] * res).astype(bf16)
        return 0

    lax.fori_loop(0, rows // block, step, 0)


def attend_pairs(cap_len, raw, text, cosine, sine, gains, tanh_lanes, half):
    rows = raw.shape[0]
    pairs = raw.shape[1] // (3 * LANES)
    caps = text.shape[0]
    width = pairs * LANES
    f32, bf16 = jnp.float32, jnp.bfloat16
    col = lambda n, w: pl.BlockSpec((n, w), lambda p: (0, p))
    fix = lambda n: pl.BlockSpec((n, LANES), lambda p: (0, 0))
    return pl.pallas_call(
        functools.partial(attend_kernel, half, min(256, rows)),
        grid=(pairs,),
        in_specs=[
            pl.BlockSpec(memory_space=pltpu.SMEM),
            col(rows, 3 * LANES),
            col(caps, 2 * LANES),
            fix(rows),
            fix(rows),
            fix(8),
            col(8, LANES),
        ],
        out_specs=[
            col(rows, LANES),
            col(rows, 3 * LANES),
            col(caps, 2 * LANES),
            col(rows, LANES),
            col(rows, LANES),
            col(rows, 2 * LANES),
        ],
        out_shape=[
            jax.ShapeDtypeStruct((rows, width), bf16),
            jax.ShapeDtypeStruct((rows, 3 * width), bf16),
            jax.ShapeDtypeStruct((caps, 2 * width), bf16),
            jax.ShapeDtypeStruct((rows, width), f32),
            jax.ShapeDtypeStruct((rows, width), f32),
            jax.ShapeDtypeStruct((rows, 2 * width), f32),
        ],
        compiler_params=pltpu.CompilerParams(vmem_limit_bytes=50 * 2**20),
        name="attend_fwd",
    )(cap_len, raw, text, cosine, sine, gains, tanh_lanes)


def attend_back_kernel(
    half,
    block,
    len_ref,
    qkv_ref,
    tkv_ref,
    raw_ref,
    text_ref,
    own_ref,
    cross_ref,
    lse_ref,
    dmix_ref,
    cos_ref,
    sin_ref,
    gain_ref,
    tanh_ref,
    dqkv_ref,
    dtext_ref,
    stat_ref,
    qs_ref,
    os_ref,
    cq_ref,
    oc_ref,
    dq_ref,
    dk_ref,
    dv_ref,
    dtk_ref,
    dtv_ref,
):
    f32, bf16 = jnp.float32, jnp.bfloat16
    rows = raw_ref.shape[0]
    same = pair_matrix(True, half)
    cross_matrix = pair_matrix(False, half)

    def pick(a, b):
        return jnp.where(lane_ids(a.shape[0]) < half, a, b)

    def parts(value):
        spot = lane_ids(rows) % half
        high = value.astype(bf16).astype(f32)
        rest = value - high
        mid = rest.astype(bf16).astype(f32)
        low = rest - mid
        return jnp.where(
            spot == 0, high, jnp.where(spot == 1, mid, jnp.where(spot == 2, low, 0.0))
        ).astype(bf16)

    def ones_like_parts(value):
        return jnp.where(lane_ids(value.shape[0]) % half < 3, 1.0, 0.0).astype(bf16)

    grad = dmix_ref[...]
    grad_f = grad.astype(f32)
    other_f = (grad_f * tanh_ref[0:1]).astype(bf16).astype(f32)
    other = other_f.astype(bf16)
    delta_s = parts(-head_sums(grad_f * own_ref[...], cross_matrix))
    delta_c = parts(-head_sums(other_f * cross_ref[...], cross_matrix))
    lse_s = parts(-lse_ref[:, :LANES])
    lse_c = parts(-lse_ref[:, LANES:])
    query = qkv_ref[:, :LANES] * jnp.asarray(half**-0.5, bf16)
    key = qkv_ref[:, LANES : 2 * LANES]
    value = qkv_ref[:, 2 * LANES :]
    tkey = tkv_ref[:, :LANES]
    tval = tkv_ref[:, LANES:]
    for head in range(2):
        aug = (lambda a, b: pick(a, b)) if head == 0 else (lambda a, b: pick(b, a))
        qs_ref[head] = aug(query, lse_s)
        cq_ref[head] = aug(query, lse_c)
        os_ref[head] = aug(grad, delta_s)
        oc_ref[head] = aug(other, delta_c)
    zero = jnp.zeros((), bf16)

    def only(a, head):
        blank = jnp.full(a.shape, zero, bf16)
        return pick(a, blank) if head == 0 else pick(blank, a)

    def aug_ones(a, head):
        ones = ones_like_parts(a)
        return pick(a, ones) if head == 0 else pick(ones, a)

    key_aug = [aug_ones(key, h) for h in range(2)]
    val_aug = [aug_ones(value, h) for h in range(2)]
    tkey_aug = [aug_ones(tkey, h) for h in range(2)]
    tval_aug = [aug_ones(tval, h) for h in range(2)]
    key_only = [only(key, h) for h in range(2)]
    tkey_only = [only(tkey, h) for h in range(2)]
    dk_ref[...] = jnp.zeros_like(dk_ref)
    dv_ref[...] = jnp.zeros_like(dv_ref)
    dtk_ref[...] = jnp.zeros_like(dtk_ref)
    dtv_ref[...] = jnp.zeros_like(dtv_ref)
    caps = tkey.shape[0]
    keep = lax.broadcasted_iota(jnp.int32, (caps, block), 0) < len_ref[0]

    def step(i, _):
        here = pl.ds(pl.multiple_of(i * block, block), block)
        dq = jnp.zeros((block, LANES), f32)
        for head in range(2):
            q_aug, o_aug = qs_ref[head, here], os_ref[head, here]
            q_only, o_only = only(q_aug, head), only(o_aug, head)
            probs = jnp.exp(nt_dot(key_aug[head], q_aug))
            grads = (probs * nt_dot(val_aug[head], o_aug)).astype(bf16)
            dv_ref[...] += jnp.dot(probs.astype(bf16), o_only, preferred_element_type=f32)
            dk_ref[...] += jnp.dot(grads, q_only, preferred_element_type=f32)
            dq += tn_dot(grads, key_only[head])
            q_aug, o_aug = cq_ref[head, here], oc_ref[head, here]
            o_only = only(o_aug, head)
            probs = jnp.where(keep, jnp.exp(nt_dot(tkey_aug[head], q_aug)), 0.0)
            grads = (probs * nt_dot(tval_aug[head], o_aug)).astype(bf16)
            dtv_ref[...] += jnp.dot(probs.astype(bf16), o_only, preferred_element_type=f32)
            dtk_ref[...] += jnp.dot(grads, q_only, preferred_element_type=f32)
            dq += tn_dot(grads, tkey_only[head])
        dq_ref[here, :] = dq * half**-0.5
        return 0

    lax.fori_loop(0, rows // block, step, 0)

    def bring_back(grad_in, raw, gain, rotate):
        inv = lax.rsqrt(head_sums(raw * raw, same) * (1.0 / half) + EPSILON)
        normed = raw * inv
        turn = grad_in.astype(bf16).astype(f32)
        if rotate:
            turn = turn * cos_ref[...] - swap_quarters(turn, half) * sin_ref[...]
        scaled = turn * gain
        mean = head_sums(scaled * normed, same) * (1.0 / half)
        return (inv * (scaled - normed * mean)).astype(bf16), jnp.sum(
            turn * normed, axis=0, keepdims=True
        )

    res, stat_q = bring_back(dq_ref[...], raw_ref[:, :LANES], gain_ref[0:1], True)
    dqkv_ref[:, :LANES] = res
    res, stat_k = bring_back(dk_ref[...], raw_ref[:, LANES : 2 * LANES], gain_ref[1:2], True)
    dqkv_ref[:, LANES : 2 * LANES] = res
    dqkv_ref[:, 2 * LANES :] = dv_ref[...].astype(bf16)
    res, stat_t = bring_back(dtk_ref[...], text_ref[:, :LANES], gain_ref[2:3], False)
    dtext_ref[:, :LANES] = res
    dtext_ref[:, LANES:] = dtv_ref[...].astype(bf16)
    stat_x = jnp.sum(grad_f * cross_ref[...], axis=0, keepdims=True)
    stat_ref[...] = jnp.concatenate(
        [stat_q, stat_k, stat_t, stat_x, jnp.zeros((4, LANES), f32)], axis=0
    )


def attend_back_pairs(window, arrays, tables, half):
    cap_len, qkv, tkv, raw, text, own, cross, lse, dmix = arrays
    cosine, sine, gains, tanh_lanes = tables
    first, pairs = window
    rows, caps = raw.shape[0], text.shape[0]
    width = pairs * LANES
    f32, bf16 = jnp.float32, jnp.bfloat16

    def col(n, w):
        return pl.BlockSpec((n, w), lambda p: (0, p + first))

    def out(n, w):
        return pl.BlockSpec((n, w), lambda p: (0, p))

    def fix(n):
        return pl.BlockSpec((n, LANES), lambda p: (0, 0))

    return pl.pallas_call(
        functools.partial(attend_back_kernel, half, min(512, rows)),
        grid=(pairs,),
        in_specs=[
            pl.BlockSpec(memory_space=pltpu.SMEM),
            col(rows, 3 * LANES),
            col(caps, 2 * LANES),
            col(rows, 3 * LANES),
            col(caps, 2 * LANES),
            col(rows, LANES),
            col(rows, LANES),
            col(rows, 2 * LANES),
            col(rows, LANES),
            fix(rows),
            fix(rows),
            fix(8),
            col(8, LANES),
        ],
        out_specs=[out(rows, 3 * LANES), out(caps, 2 * LANES), out(8, LANES)],
        out_shape=[
            jax.ShapeDtypeStruct((rows, 3 * width), bf16),
            jax.ShapeDtypeStruct((caps, 2 * width), bf16),
            jax.ShapeDtypeStruct((8, width), f32),
        ],
        scratch_shapes=[pltpu.VMEM((2, rows, LANES), bf16)] * 4
        + [pltpu.VMEM((rows, LANES), f32)] * 3
        + [pltpu.VMEM((caps, LANES), f32)] * 2,
        compiler_params=pltpu.CompilerParams(vmem_limit_bytes=50 * 2**20),
        name="attend_bwd",
    )(cap_len, qkv, tkv, raw, text, own, cross, lse, dmix, cosine, sine, gains, tanh_lanes)


def gated(value, *tokens):
    return lax.optimization_barrier((value,) + tokens)[0]


def chip_ring(size):
    depth = size // 4
    return [2 * q if q < depth else 2 * (2 * depth - 1 - q) + 1 for q in range(size // 2)]


def ring_perm(size, step):
    order = chip_ring(size)
    count = len(order)
    return [
        (order[q] * 2 + c, order[(q + step) % count] * 2 + c) for q in range(count) for c in range(2)
    ]


def flip_perm(size, bit):
    return [(i, i ^ bit) for i in range(size)]


def ring_place(size):
    depth = size // 4
    index = lax.axis_index("dp")
    chip = index // 2
    level = chip // 2
    return jnp.where(chip % 2 == 0, level, 2 * depth - 1 - level), index % 2


def chip_at(place, size):
    depth = size // 4
    place = place % (2 * depth)
    return jnp.where(place < depth, 2 * place, 2 * (2 * depth - 1 - place) + 1)


def ring_gather(shard, size):
    count = size // 2
    rows, cols = shard.shape
    half = cols // 2
    place, core = ring_place(size)
    swap = flip_perm(size, 1)
    ahead, behind = ring_perm(size, 1), ring_perm(size, -1)
    pieces = [(0, 0, shard)]
    fwd = bwd = shard
    marks = []
    for step in range(1, count // 2):
        fwd = lax.ppermute(fwd, "dp", ahead)
        bwd = lax.ppermute(bwd, "dp", behind)
        pieces += [(-step, 0, fwd), (step, 0, bwd)]
        marks.append(fwd)
    last_f = lax.ppermute(fwd[:, :half], "dp", ahead)
    last_b = lax.ppermute(bwd[:, half:], "dp", behind)
    pieces += [(count // 2, 0, last_f), (count // 2, half, last_b)]
    marks.append(last_f)
    full = jnp.zeros((count, 2, rows, cols), shard.dtype)
    for offset, low, piece in pieces:
        other = lax.ppermute(piece, "dp", swap)
        chip = chip_at(place + offset, size)
        full = lax.dynamic_update_slice(full, piece[None, None], (chip, core, 0, low))
        full = lax.dynamic_update_slice(full, other[None, None], (chip, 1 - core, 0, low))
    return full.reshape(size * rows, cols), marks


def split_cols(left, size):
    rows, cols = left.shape
    blocks = left.reshape(rows, size // 2, 2, cols // size)
    core = lax.axis_index("dp") % 2
    mine = lax.dynamic_index_in_dim(blocks, core, 2, keepdims=False).reshape(rows, cols // 2)
    other = lax.dynamic_index_in_dim(blocks, 1 - core, 2, keepdims=False).reshape(rows, cols // 2)
    return mine, other


def core_away(parts, right, size):
    away = jnp.einsum("rm,rc->mc", parts[1], right, preferred_element_type=jnp.float32)
    away = away.astype(jnp.bfloat16)
    return away, lax.ppermute(away, "dp", flip_perm(size, 1))


def core_keep(parts, right, came, size):
    kept = jnp.einsum("rm,rc->mc", parts[0], right, preferred_element_type=jnp.float32)
    kept = (kept + came.astype(jnp.float32)).astype(jnp.bfloat16)
    return kept.reshape(size // 2, -1, right.shape[1])


def side_start(mine, size):
    count, rows, cols = mine.shape
    side = (lax.axis_index("dp") // 2) % 2
    grid = mine.reshape(count // 2, 2, rows, cols)
    away = lax.dynamic_index_in_dim(grid, 1 - side, 1, keepdims=False)
    kept = lax.dynamic_index_in_dim(grid, side, 1, keepdims=False)
    return kept, lax.ppermute(away, "dp", flip_perm(size, 2))


def side_end(kept, came):
    return (kept.astype(jnp.float32) + came.astype(jnp.float32)).astype(jnp.bfloat16)


def line_start(held, size):
    depth = held.shape[0]
    level = lax.axis_index("dp") // 4
    pieces = [lax.dynamic_index_in_dim(held, level, 0, keepdims=False)]
    for step in range(1, depth):
        piece = lax.dynamic_index_in_dim(held, (level + step) % depth, 0, keepdims=False)
        perm = [(i, (i + 4 * step) % size) for i in range(size)]
        pieces.append(lax.ppermute(piece, "dp", perm))
    return pieces


def line_end(pieces):
    total = pieces[0].astype(jnp.float32)
    for piece in pieces[1:]:
        total = total + piece.astype(jnp.float32)
    return total


def swap_start(part, size, chunks):
    step = part.shape[0] // chunks
    own = [part[i * step : (i + 1) * step] for i in range(chunks)]
    if size == 2:
        return own, [lax.ppermute(o, "tensor", flip_perm(size, 1)) for o in own]
    return own, [lax.psum(o, "tensor") for o in own]


def swap_end(own, came, size):
    f32 = jnp.float32
    both = [o.astype(f32) + c.astype(f32) if size == 2 else c.astype(f32) for o, c in zip(own, came)]
    return jnp.concatenate(both, axis=0) if len(both) > 1 else both[0]


def small_gather(value, name, size):
    bit = 1
    index = lax.axis_index(name)
    while bit < size:
        came = lax.ppermute(value, name, flip_perm(size, bit))
        upper = (index // bit) % 2 == 1
        value = jnp.where(
            upper, jnp.concatenate([came, value], 0), jnp.concatenate([value, came], 0)
        )
        bit *= 2
    return value


def small_scatter(value, name, size):
    bit = size // 2
    index = lax.axis_index(name)
    while bit:
        upper = (index // bit) % 2 == 1
        low, high = value[: value.shape[0] // 2], value[value.shape[0] // 2 :]
        came = lax.ppermute(jnp.where(upper, low, high), name, flip_perm(size, bit))
        value = jnp.where(upper, high, low) + came
        bit //= 2
    return value


def small_sum(value, name, size):
    bit = 1
    while bit < size:
        value = value + lax.ppermute(value, name, flip_perm(size, bit))
        bit *= 2
    return value


def tensor_scatter(part, size):
    if size == 2:
        index = lax.axis_index("tensor")
        width = part.shape[1] // 2
        away = lax.dynamic_slice_in_dim(part, (1 - index) * width, width, 1)
        kept = lax.dynamic_slice_in_dim(part, index * width, width, 1)
        came = lax.ppermute(away, "tensor", flip_perm(size, 1))
        return kept.astype(jnp.float32) + came.astype(jnp.float32)
    return lax.psum_scatter(part, "tensor", scatter_dimension=1, tiled=True).astype(jnp.float32)


def pair_cols(arrays, head_dim):
    rows, cols = arrays[0].shape
    pad = -cols % LANES
    arrays = [jnp.pad(a, ((0, 0), (0, pad))) if pad else a for a in arrays]
    pairs = (cols + pad) // LANES
    return jnp.stack([a.reshape(rows, pairs, LANES) for a in arrays], axis=2).reshape(rows, -1)


def unpair_cols(array, count, cols):
    rows = array.shape[0]
    split = array.reshape(rows, -1, count, LANES)
    return [split[:, :, i].reshape(rows, -1)[:, :cols] for i in range(count)]


def rotary_tables(row_pos, col_pos, quarter, repeat):
    frequency = jnp.exp(-math.log(10000.0) * jnp.arange(quarter, dtype=jnp.float32) / quarter)
    angles = jnp.concatenate(
        [
            row_pos.astype(jnp.float32)[:, None] * frequency,
            col_pos.astype(jnp.float32)[:, None] * frequency,
        ],
        axis=1,
    )
    sine = jnp.sin(angles)
    return jnp.tile(jnp.cos(angles), (1, 2 * repeat)), jnp.tile(
        jnp.concatenate([-sine, sine], axis=1), (1, repeat)
    )


def local(
    size,
    groups,
    latents,
    cotangent,
    caption,
    caption_lens,
    patch_row,
    patch_col,
    timestep,
    query_proj,
    key_proj,
    value_proj,
    output_proj,
    textkey_proj,
    textval_proj,
    gate_proj,
    up_proj,
    down_proj,
    modulation,
    attn_gain,
    ffn_gain,
    query_gain,
    key_gain,
    textkey_gain,
    cross_gate,
):
    f32, bf16 = jnp.float32, jnp.bfloat16
    rows_w, chan = query_proj.shape
    units = gate_proj.shape[1]
    head_part = query_gain.shape[0]
    head_dim = head_part * size
    heads_here = chan // head_dim
    model_dim = latents.shape[1]
    padded = chan + -chan % LANES
    pairs = padded // LANES
    dp_index = lax.axis_index("dp")
    tensor_index = lax.axis_index("tensor")

    text_shard = pair_cols([textkey_proj, textval_proj], head_dim)
    text_set = lax.all_gather(text_shard, "dp", axis=0, tiled=True)
    small = jnp.concatenate(
        [
            attn_gain.astype(f32),
            ffn_gain.astype(f32),
            query_gain.astype(f32),
            key_gain.astype(f32),
            textkey_gain.astype(f32),
            timestep.astype(f32),
        ]
    )[None]
    small_all = small_gather(small, "dp", size)
    first = jnp.concatenate(
        [pair_cols([query_proj, key_proj, value_proj], head_dim), pair_cols([output_proj.T], head_dim)],
        axis=1,
    )
    full_qkvo, _ = ring_gather(first, size)
    full_qkv, full_out_t = full_qkvo[:, : 3 * padded], full_qkvo[:, 3 * padded :]
    third = gated(jnp.concatenate([gate_proj, up_proj, down_proj.T], axis=1), small_all)
    ffn_set = lax.all_gather(third, "dp", axis=0, tiled=True)

    cuts = [rows_w, 2 * rows_w, 2 * rows_w + head_part]
    gain_one = small_all[:, : cuts[0]].reshape(-1)
    gain_two = small_all[:, cuts[0] : cuts[1]].reshape(-1)
    gain_query = small_all[:, cuts[1] : cuts[2]].reshape(-1)
    gain_key = small_all[:, cuts[2] : cuts[2] + head_part].reshape(-1)
    gain_text = small_all[:, cuts[2] + head_part : cuts[2] + 2 * head_part].reshape(-1)
    steps_all = small_all[:, cuts[2] + 2 * head_part :].reshape(-1)
    embed_rows = modulation.shape[0]
    embed_dim = embed_rows * size
    embed_all = time_embed(steps_all, embed_dim)
    cond_all = (embed_all * jax.nn.sigmoid(embed_all)).astype(bf16)
    cond_here = lax.dynamic_slice_in_dim(cond_all, dp_index * embed_rows, embed_rows, 1)
    mod_part = jnp.dot(cond_here, modulation, preferred_element_type=f32)
    mod_here = small_scatter(mod_part, "dp", size)
    mod_all = small_gather(mod_here, "tensor", groups).reshape(1, -1)
    scale_one = mod_all[:, 0:model_dim]
    gate_one = jnp.tanh(mod_all[:, model_dim : 2 * model_dim])
    scale_two = mod_all[:, 2 * model_dim : 3 * model_dim]
    gate_two = jnp.tanh(mod_all[:, 3 * model_dim : 4 * model_dim])
    tanh_cross = jnp.tanh(cross_gate.astype(f32))
    tanh_lanes = jnp.pad(jnp.repeat(tanh_cross, head_dim), (0, padded - chan))
    tanh_lanes = jnp.broadcast_to(tanh_lanes[None], (8, padded))
    per_tile = LANES // head_dim
    gain_lanes = jnp.pad(
        jnp.tile(jnp.stack([gain_query, gain_key, gain_text]), (1, per_tile)), ((0, 5), (0, 0))
    )
    cosine, sine = rotary_tables(patch_row[0], patch_col[0], head_dim // 4, per_tile)
    tables = (cosine, sine, gain_lanes, tanh_lanes)

    resid_in = latents.astype(f32)
    factor_one = inv_rms(resid_in)
    normed_one = resid_in * factor_one
    attn_in = (normed_one * gain_one * (1.0 + scale_one)).astype(bf16)
    qkv_raw = jnp.dot(attn_in, full_qkv, preferred_element_type=f32)
    cap_in = caption[0]
    full_text = gated(text_set, qkv_raw)
    text_raw = jnp.dot(cap_in, full_text, preferred_element_type=f32)
    mixed_heads, qkv_bf, tkv_bf, own_out, cross_out, lse = attend_pairs(
        caption_lens, qkv_raw, text_raw, cosine, sine, gain_lanes, tanh_lanes, head_dim
    )
    attn_part = jnp.einsum("rc,dc->rd", mixed_heads, full_out_t, preferred_element_type=f32)
    attn_part = attn_part.astype(bf16)
    attn_own, attn_came = swap_start(attn_part, groups, 1)

    late_in, late_cap, late_cot = gated((attn_in, cap_in, cotangent), attn_part)
    in_split = split_cols(late_in, size)
    cap_split = split_cols(late_cap, size)
    grad_out = late_cot.astype(f32)
    grad_ffn = (gate_two * grad_out).astype(bf16)
    ffn_split = split_cols(grad_ffn, size)
    full_ffn = gated(ffn_set, attn_part, in_split, cap_split, ffn_split)
    full_gu, full_down_t = full_ffn[:, : 2 * units], full_ffn[:, 2 * units :]
    dhidden = jnp.dot(grad_ffn, full_down_t, preferred_element_type=f32)
    attn_came = gated(attn_came, dhidden)
    attn_out = swap_end(attn_own, attn_came, groups)

    residual = resid_in + gate_one * attn_out
    factor_two = inv_rms(residual)
    normed_two = residual * factor_two
    ffn_in = (normed_two * gain_two * (1.0 + scale_two)).astype(bf16)
    gate_pre = jnp.dot(ffn_in, full_gu[:, :units], preferred_element_type=f32)
    up_pre = jnp.dot(ffn_in, full_gu[:, units:], preferred_element_type=f32)
    sig_gate = jax.nn.sigmoid(gate_pre)
    act_gate = gate_pre * sig_gate
    hidden = (act_gate * up_pre).astype(bf16)
    dgate_pre = (dhidden * up_pre * sig_gate * (1.0 + gate_pre * (1.0 - sig_gate))).astype(bf16)
    dup_pre = (dhidden * act_gate).astype(bf16)
    dboth = jnp.concatenate([dgate_pre, dup_pre], axis=1)
    dffn_part = jnp.einsum("rf,df->rd", dboth, full_gu, preferred_element_type=f32).astype(bf16)
    dffn_own, dffn_came = swap_start(dffn_part, groups, 1)

    hidden_l, dboth_l, ffn_in_l = gated((hidden, dboth, ffn_in), dffn_part)
    gu_split = split_cols(ffn_in_l, size)
    down_away, down_came = core_away(ffn_split, hidden_l, size)
    gu_away, gu_came = core_away(gu_split, dboth_l, size)
    hidden_l = gated(hidden, down_away, gu_away)
    ffn_part = jnp.einsum("rf,df->rd", hidden_l, full_down_t, preferred_element_type=f32)
    ffn_part = ffn_part.astype(bf16)
    ffn_own, ffn_came = swap_start(gated(ffn_part, dffn_part), groups, 1)
    down_came = gated(down_came, ffn_part)
    down_kept, down_x = side_start(core_keep(ffn_split, hidden, down_came, size), size)
    gu_came = gated(gu_came, down_kept)
    gu_kept, gu_x = side_start(core_keep(gu_split, dboth, gu_came, size), size)
    dffn_came = gated(dffn_came, gu_kept)
    dffn_in = swap_end(dffn_own, dffn_came, groups)

    gain_mul = gain_two * (1.0 + scale_two)
    weighed = jnp.sum(dffn_in * normed_two, axis=0)
    grad_gaintwo = weighed * (1.0 + scale_two[0])
    dscale_two = weighed * gain_two
    dresid = grad_out + norm_back(dffn_in * gain_mul, normed_two, factor_two)
    dgate_one = jnp.sum(dresid * attn_out, axis=0) * (1.0 - gate_one[0] ** 2)
    grad_attn = (gate_one * dresid).astype(bf16)
    dmixed = jnp.dot(grad_attn, full_out_t, preferred_element_type=f32).astype(bf16)
    out_split = split_cols(gated(grad_attn, dmixed), size)
    out_away, out_came = core_away(out_split, mixed_heads, size)
    down_x = gated(down_x, out_away)
    down_line = line_start(side_end(down_kept, down_x), size)
    out_came = gated(out_came, down_line[0])
    out_kept, out_x = side_start(core_keep(out_split, mixed_heads, out_came, size), size)

    split = pairs - pairs // 2
    windows = [(0, split), (split, pairs - split)]
    arrays = (caption_lens, qkv_bf, tkv_bf, qkv_raw, text_raw, own_out, cross_out, lse)
    qkv_cols = [(3 * LANES * a, 3 * LANES * (a + b)) for a, b in windows]
    text_cols = [(2 * LANES * a, 2 * LANES * (a + b)) for a, b in windows]
    dmixed_a = gated(dmixed, out_kept, down_line[0])
    dqkv_a, dtext_a, stats_a = attend_back_pairs(windows[0], arrays + (dmixed_a,), tables, head_dim)
    gu_x = gated(gu_x, dqkv_a)
    gu_line = line_start(side_end(gu_kept, gu_x), size)
    text_a_away, text_a_came = core_away(cap_split, gated(dtext_a, gu_line[0]), size)
    qkv_a_away, qkv_a_came = core_away(in_split, gated(dqkv_a, text_a_away), size)
    out_x = gated(out_x, qkv_a_away)
    out_line = line_start(side_end(out_kept, out_x), size)
    text_a_came = gated(text_a_came, out_line[0])
    text_a_kept, text_a_x = side_start(core_keep(cap_split, dtext_a, text_a_came, size), size)
    qkv_a_came = gated(qkv_a_came, text_a_kept)
    qkv_a_kept, qkv_a_x = side_start(core_keep(in_split, dqkv_a, qkv_a_came, size), size)
    dmixed_b = gated(dmixed, qkv_a_kept)
    dqkv_b, dtext_b, stats_b = attend_back_pairs(windows[1], arrays + (dmixed_b,), tables, head_dim)
    dqkv = jnp.concatenate([dqkv_a, dqkv_b], axis=1)
    dtext = jnp.concatenate([dtext_a, dtext_b], axis=1)
    dattn_part = jnp.einsum("rc,dc->rd", dqkv, full_qkv, preferred_element_type=f32).astype(bf16)
    dattn_own, dattn_came = swap_start(dattn_part, groups, 1)
    dtext_l, dqkv_l = gated((dtext_b, dqkv_b), dattn_part)
    text_b_away, text_b_came = core_away(cap_split, dtext_l, size)
    qkv_b_away, qkv_b_came = core_away(in_split, dqkv_l, size)
    text_a_x = gated(text_a_x, text_b_away, qkv_b_away)
    text_a_line = line_start(side_end(text_a_kept, text_a_x), size)
    text_b_came = gated(text_b_came, text_a_line[0])
    text_b_kept, text_b_x = side_start(core_keep(cap_split, dtext_b, text_b_came, size), size)
    qkv_b_came = gated(qkv_b_came, text_b_kept)
    qkv_b_kept, qkv_b_x = side_start(core_keep(in_split, dqkv_b, qkv_b_came, size), size)
    qkv_a_x = gated(qkv_a_x, qkv_b_kept)
    qkv_a_line = line_start(side_end(qkv_a_kept, qkv_a_x), size)
    caption_part = jnp.einsum(
        "bf,ef->be", gated(dtext, qkv_a_line[0]), full_text, preferred_element_type=f32
    )
    dcaption = tensor_scatter(caption_part.astype(bf16), groups)

    stats = jnp.concatenate([stats_a, stats_b], axis=1)
    stat_sums = stats[:4, :chan].reshape(4, heads_here, head_dim)
    xgate_here = jnp.sum(stat_sums[3], axis=1) * (1.0 - tanh_cross**2)
    grad_xgate = small_sum(xgate_here, "dp", size)
    ffn_came = gated(ffn_came, caption_part)
    ffn_out = swap_end(ffn_own, ffn_came, groups)
    output = (residual + gate_two * ffn_out).astype(bf16)
    dgate_two = jnp.sum(grad_out * ffn_out, axis=0) * (1.0 - gate_two[0] ** 2)
    down_t = line_end(gated(down_line, caption_part))
    gate_up = line_end(gated(gu_line, down_t))
    output_t = line_end(gated(out_line, gate_up))
    text_b_x = gated(text_b_x, output_t)
    text_b_line = line_start(side_end(text_b_kept, text_b_x), size)
    qkv_b_x = gated(qkv_b_x, text_b_line[0])
    qkv_b_line = line_start(side_end(qkv_b_kept, qkv_b_x), size)
    dattn_came = gated(dattn_came, qkv_b_line[0])
    dattn_in = swap_end(dattn_own, dattn_came, groups)
    weighed_one = jnp.sum(dattn_in * normed_one, axis=0)
    grad_gainone = weighed_one * (1.0 + scale_one[0])
    dscale_one = weighed_one * gain_one
    grad_latents = (
        dresid + norm_back(dattn_in * gain_one * (1.0 + scale_one), normed_one, factor_one)
    ).astype(bf16)
    text_a = line_end(gated(text_a_line, dattn_in))
    qkv_a = line_end(gated(qkv_a_line, dattn_in))

    dmod_all = jnp.concatenate([dscale_one, dgate_one, dscale_two, dgate_two]).astype(bf16)
    cols_here = modulation.shape[1]
    dmod_here = lax.dynamic_slice_in_dim(dmod_all, tensor_index * cols_here, cols_here, 0)
    dmod_set = small_gather(dmod_here[None].astype(f32), "dp", size).astype(bf16)
    grad_modul = jnp.einsum("bt,bc->tc", cond_here, dmod_set, preferred_element_type=f32)
    embed_part = jnp.einsum("bc,tc->bt", dmod_set, modulation, preferred_element_type=f32)
    embed_set = small_gather(embed_part[None], "dp", size)
    embed_row = lax.dynamic_index_in_dim(embed_set, dp_index, 1, keepdims=False).reshape(1, -1)
    embed_sum = small_sum(embed_row, "tensor", groups)
    embed_own = lax.dynamic_slice_in_dim(embed_all, dp_index, 1, 0)
    sig_own = jax.nn.sigmoid(embed_own)
    dembed_all = embed_sum * (sig_own * (1.0 + embed_own * (1.0 - sig_own)))
    width = embed_dim // groups
    dembed = lax.dynamic_slice_in_dim(dembed_all, tensor_index * width, width, 1)

    gains_heads = small_sum(jnp.sum(stat_sums[:3], axis=1), "tensor", groups)
    gains_set = jnp.concatenate(
        [
            grad_gainone.reshape(size, rows_w),
            grad_gaintwo.reshape(size, rows_w),
            gains_heads[0].reshape(size, head_part),
            gains_heads[1].reshape(size, head_part),
            gains_heads[2].reshape(size, head_part),
        ],
        axis=1,
    )
    gains_own = small_scatter(gains_set, "dp", size)[0]
    text_b = line_end(text_b_line)
    qkv_b = line_end(qkv_b_line)
    qkv_grads = jnp.concatenate([qkv_a, qkv_b], axis=1)
    text_grads = jnp.concatenate([text_a, text_b], axis=1)
    return (
        output,
        grad_latents,
        dcaption.astype(bf16)[None],
        dembed,
        *unpair_cols(qkv_grads, 3, chan),
        output_t[:, :chan].T,
        *unpair_cols(text_grads, 2, chan),
        gate_up[:, :units],
        gate_up[:, units:],
        down_t.T,
        grad_modul,
        gains_own[: cuts[0]],
        gains_own[cuts[0] : cuts[1]],
        gains_own[cuts[1] : cuts[2]],
        gains_own[cuts[2] : cuts[2] + head_part],
        gains_own[cuts[2] + head_part :],
        grad_xgate,
    )


def solution(mesh):
    in_specs = (
        P("dp", None),
        P("dp", None),
        P("dp", None, None),
        P("dp"),
        P("dp", None),
        P("dp", None),
        P("dp"),
        P("dp", "tensor"),
        P("dp", "tensor"),
        P("dp", "tensor"),
        P("tensor", "dp"),
        P("dp", "tensor"),
        P("dp", "tensor"),
        P("dp", "tensor"),
        P("dp", "tensor"),
        P("tensor", "dp"),
        P("dp", "tensor"),
        P("dp"),
        P("dp"),
        P("dp"),
        P("dp"),
        P("dp"),
        P("tensor"),
    )
    out_specs = (
        P("dp", None),
        P("dp", None),
        P("dp", None, "tensor"),
        P("dp", "tensor"),
        P("dp", "tensor"),
        P("dp", "tensor"),
        P("dp", "tensor"),
        P("tensor", "dp"),
        P("dp", "tensor"),
        P("dp", "tensor"),
        P("dp", "tensor"),
        P("dp", "tensor"),
        P("tensor", "dp"),
        P("dp", "tensor"),
        P("dp"),
        P("dp"),
        P("dp"),
        P("dp"),
        P("dp"),
        P("tensor"),
    )
    bound = functools.partial(local, mesh.shape["dp"], mesh.shape["tensor"])
    return jax.shard_map(bound, mesh=mesh, in_specs=in_specs, out_specs=out_specs, check_vma=False)
```

```python
import functools
import math

import jax
import jax.numpy as jnp
from jax import lax
from jax.experimental import pallas as pl
from jax.experimental.pallas import tpu as pltpu
from jax.sharding import PartitionSpec as P

EPSILON = 1e-06


def inv_rms(values):
    return lax.rsqrt(jnp.mean(values * values, axis=-1, keepdims=True) + EPSILON)


def time_embed(step_vals, embed_width):
    half_width = embed_width // 2
    frequency = jnp.exp(-math.log(10000.0) * jnp.arange(half_width, dtype=jnp.float32) / half_width)
    phases = step_vals.astype(jnp.float32)[:, None] * frequency
    return jnp.concatenate([jnp.cos(phases), jnp.sin(phases)], axis=1)


def norm_back(grad_hat, normed, factor):
    return factor * (grad_hat - normed * jnp.mean(grad_hat * normed, axis=-1, keepdims=True))


LANES = 128
LIGHT = pl.CostEstimate(flops=1, transcendentals=0, bytes_accessed=1)


def lane_ids(rows):
    return lax.broadcasted_iota(jnp.int32, (rows, LANES), 1)


def pair_matrix(same, half):
    row = lax.broadcasted_iota(jnp.int32, (LANES, LANES), 0) // half
    col = lax.broadcasted_iota(jnp.int32, (LANES, LANES), 1) // half
    return jnp.where((row == col) == same, 1.0, 0.0).astype(jnp.bfloat16)


def head_sums(values, matrix):
    high = values.astype(jnp.bfloat16)
    low = (values - high.astype(jnp.float32)).astype(jnp.bfloat16)
    return jnp.dot(high, matrix, preferred_element_type=jnp.float32) + jnp.dot(
        low, matrix, preferred_element_type=jnp.float32
    )


def swap_quarters(values, half):
    rows = values.shape[0]
    first = lane_ids(rows) % half < half // 2
    return jnp.where(
        first,
        pltpu.roll(values, LANES - half // 2, 1),
        pltpu.roll(values, half // 2, 1),
    )


def nt_dot(left, right):
    return lax.dot_general(
        left, right, (((1,), (1,)), ((), ())), preferred_element_type=jnp.float32
    )


def tn_dot(left, right):
    return lax.dot_general(
        left, right, (((0,), (0,)), ((), ())), preferred_element_type=jnp.float32
    )


def attend_kernel(half, block, fresh, *refs):
    f32, bf16 = jnp.float32, jnp.bfloat16
    matrix = pair_matrix(True, half)
    if fresh:
        len_ref, rawq_ref, rawk_ref, rawv_ref, text_ref, tval_ref = refs[:6]
        cos_ref, sin_ref, cosk_ref, sink_ref, gain_ref, tanh_ref = refs[6:12]
        mixed_ref, query_ref, own_ref, cross_ref, lse_ref, kv_ref, tkv_ref = refs[12:]
    else:
        len_ref, rawq_ref, kv_ref, tkv_ref, cos_ref, sin_ref, gain_ref, tanh_ref = refs[:8]
        mixed_ref, query_ref, own_ref, cross_ref, lse_ref = refs[12:]

    def hat(raw):
        return raw * lax.rsqrt(head_sums(raw * raw, matrix) * (1.0 / half) + EPSILON)

    def turned(raw, gain, cosine, sine):
        value = hat(raw) * gain
        return (value * cosine + swap_quarters(value, half) * sine).astype(bf16)

    query_ref[...] = turned(rawq_ref[...], gain_ref[0:1], cos_ref[...], sin_ref[...])
    if fresh:
        kv_ref[:, :LANES] = turned(rawk_ref[...], gain_ref[1:2], cosk_ref[...], sink_ref[...])
        kv_ref[:, LANES:] = rawv_ref[...].astype(bf16)
        tkv_ref[:, :LANES] = (hat(text_ref[...]) * gain_ref[2:3]).astype(bf16)
        tkv_ref[:, LANES:] = tval_ref[...].astype(bf16)
    key, value = kv_ref[:, :LANES], kv_ref[:, LANES:]
    tkey, tval = tkv_ref[:, :LANES], tkv_ref[:, LANES:]
    one = jnp.ones((), bf16)
    zero = jnp.zeros((), bf16)

    def pick(a, b):
        return jnp.where(lane_ids(a.shape[0]) < half, a, b)

    def fill(a, fillers, first):
        other = jnp.full(a.shape, fillers, bf16)
        return pick(a, other) if first else pick(other, a)

    value_ones = [fill(value, one, True), fill(value, one, False)]
    tval_ones = [fill(tval, one, True), fill(tval, one, False)]
    keep = lax.broadcasted_iota(jnp.int32, (block, tkey.shape[0]), 1) < len_ref[0]

    def step(i, _):
        here = pl.ds(pl.multiple_of(i * block, block), block)
        q_blk = query_ref[here, :] * jnp.asarray(half**-0.5, bf16)
        outs = []
        texts = []
        for head in range(2):
            q_one = fill(q_blk, zero, head == 0)
            e_self = jnp.exp(nt_dot(q_one, key)).astype(bf16)
            outs.append(jnp.dot(e_self, value_ones[head], preferred_element_type=f32))
            e_text = jnp.where(keep, jnp.exp(nt_dot(q_one, tkey)), 0.0).astype(bf16)
            texts.append(jnp.dot(e_text, tval_ones[head], preferred_element_type=f32))
        for n, (a, b) in enumerate((outs, texts)):
            total = pick(b, a)
            lse_ref[here, n * LANES : (n + 1) * LANES] = jnp.log(total)
            res = pick(a, b) / pltpu.roll(total, half, 1)
            if n == 0:
                own = res
                own_ref[here, :] = res
            else:
                cross_ref[here, :] = res
                mixed_ref[here, :] = (own + tanh_ref[0:1] * res).astype(bf16)
        return 0

    lax.fori_loop(0, query_ref.shape[0] // block, step, 0)


def attend_rows(part, cap_len, raw, text, tables, half, kept=None):
    cosine, sine, gains, tanh_lanes = tables
    rows, caps = raw.shape[0], text.shape[0]
    count = rows // 2
    width = raw.shape[1] // 3
    f32, bf16 = jnp.float32, jnp.bfloat16
    fresh = kept is None

    def piece(scale, shift, wide=1):
        return pl.BlockSpec((count, wide * LANES), lambda p: (part, scale * p + shift))

    table = pl.BlockSpec((count, LANES), lambda p: (part, 0))
    whole = pl.BlockSpec(memory_space=pl.ANY)
    smem = pl.BlockSpec(memory_space=pltpu.SMEM)
    kv_block = pl.BlockSpec((rows, 2 * LANES), lambda p: (0, p))
    tkv_block = pl.BlockSpec((caps, 2 * LANES), lambda p: (0, p))
    tail_specs = [fixed_block(8), lane_block(8, 1, 0)]
    out_specs = [
        pl.BlockSpec((count, LANES), lambda p: (0, p)),
        piece(1, 0),
        piece(1, 0),
        piece(1, 0),
        piece(1, 0, 2),
    ]
    out_shape = [
        jax.ShapeDtypeStruct((count, width), bf16),
        jax.ShapeDtypeStruct((rows, width), bf16),
        jax.ShapeDtypeStruct((rows, width), f32),
        jax.ShapeDtypeStruct((rows, width), f32),
        jax.ShapeDtypeStruct((rows, 2 * width), f32),
    ]
    if fresh:
        in_specs = [smem, piece(3, 0), lane_block(rows, 3, 1), lane_block(rows, 3, 2)]
        in_specs += [lane_block(caps, 2, 0), lane_block(caps, 2, 1)]
        in_specs += [table, table, fixed_block(rows), fixed_block(rows)] + tail_specs
        operands = (cap_len, raw, raw, raw, text, text, cosine, sine, cosine, sine)
        operands += (gains, tanh_lanes)
        out_specs += [kv_block, tkv_block]
        out_shape += [
            jax.ShapeDtypeStruct((rows, 2 * width), bf16),
            jax.ShapeDtypeStruct((caps, 2 * width), bf16),
        ]
        aliases = {}
    else:
        query, own, cross, lse, kv, tkv = kept
        in_specs = [smem, piece(3, 0), kv_block, tkv_block, table, table] + tail_specs
        in_specs += [whole] * 4
        operands = (cap_len, raw, kv, tkv, cosine, sine, gains, tanh_lanes)
        operands += (query, own, cross, lse)
        aliases = {8: 1, 9: 2, 10: 3, 11: 4}
    return pl.pallas_call(
        functools.partial(attend_kernel, half, min(256, count), fresh),
        grid=(width // LANES,),
        in_specs=in_specs,
        out_specs=out_specs,
        out_shape=out_shape,
        input_output_aliases=aliases,
        compiler_params=pltpu.CompilerParams(vmem_limit_bytes=50 * 2**20),
        cost_estimate=LIGHT,
        name="attend_fwd",
    )(*operands)


def pick_head(a, b, first, half):
    low = lane_ids(a.shape[0]) < half
    return jnp.where(low, a, b) if first else jnp.where(low, b, a)


def three_parts(value, half):
    spot = lane_ids(value.shape[0]) % half
    high = value.astype(jnp.bfloat16).astype(jnp.float32)
    rest = value - high
    mid = rest.astype(jnp.bfloat16).astype(jnp.float32)
    low = rest - mid
    parts = jnp.where(spot == 0, high, jnp.where(spot == 1, mid, jnp.where(spot == 2, low, 0.0)))
    return parts.astype(jnp.bfloat16)


def with_ones(value, first, half):
    ones = jnp.where(lane_ids(value.shape[0]) % half < 3, 1.0, 0.0).astype(jnp.bfloat16)
    return pick_head(value, ones, first, half)


def only_head(value, first, half):
    return pick_head(value, jnp.zeros(value.shape, jnp.bfloat16), first, half)


def norm_return(grad_in, raw, gain, half, turn):
    same = pair_matrix(True, half)
    inv = lax.rsqrt(head_sums(raw * raw, same) * (1.0 / half) + EPSILON)
    normed = raw * inv
    back = grad_in.astype(jnp.bfloat16).astype(jnp.float32)
    if turn is not None:
        back = back * turn[0][...] - swap_quarters(back, half) * turn[1][...]
    scaled = back * gain
    mean = head_sums(scaled * normed, same) * (1.0 / half)
    stat = jnp.sum(back * normed, axis=0, keepdims=True)
    return (inv * (scaled - normed * mean)).astype(jnp.bfloat16), stat


def score_grads(key_aug, val_aug, q_aug, o_aug, keep):
    probs = jnp.exp(nt_dot(key_aug, q_aug))
    if keep is not None:
        probs = jnp.where(keep, probs, 0.0)
    return probs.astype(jnp.bfloat16), (probs * nt_dot(val_aug, o_aug)).astype(jnp.bfloat16)


def cross_back_kernel(
    half,
    block,
    len_ref,
    query_ref,
    tkv_ref,
    text_ref,
    cross_ref,
    lse_ref,
    dmix_ref,
    gain_ref,
    tanh_ref,
    dq_ref,
    dtext_ref,
    stat_ref,
    qs_ref,
    os_ref,
    dk_ref,
    dv_ref,
):
    f32, bf16 = jnp.float32, jnp.bfloat16
    rows, caps = query_ref.shape[0], tkv_ref.shape[0]
    grad_f = dmix_ref[...].astype(f32)
    other = (grad_f * tanh_ref[0:1]).astype(bf16)
    delta = three_parts(
        -head_sums(other.astype(f32) * cross_ref[...], pair_matrix(False, half)), half
    )
    lse = three_parts(-lse_ref[...], half)
    query = query_ref[...] * jnp.asarray(half**-0.5, bf16)
    tkey, tval = tkv_ref[:, :LANES], tkv_ref[:, LANES:]
    for head in range(2):
        qs_ref[head] = pick_head(query, lse, head == 0, half)
        os_ref[head] = pick_head(other, delta, head == 0, half)
    key_aug = [with_ones(tkey, h == 0, half) for h in range(2)]
    val_aug = [with_ones(tval, h == 0, half) for h in range(2)]
    key_only = [only_head(tkey, h == 0, half) for h in range(2)]
    dk_ref[...] = jnp.zeros_like(dk_ref)
    dv_ref[...] = jnp.zeros_like(dv_ref)
    keep = lax.broadcasted_iota(jnp.int32, (caps, block), 0) < len_ref[0]

    def step(i, _):
        here = pl.ds(pl.multiple_of(i * block, block), block)
        dq = jnp.zeros((block, LANES), f32)
        for head in range(2):
            q_aug, o_aug = qs_ref[head, here], os_ref[head, here]
            probs, grads = score_grads(key_aug[head], val_aug[head], q_aug, o_aug, keep)
            dv_ref[...] += jnp.dot(
                probs, only_head(o_aug, head == 0, half), preferred_element_type=f32
            )
            dk_ref[...] += jnp.dot(
                grads, only_head(q_aug, head == 0, half), preferred_element_type=f32
            )
            dq += tn_dot(grads, key_only[head])
        dq_ref[here, :] = dq * half**-0.5
        return 0

    lax.fori_loop(0, rows // block, step, 0)
    res, stat_t = norm_return(dk_ref[...], text_ref[...], gain_ref[2:3], half, None)
    dtext_ref[:, :LANES] = res
    dtext_ref[:, LANES:] = dv_ref[...].astype(bf16)
    stat_x = jnp.sum(grad_f * cross_ref[...], axis=0, keepdims=True)
    stat_ref[...] = jnp.concatenate([stat_t, stat_x, jnp.zeros((6, LANES), f32)], axis=0)


def self_back_kernel(
    half,
    block,
    query_ref,
    key_ref,
    val_ref,
    rawq_ref,
    rawk_ref,
    own_ref,
    lse_ref,
    dmix_ref,
    dqc_ref,
    cos_ref,
    sin_ref,
    gain_ref,
    dqkv_ref,
    stat_ref,
    qs_ref,
    os_ref,
    dq_ref,
    dk_ref,
    dv_ref,
):
    f32, bf16 = jnp.float32, jnp.bfloat16
    rows = query_ref.shape[0]
    grad = dmix_ref[...]
    delta = three_parts(
        -head_sums(grad.astype(f32) * own_ref[...], pair_matrix(False, half)), half
    )
    lse = three_parts(-lse_ref[...], half)
    query = query_ref[...] * jnp.asarray(half**-0.5, bf16)
    key, value = key_ref[...], val_ref[...]
    for head in range(2):
        qs_ref[head] = pick_head(query, lse, head == 0, half)
        os_ref[head] = pick_head(grad, delta, head == 0, half)
    key_aug = [with_ones(key, h == 0, half) for h in range(2)]
    val_aug = [with_ones(value, h == 0, half) for h in range(2)]
    key_only = [only_head(key, h == 0, half) for h in range(2)]
    dk_ref[...] = jnp.zeros_like(dk_ref)
    dv_ref[...] = jnp.zeros_like(dv_ref)

    def step(i, _):
        here = pl.ds(pl.multiple_of(i * block, block), block)
        dq = jnp.zeros((block, LANES), f32)
        for head in range(2):
            q_aug, o_aug = qs_ref[head, here], os_ref[head, here]
            probs, grads = score_grads(key_aug[head], val_aug[head], q_aug, o_aug, None)
            dv_ref[...] += jnp.dot(
                probs, only_head(o_aug, head == 0, half), preferred_element_type=f32
            )
            dk_ref[...] += jnp.dot(
                grads, only_head(q_aug, head == 0, half), preferred_element_type=f32
            )
            dq += tn_dot(grads, key_only[head])
        dq_ref[here, :] = dqc_ref[here, :] + dq * half**-0.5
        return 0

    lax.fori_loop(0, rows // block, step, 0)
    turn = (cos_ref, sin_ref)
    res, stat_q = norm_return(dq_ref[...], rawq_ref[...], gain_ref[0:1], half, turn)
    dqkv_ref[:, :LANES] = res
    res, stat_k = norm_return(dk_ref[...], rawk_ref[...], gain_ref[1:2], half, turn)
    dqkv_ref[:, LANES : 2 * LANES] = res
    dqkv_ref[:, 2 * LANES :] = dv_ref[...].astype(bf16)
    stat_ref[...] = jnp.concatenate([stat_q, stat_k, jnp.zeros((6, LANES), f32)], axis=0)


def lane_block(rows, scale, shift):
    return pl.BlockSpec((rows, LANES), lambda p: (0, scale * p + shift))


def fixed_block(rows):
    return pl.BlockSpec((rows, LANES), lambda p: (0, 0))


def cross_back(cap_len, query, tkv, text, cross, lse, dmix, tables, half):
    gains, tanh_lanes = tables[2], tables[3]
    rows, caps = query.shape[0], text.shape[0]
    width = dmix.shape[1]
    f32, bf16 = jnp.float32, jnp.bfloat16
    return pl.pallas_call(
        functools.partial(cross_back_kernel, half, min(512, rows)),
        grid=(width // LANES,),
        in_specs=[
            pl.BlockSpec(memory_space=pltpu.SMEM),
            lane_block(rows, 1, 0),
            pl.BlockSpec((caps, 2 * LANES), lambda p: (0, p)),
            lane_block(caps, 2, 0),
            lane_block(rows, 1, 0),
            lane_block(rows, 2, 1),
            lane_block(rows, 1, 0),
            fixed_block(8),
            lane_block(8, 1, 0),
        ],
        out_specs=[
            lane_block(rows, 1, 0),
            pl.BlockSpec((caps, 2 * LANES), lambda p: (0, p)),
            lane_block(8, 1, 0),
        ],
        out_shape=[
            jax.ShapeDtypeStruct((rows, width), f32),
            jax.ShapeDtypeStruct((caps, 2 * width), bf16),
            jax.ShapeDtypeStruct((8, width), f32),
        ],
        scratch_shapes=[pltpu.VMEM((2, rows, LANES), bf16)] * 2
        + [pltpu.VMEM((caps, LANES), f32)] * 2,
        compiler_params=pltpu.CompilerParams(vmem_limit_bytes=40 * 2**20),
        cost_estimate=LIGHT,
        name="cross_bwd",
    )(cap_len, query, tkv, text, cross, lse, dmix, gains, tanh_lanes)


def self_back(window, query, kv, raw, own, lse, dmix, dq_cross, tables, half):
    cosine, sine, gains, _ = tables
    first, pairs = window
    rows = raw.shape[0]
    width = pairs * LANES
    f32, bf16 = jnp.float32, jnp.bfloat16
    return pl.pallas_call(
        functools.partial(self_back_kernel, half, min(512, rows)),
        grid=(pairs,),
        in_specs=[
            lane_block(rows, 1, first),
            lane_block(rows, 2, 2 * first),
            lane_block(rows, 2, 2 * first + 1),
            lane_block(rows, 3, 3 * first),
            lane_block(rows, 3, 3 * first + 1),
            lane_block(rows, 1, first),
            lane_block(rows, 2, 2 * first),
            lane_block(rows, 1, first),
            lane_block(rows, 1, first),
            fixed_block(rows),
            fixed_block(rows),
            fixed_block(8),
        ],
        out_specs=[pl.BlockSpec((rows, 3 * LANES), lambda p: (0, p)), lane_block(8, 1, 0)],
        out_shape=[
            jax.ShapeDtypeStruct((rows, 3 * width), bf16),
            jax.ShapeDtypeStruct((8, width), f32),
        ],
        scratch_shapes=[pltpu.VMEM((2, rows, LANES), bf16)] * 2
        + [pltpu.VMEM((rows, LANES), f32)] * 3,
        compiler_params=pltpu.CompilerParams(vmem_limit_bytes=50 * 2**20),
        cost_estimate=LIGHT,
        name="self_bwd",
    )(query, kv, kv, raw, raw, own, lse, dmix, dq_cross, cosine, sine, gains)


def feed_kernel(x_ref, grad_ref, gate_ref, up_ref, down_ref, hidden_ref, both_ref):
    f32, bf16 = jnp.float32, jnp.bfloat16
    gate = jnp.dot(x_ref[...], gate_ref[...], preferred_element_type=f32)
    up = jnp.dot(x_ref[...], up_ref[...], preferred_element_type=f32)
    dhidden = jnp.dot(grad_ref[...], down_ref[...], preferred_element_type=f32)
    sig = 1.0 / (1.0 + jnp.exp(-gate))
    act = gate * sig
    hidden_ref[...] = (act * up).astype(bf16)
    tile = gate_ref.shape[1]
    both_ref[:, :tile] = (dhidden * up * sig * (1.0 + gate * (1.0 - sig))).astype(bf16)
    both_ref[:, tile:] = (dhidden * act).astype(bf16)


def feed_forward(x, grad, weights, units, tile):
    rows, depth = x.shape
    count = units // tile
    bf16 = jnp.bfloat16

    def cols(scale, shift):
        return pl.BlockSpec((depth, tile), lambda j: (0, scale * j + shift))

    whole = pl.BlockSpec((rows, depth), lambda j: (0, 0))
    return pl.pallas_call(
        feed_kernel,
        grid=(count,),
        in_specs=[whole, whole, cols(2, 0), cols(2, 1), cols(1, 2 * count)],
        out_specs=[
            pl.BlockSpec((rows, tile), lambda j: (0, j)),
            pl.BlockSpec((rows, 2 * tile), lambda j: (0, j)),
        ],
        out_shape=[
            jax.ShapeDtypeStruct((rows, units), bf16),
            jax.ShapeDtypeStruct((rows, 2 * units), bf16),
        ],
        compiler_params=pltpu.CompilerParams(vmem_limit_bytes=58 * 2**20),
        cost_estimate=LIGHT,
        name="feed_forward",
    )(x, grad, weights, weights, weights)


def outer_kernel(size, bits, me_ref, left_ref, right_ref, keep_ref, away_ref, total_ref):
    total_ref[...] = tn_dot(left_ref[...], right_ref[...])
    rows = keep_ref.shape[0] // (size // 2)
    for place in range(size):
        slot = sum(((place >> (len(bits) - 1 - k)) & 1) << bit for k, bit in enumerate(bits))
        start = pl.multiple_of((me_ref[0] ^ slot) * rows, 16)
        block = total_ref[pl.ds(start, rows), :].astype(jnp.bfloat16)
        out_ref = keep_ref if place < size // 2 else away_ref
        spot = place % (size // 2)
        out_ref[spot * rows : (spot + 1) * rows, :] = block


def outer_grads(me, left, right, size, bits, tile):
    tokens, depth = left.shape
    cols = right.shape[1]
    half = jax.ShapeDtypeStruct((depth // 2, cols), jnp.bfloat16)
    return pl.pallas_call(
        functools.partial(outer_kernel, size, bits),
        grid=(cols // tile,),
        in_specs=[
            pl.BlockSpec(memory_space=pltpu.SMEM),
            pl.BlockSpec((tokens, depth), lambda j: (0, 0)),
            pl.BlockSpec((tokens, tile), lambda j: (0, j)),
        ],
        out_specs=[pl.BlockSpec((depth // 2, tile), lambda j: (0, j))] * 2,
        out_shape=[half, half],
        scratch_shapes=[pltpu.VMEM((depth, tile), jnp.float32)],
        compiler_params=pltpu.CompilerParams(vmem_limit_bytes=50 * 2**20),
        cost_estimate=LIGHT,
        name="outer_grads",
    )(me, left, right)


def product_kernel(turned, has_add, *refs):
    left_ref, right_ref = refs[:2]
    dot = nt_dot if turned else (lambda a, b: jnp.dot(a, b, preferred_element_type=jnp.float32))
    total = dot(left_ref[...], right_ref[...])
    if has_add:
        total = total + refs[2][...].astype(jnp.float32)
    refs[-1][...] = total.astype(refs[-1].dtype)


def product(left, right, cols, tile, dtype, turned=False, shift=0, add=None, part=(0, 1)):
    depth = left.shape[1]
    rows = left.shape[0] // part[1]
    if turned:
        right_block = pl.BlockSpec((tile, depth), lambda j: (j, shift))
    else:
        right_block = pl.BlockSpec((depth, tile), lambda j: (0, j + shift))
    in_specs = [pl.BlockSpec((rows, depth), lambda j: (part[0], 0)), right_block]
    if add is not None:
        in_specs.append(pl.BlockSpec((rows, tile), lambda j: (0, j)))
    return pl.pallas_call(
        functools.partial(product_kernel, turned, add is not None),
        grid=(cols // tile,),
        in_specs=in_specs,
        out_specs=pl.BlockSpec((rows, tile), lambda j: (0, j)),
        out_shape=jax.ShapeDtypeStruct((rows, cols), dtype),
        compiler_params=pltpu.CompilerParams(vmem_limit_bytes=58 * 2**20),
        cost_estimate=LIGHT,
        name="product",
    )(left, right, *([] if add is None else [add]))


def blank(shape, dtype):
    return pl.pallas_call(
        lambda out_ref: None,
        out_specs=pl.BlockSpec(memory_space=pl.ANY),
        out_shape=jax.ShapeDtypeStruct(shape, dtype),
        name="blank",
    )()


def gated(value, *tokens):
    return lax.optimization_barrier((value,) + tokens)[0]


def chip_ring(size):
    depth = size // 4
    return [2 * q if q < depth else 2 * (2 * depth - 1 - q) + 1 for q in range(size // 2)]


def ring_perm(size, step):
    order = chip_ring(size)
    count = len(order)
    return [
        (order[q] * 2 + c, order[(q + step) % count] * 2 + c) for q in range(count) for c in range(2)
    ]


def flip_perm(size, bit):
    return [(i, i ^ bit) for i in range(size)]


def ring_place(size):
    depth = size // 4
    index = lax.axis_index("dp")
    chip = index // 2
    level = chip // 2
    return jnp.where(chip % 2 == 0, level, 2 * depth - 1 - level), index % 2


def chip_at(place, size):
    depth = size // 4
    place = place % (2 * depth)
    return jnp.where(place < depth, 2 * place, 2 * (2 * depth - 1 - place) + 1)


def ring_gather(shard, size, hop):
    count = size // 2
    rows, cols = shard.shape
    half = cols // 2
    place, core = ring_place(size)
    swap = flip_perm(size, 1)
    ahead, behind = ring_perm(size, 1), ring_perm(size, -1)
    pieces = [(0, 0, shard)]
    fwd = bwd = shard
    for step in range(1, count // 2):
        fwd = lax.ppermute(fwd, "dp", ahead)
        bwd = lax.ppermute(bwd, "dp", behind)
        pieces += [(-step, 0, fwd), (step, 0, bwd)]
        token = hop(fwd, bwd)
        if token is not None:
            fwd, bwd = gated((fwd, bwd), token)
    last_f = lax.ppermute(fwd[:, :half], "dp", ahead)
    last_b = lax.ppermute(bwd[:, half:], "dp", behind)
    pieces += [(count // 2, 0, last_f), (count // 2, half, last_b)]
    full = blank((count, 2, rows, cols), shard.dtype)
    for offset, low, piece in pieces:
        other = lax.ppermute(piece, "dp", swap)
        chip = chip_at(place + offset, size)
        full = lax.dynamic_update_slice(full, piece[None, None], (chip, core, 0, low))
        full = lax.dynamic_update_slice(full, other[None, None], (chip, 1 - core, 0, low))
    return full.reshape(size * rows, cols)


class SmallScatter:
    def __init__(self, value, size):
        self.value, self.size, self.bit = value, size, 0

    def left(self):
        return self.value.shape[0] > 1

    def hop(self, *tokens):
        if not self.left():
            return None
        index = lax.axis_index("dp")
        value = gated(self.value, *tokens) if tokens else self.value
        pairs = value.reshape(value.shape[0] // 2, 2, value.shape[1])
        upper = (index >> self.bit) % 2 == 1
        away = jnp.where(upper, pairs[:, 0], pairs[:, 1])
        came = lax.ppermute(away, "dp", flip_perm(self.size, 1 << self.bit))
        self.value = jnp.where(upper, pairs[:, 1], pairs[:, 0]) + came
        self.bit += 1
        return came


class Halving:
    def __init__(self, size, bits, keep, away):
        self.size, self.bits, self.stage = size, bits, 0
        self.terms = [keep]
        self.out = away

    def start(self):
        bit = self.bits[self.stage]
        self.came = lax.ppermute(self.out, "dp", flip_perm(self.size, 1 << bit))
        self.stage += 1

    def land(self, *tokens):
        self.came = gated(self.came, *tokens)
        return self.came

    def finish(self, *tokens):
        self.terms.append(gated(self.came, *tokens) if tokens else self.came)
        rows = self.terms[-1].shape[0]
        last = self.stage == len(self.bits)
        half = rows if last else rows // 2
        low = 0 if last else half
        total = sum(term[low : low + half].astype(jnp.float32) for term in self.terms)
        self.out = total if last else total.astype(jnp.bfloat16)
        self.terms = [term[:half] for term in self.terms]
        return self.out

    def drain(self, *tokens):
        while self.stage < len(self.bits):
            self.finish(*tokens)
            self.start()
            tokens = ()
        self.terms.append(gated(self.came, *tokens) if tokens else self.came)
        rows = self.terms[-1].shape[0]
        return [term[:rows] for term in self.terms]


def swap_start(part, size, chunks):
    step = part.shape[0] // chunks
    own = [part[i * step : (i + 1) * step] for i in range(chunks)]
    if size == 2:
        return own, [lax.ppermute(o, "tensor", flip_perm(size, 1)) for o in own]
    return own, [lax.psum(o, "tensor") for o in own]


def swap_end(own, came, size):
    f32 = jnp.float32
    both = [o.astype(f32) + c.astype(f32) if size == 2 else c.astype(f32) for o, c in zip(own, came)]
    return jnp.concatenate(both, axis=0) if len(both) > 1 else both[0]


def small_gather(value, name, size, tokens=(), steps=None):
    index = lax.axis_index(name)
    for k in range(size.bit_length() - 1):
        bit = 1 << k
        if k < len(tokens):
            value = gated(value, tokens[k])
        came = lax.ppermute(value, name, flip_perm(size, bit))
        upper = (index // bit) % 2 == 1
        value = jnp.where(
            upper, jnp.concatenate([came, value], 0), jnp.concatenate([value, came], 0)
        )
        if steps is not None:
            steps.append(value)
    return value


def small_sum(value, name, size):
    bit = 1
    while bit < size:
        value = value + lax.ppermute(value, name, flip_perm(size, bit))
        bit *= 2
    return value


def tensor_scatter(part, size):
    if size == 2:
        index = lax.axis_index("tensor")
        width = part.shape[1] // 2
        away = lax.dynamic_slice_in_dim(part, (1 - index) * width, width, 1)
        kept = lax.dynamic_slice_in_dim(part, index * width, width, 1)
        came = lax.ppermute(away, "tensor", flip_perm(size, 1))
        return kept.astype(jnp.float32) + came.astype(jnp.float32)
    return lax.psum_scatter(part, "tensor", scatter_dimension=1, tiled=True).astype(jnp.float32)


def weave_kernel(tile, plan, *refs):
    out_ref = refs[-1]
    out_ref[...] = jnp.zeros_like(out_ref)
    for target, source, low, wide, turned in plan:
        if turned:
            out_ref[:, target : target + wide] = refs[source][low : low + wide, :].T
        else:
            out_ref[:, target : target + wide] = refs[source][:, low : low + wide]


def weave(arrays, tile, last=None):
    rows, cols = arrays[0].shape
    count = -(-cols // tile)
    plan = []
    target = 0
    for i in range(count):
        for source in range(len(arrays)):
            plan.append((target, source, i * tile, min(tile, cols - i * tile), False))
            target += tile
    operands = list(arrays)
    if last is not None:
        plan.append((target, len(arrays), 0, last.shape[0], True))
        target += last.shape[0] + -last.shape[0] % tile
        operands.append(last)
    return pl.pallas_call(
        functools.partial(weave_kernel, tile, plan),
        out_shape=jax.ShapeDtypeStruct((rows, target), arrays[0].dtype),
        compiler_params=pltpu.CompilerParams(vmem_limit_bytes=30 * 2**20),
        cost_estimate=LIGHT,
        name="weave",
    )(*operands)


def gather_sum_kernel(tile, count, terms, *refs):
    total = refs[0][...].astype(jnp.float32)
    for ref in refs[1:terms]:
        total = total + ref[...].astype(jnp.float32)
    outs = refs[terms:]
    cols = outs[0].shape[1]
    for i in range(-(-cols // tile)):
        wide = min(tile, cols - i * tile)
        for n, out_ref in enumerate(outs):
            start = (i * count + n) * tile
            out_ref[:, i * tile : i * tile + wide] = total[:, start : start + wide]


def gather_sum(terms, tile, count, cols):
    rows, wide = terms[0].shape
    block = rows
    while block * wide * (2 * len(terms) + 8) > 24 * 2**20 and block % 32 == 0:
        block //= 2
    return pl.pallas_call(
        functools.partial(gather_sum_kernel, tile, count, len(terms)),
        grid=(rows // block,),
        in_specs=[pl.BlockSpec((block, wide), lambda r: (r, 0)) for _ in terms],
        out_specs=[pl.BlockSpec((block, cols), lambda r: (r, 0))] * count,
        out_shape=[jax.ShapeDtypeStruct((rows, cols), jnp.float32)] * count,
        compiler_params=pltpu.CompilerParams(vmem_limit_bytes=58 * 2**20),
        cost_estimate=LIGHT,
        name="gather_sum",
    )(*terms)


def rotary_tables(row_pos, col_pos, quarter, repeat):
    frequency = jnp.exp(-math.log(10000.0) * jnp.arange(quarter, dtype=jnp.float32) / quarter)
    angles = jnp.concatenate(
        [
            row_pos.astype(jnp.float32)[:, None] * frequency,
            col_pos.astype(jnp.float32)[:, None] * frequency,
        ],
        axis=1,
    )
    sine = jnp.sin(angles)
    return jnp.tile(jnp.cos(angles), (1, 2 * repeat)), jnp.tile(
        jnp.concatenate([-sine, sine], axis=1), (1, repeat)
    )


def local(
    size,
    groups,
    latents,
    cotangent,
    caption,
    caption_lens,
    patch_row,
    patch_col,
    timestep,
    query_proj,
    key_proj,
    value_proj,
    output_proj,
    textkey_proj,
    textval_proj,
    gate_proj,
    up_proj,
    down_proj,
    modulation,
    attn_gain,
    ffn_gain,
    query_gain,
    key_gain,
    textkey_gain,
    cross_gate,
):
    f32, bf16 = jnp.float32, jnp.bfloat16
    rows_w, chan = query_proj.shape
    units = gate_proj.shape[1]
    head_part = query_gain.shape[0]
    head_dim = head_part * size
    heads_here = chan // head_dim
    model_dim = latents.shape[1]
    padded = chan + -chan % LANES
    pairs = padded // LANES
    dp_index = lax.axis_index("dp")
    tensor_index = lax.axis_index("tensor")

    small = jnp.concatenate(
        [
            attn_gain.astype(f32),
            ffn_gain.astype(f32),
            query_gain.astype(f32),
            key_gain.astype(f32),
            textkey_gain.astype(f32),
            timestep.astype(f32),
        ]
    )[None]
    steps = []
    small_all = small_gather(small, "dp", size, (), steps)
    textkey_l, textval_l = gated((textkey_proj, textval_proj), steps[0])
    text_shard = weave([textkey_l, textval_l], LANES)
    text_set = lax.all_gather(text_shard, "dp", axis=0, tiled=True)
    query_l, key_l, value_l, output_l = gated(
        (query_proj, key_proj, value_proj, output_proj), steps[1]
    )
    first = weave([query_l, key_l, value_l], LANES, output_l)
    cuts = [rows_w, 2 * rows_w, 2 * rows_w + head_part]
    gain_one = small_all[:, : cuts[0]].reshape(-1)
    gain_two = small_all[:, cuts[0] : cuts[1]].reshape(-1)
    gain_query = small_all[:, cuts[1] : cuts[2]].reshape(-1)
    gain_key = small_all[:, cuts[2] : cuts[2] + head_part].reshape(-1)
    gain_text = small_all[:, cuts[2] + head_part : cuts[2] + 2 * head_part].reshape(-1)
    steps_all = small_all[:, cuts[2] + 2 * head_part :].reshape(-1)
    embed_rows = modulation.shape[0]
    embed_dim = embed_rows * size
    embed_all = time_embed(steps_all, embed_dim)
    cond_all = (embed_all * jax.nn.sigmoid(embed_all)).astype(bf16)
    cond_here = lax.dynamic_slice_in_dim(cond_all, dp_index * embed_rows, embed_rows, 1)
    mod_part = jnp.dot(cond_here, modulation, preferred_element_type=f32)
    mod_sums = SmallScatter(mod_part, size)
    mod_sums.hop()
    full_qkvo = ring_gather(gated(first, small_all), size, mod_sums.hop)
    while mod_sums.left():
        mod_sums.hop()
    mod_here = mod_sums.value
    mod_all = small_gather(mod_here, "tensor", groups).reshape(1, -1)
    tile = 256
    blocks = units // tile
    gate_l, up_l, down_l = gated((gate_proj, up_proj, down_proj), first)
    third = weave([gate_l, up_l], tile, down_l)
    ffn_set = lax.all_gather(gated(third, small_all), "dp", axis=0, tiled=True)
    scale_one = mod_all[:, 0:model_dim]
    gate_one = jnp.tanh(mod_all[:, model_dim : 2 * model_dim])
    scale_two = mod_all[:, 2 * model_dim : 3 * model_dim]
    gate_two = jnp.tanh(mod_all[:, 3 * model_dim : 4 * model_dim])
    tanh_cross = jnp.tanh(cross_gate.astype(f32))
    tanh_lanes = jnp.pad(jnp.repeat(tanh_cross, head_dim), (0, padded - chan))
    tanh_lanes = jnp.broadcast_to(tanh_lanes[None], (8, padded))
    per_tile = LANES // head_dim
    gain_lanes = jnp.pad(
        jnp.tile(jnp.stack([gain_query, gain_key, gain_text]), (1, per_tile)), ((0, 5), (0, 0))
    )
    cosine, sine = rotary_tables(patch_row[0], patch_col[0], head_dim // 4, per_tile)
    tables = (cosine, sine, gain_lanes, tanh_lanes)

    resid_in = latents.astype(f32)
    factor_one = inv_rms(resid_in)
    normed_one = resid_in * factor_one
    attn_in = (normed_one * gain_one * (1.0 + scale_one)).astype(bf16)
    qkv_raw = product(attn_in, full_qkvo, 3 * padded, 3 * LANES, f32)
    cap_in = caption[0]
    full_text = gated(text_set, qkv_raw)
    text_raw = product(cap_in, full_text, 2 * padded, 256, f32)
    mixed_a, query_bf, own_out, cross_out, lse, kv_bf, tkv_bf = attend_rows(
        0, caption_lens, qkv_raw, text_raw, tables, head_dim
    )
    part_a = product(mixed_a, full_qkvo, model_dim, 512, bf16, True, 3)
    own_a, came_a = swap_start(part_a, groups, 1)
    kept = gated((query_bf, own_out, cross_out, lse, kv_bf, tkv_bf), part_a)
    mixed_b, query_bf, own_out, cross_out, lse = attend_rows(
        1, caption_lens, qkv_raw, text_raw, tables, head_dim, kept
    )
    attn_part = product(mixed_b, full_qkvo, model_dim, 512, bf16, True, 3)
    mixed_heads = jnp.concatenate([mixed_a, mixed_b], axis=0)
    mod_set = lax.all_gather(gated(modulation, attn_part), "dp", axis=0, tiled=True)

    grad_out = gated(cotangent, attn_part).astype(f32)
    grad_ffn = (gate_two * grad_out).astype(bf16)
    came_a = gated(came_a, grad_ffn)
    own_b, came_b = swap_start(gated(attn_part, came_a), groups, 1)
    came_b = gated(came_b, came_a)
    attn_out = jnp.concatenate(
        [swap_end(own_a, came_a, groups), swap_end(own_b, came_b, groups)], axis=0
    )
    me = dp_index.astype(jnp.int32)[None]
    depth_bits = list(range(2, size.bit_length() - 1))
    side_first = [0, 1] + depth_bits
    line_first = [0, 2, 1] + depth_bits[1:]

    residual = resid_in + gate_one * attn_out
    factor_two = inv_rms(residual)
    normed_two = residual * factor_two
    ffn_in = (normed_two * gain_two * (1.0 + scale_two)).astype(bf16)
    full_ffn = gated(ffn_set, attn_part)
    hidden, dboth = feed_forward(ffn_in, grad_ffn, full_ffn, units, tile)
    def staged(left, right, bits, tile_cols):
        return Halving(size, bits, *outer_grads(me, left, right, size, bits, tile_cols))

    dffn_one = product(dboth, full_ffn, model_dim, 512, bf16, True, 0, None, (0, 2))
    dffn_two = product(gated(dboth, dffn_one), full_ffn, model_dim, 512, bf16, True, 0, None, (1, 2))
    one_own, one_came = swap_start(dffn_one, groups, 1)
    down = staged(grad_ffn, gated(hidden, dffn_two), line_first, 512)
    down.start()
    one_came = gated(one_came, down.out)
    two_own, two_came = swap_start(gated(dffn_two, one_came), groups, 1)
    grown = staged(ffn_in, gated(dboth, down.out, one_came), side_first, 512)
    grown.start()
    ffn_part = product(gated(hidden, grown.out, mod_set), full_ffn, model_dim, 512, bf16, True, 2)
    two_came = gated(two_came, ffn_part)
    down.finish(two_came)
    down.start()
    grown.finish(down.out)
    grown.start()
    dffn_in = jnp.concatenate(
        [swap_end(one_own, one_came, groups), swap_end(two_own, two_came, groups)], axis=0
    )

    gain_mul = gain_two * (1.0 + scale_two)
    weighed = jnp.sum(dffn_in * normed_two, axis=0)
    grad_gaintwo = weighed * (1.0 + scale_two[0])
    dscale_two = weighed * gain_two
    dresid = grad_out + norm_back(dffn_in * gain_mul, normed_two, factor_two)
    dgate_one = jnp.sum(dresid * attn_out, axis=0) * (1.0 - gate_one[0] ** 2)
    grad_attn = (gate_one * dresid).astype(bf16)
    dmixed = product(grad_attn, full_qkvo, padded, LANES, bf16, False, 3 * padded // LANES)
    ffn_own, ffn_came = swap_start(gated(ffn_part, dmixed), groups, 1)
    dq_cross, dtext, stats_c = cross_back(
        caption_lens, query_bf, tkv_bf, text_raw, cross_out, lse, dmixed, tables, head_dim
    )
    down.finish(dq_cross)
    down.start()
    grown.finish(down.out)
    grown.start()
    text = staged(cap_in, gated(dtext, grown.out), side_first, 256)
    text.start()
    split = pairs - pairs // 2
    windows = [(0, split), (split, pairs - split)]
    common = (query_bf, kv_bf, qkv_raw, own_out, lse)
    dmixed_a = gated(dmixed, text.out)
    gate_part = jnp.sum(grad_out * gated(ffn_part, dmixed).astype(f32), axis=0)
    dqkv_a, stats_a = self_back(windows[0], *common, dmixed_a, dq_cross, tables, head_dim)
    down.finish(dqkv_a)
    down.start()
    grown.finish(down.out)
    grown.start()
    text.finish(grown.out)
    text.start()
    first_qkv = staged(attn_in, gated(dqkv_a, text.out), line_first, 3 * LANES)
    first_qkv.start()
    outp = staged(gated(grad_attn, first_qkv.out), mixed_heads, side_first, padded)
    outp.start()
    edge = 3 * LANES * split
    even = pairs == 2 * split
    wide_a = full_qkvo if even else full_qkvo[:, :edge]
    wide_b = full_qkvo if even else full_qkvo[:, edge : 3 * padded]
    dattn_a = product(gated(dqkv_a, outp.out), wide_a, model_dim, 512, f32, True)
    dmixed_b = gated(dmixed, dattn_a, gate_part)
    dqkv_b, stats_b = self_back(windows[1], *common, dmixed_b, dq_cross, tables, head_dim)
    landed = (down.land(dqkv_b), grown.land(dqkv_b), gated(ffn_came, dqkv_b))
    ffn_came = landed[2]
    dqkv_l = gated(dqkv_b, *landed)
    dattn_part = product(dqkv_l, wide_b, model_dim, 512, bf16, True, int(even), dattn_a)
    half_rows = dattn_part.shape[0] // 2
    high_own, high_came = swap_start(dattn_part[:half_rows], groups, 1)
    last_qkv = staged(attn_in, gated(dqkv_b, dattn_part), side_first, 3 * LANES)
    last_qkv.start()
    text.finish(last_qkv.out)
    text.start()
    first_qkv.finish(text.out)
    first_qkv.start()
    outp.finish(first_qkv.out)
    outp.start()
    caption_part = product(gated(dtext, outp.out), full_text, cap_in.shape[1], 1024, bf16, True)
    high_came = gated(high_came, caption_part)
    base_own, base_came = swap_start(gated(dattn_part[half_rows:], high_came), groups, 1)
    last_qkv.finish(high_came)
    last_qkv.start()
    weighed_part = jnp.sum(gated(dattn_part, last_qkv.out).astype(f32) * normed_one, axis=0)
    grad_gate, grad_up = gather_sum(grown.drain(last_qkv.out), tile, 2, units)
    down_terms = down.drain(grad_gate)
    down_t = sum(term.astype(f32) for term in down_terms)
    text.finish(down_t)
    text.start()
    outp.finish(text.out)
    outp.start()
    first_qkv.finish(outp.out)
    first_qkv.start()
    base_came = gated(base_came, first_qkv.out)
    stats = jnp.concatenate([stats_a, stats_b], axis=1)[:2]
    stat_sums = jnp.concatenate([stats, stats_c[:2]], axis=0)[:, :chan]
    stat_sums = jnp.sum(stat_sums.reshape(4, heads_here, head_dim), axis=(1,))
    xgate_rows = stats_c[1, :chan].reshape(heads_here, head_dim)
    xgate_here = jnp.sum(xgate_rows, axis=1) * (1.0 - tanh_cross**2)
    sums_part = jnp.concatenate([weighed_part, gate_part, stat_sums[:3].reshape(-1)])[None]
    sums = small_sum(gated(sums_part, base_came), "tensor", groups)[0]
    dattn_in = jnp.concatenate(
        [swap_end(high_own, high_came, groups), swap_end(base_own, base_came, groups)], axis=0
    )
    grad_latents = (
        dresid + norm_back(dattn_in * gain_one * (1.0 + scale_one), normed_one, factor_one)
    ).astype(bf16)
    last_qkv.finish(grad_latents)
    last_qkv.start()
    sums = gated(sums, last_qkv.out)
    weighed_one, head_gains = sums[:model_dim], sums[2 * model_dim :]
    dgate_two = sums[model_dim : 2 * model_dim] * (1.0 - gate_two[0] ** 2)
    grad_gainone = weighed_one * (1.0 + scale_one[0])
    dscale_one = weighed_one * gain_one
    dmod_all = jnp.concatenate([dscale_one, dgate_one, dscale_two, dgate_two])
    cols_here = modulation.shape[1]
    dmod_here = lax.dynamic_slice_in_dim(dmod_all, tensor_index * cols_here, cols_here, 0)
    row = jnp.concatenate([dmod_here, grad_gainone, grad_gaintwo, head_gains, xgate_here])
    row = row.astype(bf16).astype(f32)[None]
    dcaption = tensor_scatter(gated(caption_part, sums), groups)
    ffn_out = swap_end(ffn_own, gated(ffn_came, row), groups)
    output = (residual + gate_two * ffn_out).astype(bf16)
    embed_row = jnp.einsum(
        "bc,tc->bt", row[:, :cols_here].astype(bf16), mod_set, preferred_element_type=f32
    )
    first_qkv.finish(output)
    first_qkv.start()
    outp.finish(first_qkv.out)
    outp.start()
    rows_set = small_gather(row, "dp", size, [row, output, first_qkv.out, outp.out])
    grad_textkey, grad_textval = gather_sum(text.drain(outp.out), LANES, 2, chan)
    last_qkv.finish(grad_textkey)
    last_qkv.start()
    dmod_set = rows_set[:, :cols_here].astype(bf16)
    gain_sums = jnp.sum(rows_set[:, cols_here:], axis=0)
    grad_modul = jnp.einsum("bt,bc->tc", cond_here, dmod_set, preferred_element_type=f32)
    embed_sum = small_sum(embed_row, "tensor", groups)
    embed_own = lax.dynamic_slice_in_dim(embed_all, dp_index, 1, 0)
    sig_own = jax.nn.sigmoid(embed_own)
    dembed_all = embed_sum * (sig_own * (1.0 + embed_own * (1.0 - sig_own)))
    width = embed_dim // groups
    dembed = lax.dynamic_slice_in_dim(dembed_all, tensor_index * width, width, 1)
    output_t = sum(term.astype(f32) for term in outp.drain(last_qkv.out))
    wide = min(split * LANES, chan)
    parts_a = gather_sum(first_qkv.drain(output_t), LANES, 3, wide)
    parts_b = gather_sum(last_qkv.drain(parts_a[0]), LANES, 3, chan - wide)
    grad_query, grad_key, grad_value = [
        jnp.concatenate([one, two], axis=1) for one, two in zip(parts_a, parts_b)
    ]

    def own_part(start, width):
        return lax.dynamic_slice_in_dim(gain_sums, start + dp_index * width, width, 0)

    heads_at = 2 * model_dim
    gate_at = heads_at + 3 * head_dim
    return (
        output,
        grad_latents,
        dcaption.astype(bf16)[None],
        dembed,
        grad_query,
        grad_key,
        grad_value,
        output_t[:, :chan].T,
        grad_textkey,
        grad_textval,
        grad_gate,
        grad_up,
        down_t.T,
        grad_modul,
        own_part(0, rows_w),
        own_part(model_dim, rows_w),
        own_part(heads_at, head_part),
        own_part(heads_at + head_dim, head_part),
        own_part(heads_at + 2 * head_dim, head_part),
        gain_sums[gate_at:],
    )


def solution(mesh):
    in_specs = (
        P("dp", None),
        P("dp", None),
        P("dp", None, None),
        P("dp"),
        P("dp", None),
        P("dp", None),
        P("dp"),
        P("dp", "tensor"),
        P("dp", "tensor"),
        P("dp", "tensor"),
        P("tensor", "dp"),
        P("dp", "tensor"),
        P("dp", "tensor"),
        P("dp", "tensor"),
        P("dp", "tensor"),
        P("tensor", "dp"),
        P("dp", "tensor"),
        P("dp"),
        P("dp"),
        P("dp"),
        P("dp"),
        P("dp"),
        P("tensor"),
    )
    out_specs = (
        P("dp", None),
        P("dp", None),
        P("dp", None, "tensor"),
        P("dp", "tensor"),
        P("dp", "tensor"),
        P("dp", "tensor"),
        P("dp", "tensor"),
        P("tensor", "dp"),
        P("dp", "tensor"),
        P("dp", "tensor"),
        P("dp", "tensor"),
        P("dp", "tensor"),
        P("tensor", "dp"),
        P("dp", "tensor"),
        P("dp"),
        P("dp"),
        P("dp"),
        P("dp"),
        P("dp"),
        P("tensor"),
    )
    bound = functools.partial(local, mesh.shape["dp"], mesh.shape["tensor"])
    return jax.shard_map(bound, mesh=mesh, in_specs=in_specs, out_specs=out_specs, check_vma=False)
```

```python
import functools
import math

import jax
import jax.numpy as jnp
from jax import lax
from jax.experimental import pallas as pl
from jax.experimental.pallas import tpu as pltpu
from jax.sharding import PartitionSpec as P

EPSILON = 1e-06


def inv_rms(values):
    return lax.rsqrt(jnp.mean(values * values, axis=-1, keepdims=True) + EPSILON)


def time_embed(step_vals, embed_width):
    half_width = embed_width // 2
    frequency = jnp.exp(-math.log(10000.0) * jnp.arange(half_width, dtype=jnp.float32) / half_width)
    phases = step_vals.astype(jnp.float32)[:, None] * frequency
    return jnp.concatenate([jnp.cos(phases), jnp.sin(phases)], axis=1)


def norm_back(grad_hat, normed, factor):
    return factor * (grad_hat - normed * jnp.mean(grad_hat * normed, axis=-1, keepdims=True))


LANES = 128
LIGHT = pl.CostEstimate(flops=1, transcendentals=0, bytes_accessed=1)


def lane_ids(rows):
    return lax.broadcasted_iota(jnp.int32, (rows, LANES), 1)


def pair_matrix(same, half):
    row = lax.broadcasted_iota(jnp.int32, (LANES, LANES), 0) // half
    col = lax.broadcasted_iota(jnp.int32, (LANES, LANES), 1) // half
    return jnp.where((row == col) == same, 1.0, 0.0).astype(jnp.bfloat16)


def head_sums(values, matrix):
    high = values.astype(jnp.bfloat16)
    low = (values - high.astype(jnp.float32)).astype(jnp.bfloat16)
    return jnp.dot(high, matrix, preferred_element_type=jnp.float32) + jnp.dot(
        low, matrix, preferred_element_type=jnp.float32
    )


def swap_quarters(values, half):
    rows = values.shape[0]
    first = lane_ids(rows) % half < half // 2
    return jnp.where(
        first,
        pltpu.roll(values, LANES - half // 2, 1),
        pltpu.roll(values, half // 2, 1),
    )


def nt_dot(left, right):
    return lax.dot_general(
        left, right, (((1,), (1,)), ((), ())), preferred_element_type=jnp.float32
    )


def tn_dot(left, right):
    return lax.dot_general(
        left, right, (((0,), (0,)), ((), ())), preferred_element_type=jnp.float32
    )


def attend_kernel(half, block, fresh, *refs):
    f32, bf16 = jnp.float32, jnp.bfloat16
    matrix = pair_matrix(True, half)
    if fresh:
        len_ref, rawq_ref, rawk_ref, rawv_ref, text_ref, tval_ref = refs[:6]
        cos_ref, sin_ref, cosk_ref, sink_ref, gain_ref, tanh_ref = refs[6:12]
        mixed_ref, query_ref, own_ref, cross_ref, lse_ref, kv_ref, tkv_ref = refs[12:]
    else:
        len_ref, rawq_ref, kv_ref, tkv_ref, cos_ref, sin_ref, gain_ref, tanh_ref = refs[:8]
        mixed_ref, query_ref, own_ref, cross_ref, lse_ref = refs[12:]

    def hat(raw):
        return raw * lax.rsqrt(head_sums(raw * raw, matrix) * (1.0 / half) + EPSILON)

    def turned(raw, gain, cosine, sine):
        value = hat(raw) * gain
        return (value * cosine + swap_quarters(value, half) * sine).astype(bf16)

    query_ref[...] = turned(rawq_ref[...], gain_ref[0:1], cos_ref[...], sin_ref[...])
    if fresh:
        kv_ref[:, :LANES] = turned(rawk_ref[...], gain_ref[1:2], cosk_ref[...], sink_ref[...])
        kv_ref[:, LANES:] = rawv_ref[...].astype(bf16)
        tkv_ref[:, :LANES] = (hat(text_ref[...]) * gain_ref[2:3]).astype(bf16)
        tkv_ref[:, LANES:] = tval_ref[...].astype(bf16)
    key, value = kv_ref[:, :LANES], kv_ref[:, LANES:]
    tkey, tval = tkv_ref[:, :LANES], tkv_ref[:, LANES:]
    one = jnp.ones((), bf16)
    zero = jnp.zeros((), bf16)

    def pick(a, b):
        return jnp.where(lane_ids(a.shape[0]) < half, a, b)

    def fill(a, fillers, first):
        other = jnp.full(a.shape, fillers, bf16)
        return pick(a, other) if first else pick(other, a)

    value_ones = [fill(value, one, True), fill(value, one, False)]
    tval_ones = [fill(tval, one, True), fill(tval, one, False)]
    keep = lax.broadcasted_iota(jnp.int32, (block, tkey.shape[0]), 1) < len_ref[0]

    def step(i, _):
        here = pl.ds(pl.multiple_of(i * block, block), block)
        q_blk = query_ref[here, :] * jnp.asarray(half**-0.5, bf16)
        outs = []
        texts = []
        for head in range(2):
            q_one = fill(q_blk, zero, head == 0)
            e_self = jnp.exp(nt_dot(q_one, key)).astype(bf16)
            outs.append(jnp.dot(e_self, value_ones[head], preferred_element_type=f32))
            e_text = jnp.where(keep, jnp.exp(nt_dot(q_one, tkey)), 0.0).astype(bf16)
            texts.append(jnp.dot(e_text, tval_ones[head], preferred_element_type=f32))
        for n, (a, b) in enumerate((outs, texts)):
            total = pick(b, a)
            lse_ref[here, n * LANES : (n + 1) * LANES] = jnp.log(total)
            res = pick(a, b) / pltpu.roll(total, half, 1)
            if n == 0:
                own = res
                own_ref[here, :] = res
            else:
                cross_ref[here, :] = res
                mixed_ref[here, :] = (own + tanh_ref[0:1] * res).astype(bf16)
        return 0

    lax.fori_loop(0, query_ref.shape[0] // block, step, 0)


def attend_rows(part, cap_len, raw, text, tables, half, kept=None):
    cosine, sine, gains, tanh_lanes = tables
    rows, caps = raw.shape[0], text.shape[0]
    count = rows // 2
    width = tanh_lanes.shape[1]
    f32, bf16 = jnp.float32, jnp.bfloat16
    fresh = kept is None

    def piece(scale, shift, wide=1):
        return pl.BlockSpec((count, wide * LANES), lambda p: (part, scale * p + shift))

    table = pl.BlockSpec((count, LANES), lambda p: (part, 0))
    whole = pl.BlockSpec(memory_space=pl.ANY)
    smem = pl.BlockSpec(memory_space=pltpu.SMEM)
    kv_block = pl.BlockSpec((rows, 2 * LANES), lambda p: (0, p))
    tkv_block = pl.BlockSpec((caps, 2 * LANES), lambda p: (0, p))
    tail_specs = [fixed_block(8), lane_block(8, 1, 0)]
    out_specs = [
        pl.BlockSpec((count, LANES), lambda p: (0, p)),
        piece(1, 0),
        piece(1, 0),
        piece(1, 0),
        piece(1, 0, 2),
    ]
    out_shape = [
        jax.ShapeDtypeStruct((count, width), bf16),
        jax.ShapeDtypeStruct((rows, width), bf16),
        jax.ShapeDtypeStruct((rows, width), f32),
        jax.ShapeDtypeStruct((rows, width), f32),
        jax.ShapeDtypeStruct((rows, 2 * width), f32),
    ]
    if fresh:
        in_specs = [smem, piece(3, 0), lane_block(rows, 3, 1), lane_block(rows, 3, 2)]
        in_specs += [lane_block(caps, 2, 0), lane_block(caps, 2, 1)]
        in_specs += [table, table, fixed_block(rows), fixed_block(rows)] + tail_specs
        operands = (cap_len, raw, raw, raw, text, text, cosine, sine, cosine, sine)
        operands += (gains, tanh_lanes)
        out_specs += [kv_block, tkv_block]
        out_shape += [
            jax.ShapeDtypeStruct((rows, 2 * width), bf16),
            jax.ShapeDtypeStruct((caps, 2 * width), bf16),
        ]
        aliases = {}
    else:
        query, own, cross, lse, kv, tkv = kept
        in_specs = [smem, piece(3, 0), kv_block, tkv_block, table, table] + tail_specs
        in_specs += [whole] * 4
        operands = (cap_len, raw, kv, tkv, cosine, sine, gains, tanh_lanes)
        operands += (query, own, cross, lse)
        aliases = {8: 1, 9: 2, 10: 3, 11: 4}
    return pl.pallas_call(
        functools.partial(attend_kernel, half, min(256, count), fresh),
        grid=(width // LANES,),
        in_specs=in_specs,
        out_specs=out_specs,
        out_shape=out_shape,
        input_output_aliases=aliases,
        compiler_params=pltpu.CompilerParams(vmem_limit_bytes=50 * 2**20),
        cost_estimate=LIGHT,
        name="attend_fwd",
    )(*operands)


def pick_head(a, b, first, half):
    low = lane_ids(a.shape[0]) < half
    return jnp.where(low, a, b) if first else jnp.where(low, b, a)


def three_parts(value, half):
    spot = lane_ids(value.shape[0]) % half
    high = value.astype(jnp.bfloat16).astype(jnp.float32)
    rest = value - high
    mid = rest.astype(jnp.bfloat16).astype(jnp.float32)
    low = rest - mid
    parts = jnp.where(spot == 0, high, jnp.where(spot == 1, mid, jnp.where(spot == 2, low, 0.0)))
    return parts.astype(jnp.bfloat16)


def with_ones(value, first, half):
    ones = jnp.where(lane_ids(value.shape[0]) % half < 3, 1.0, 0.0).astype(jnp.bfloat16)
    return pick_head(value, ones, first, half)


def only_head(value, first, half):
    return pick_head(value, jnp.zeros(value.shape, jnp.bfloat16), first, half)


def norm_return(grad_in, raw, gain, half, turn):
    same = pair_matrix(True, half)
    inv = lax.rsqrt(head_sums(raw * raw, same) * (1.0 / half) + EPSILON)
    normed = raw * inv
    back = grad_in.astype(jnp.bfloat16).astype(jnp.float32)
    if turn is not None:
        back = back * turn[0][...] - swap_quarters(back, half) * turn[1][...]
    scaled = back * gain
    mean = head_sums(scaled * normed, same) * (1.0 / half)
    stat = jnp.sum(back * normed, axis=0, keepdims=True)
    return (inv * (scaled - normed * mean)).astype(jnp.bfloat16), stat


def score_grads(key_aug, val_aug, q_aug, o_aug, keep):
    probs = jnp.exp(nt_dot(key_aug, q_aug))
    if keep is not None:
        probs = jnp.where(keep, probs, 0.0)
    return probs.astype(jnp.bfloat16), (probs * nt_dot(val_aug, o_aug)).astype(jnp.bfloat16)


def cross_back_kernel(
    half,
    block,
    len_ref,
    query_ref,
    tkv_ref,
    text_ref,
    cross_ref,
    lse_ref,
    dmix_ref,
    gain_ref,
    tanh_ref,
    dq_ref,
    dtext_ref,
    stat_ref,
    qs_ref,
    os_ref,
    dk_ref,
    dv_ref,
):
    f32, bf16 = jnp.float32, jnp.bfloat16
    rows, caps = query_ref.shape[0], tkv_ref.shape[0]
    grad_f = dmix_ref[...].astype(f32)
    other = (grad_f * tanh_ref[0:1]).astype(bf16)
    delta = three_parts(
        -head_sums(other.astype(f32) * cross_ref[...], pair_matrix(False, half)), half
    )
    lse = three_parts(-lse_ref[...], half)
    query = query_ref[...] * jnp.asarray(half**-0.5, bf16)
    tkey, tval = tkv_ref[:, :LANES], tkv_ref[:, LANES:]
    for head in range(2):
        qs_ref[head] = pick_head(query, lse, head == 0, half)
        os_ref[head] = pick_head(other, delta, head == 0, half)
    key_aug = [with_ones(tkey, h == 0, half) for h in range(2)]
    val_aug = [with_ones(tval, h == 0, half) for h in range(2)]
    key_only = [only_head(tkey, h == 0, half) for h in range(2)]
    dk_ref[...] = jnp.zeros_like(dk_ref)
    dv_ref[...] = jnp.zeros_like(dv_ref)
    keep = lax.broadcasted_iota(jnp.int32, (caps, block), 0) < len_ref[0]

    def step(i, _):
        here = pl.ds(pl.multiple_of(i * block, block), block)
        dq = jnp.zeros((block, LANES), f32)
        for head in range(2):
            q_aug, o_aug = qs_ref[head, here], os_ref[head, here]
            probs, grads = score_grads(key_aug[head], val_aug[head], q_aug, o_aug, keep)
            dv_ref[...] += jnp.dot(
                probs, only_head(o_aug, head == 0, half), preferred_element_type=f32
            )
            dk_ref[...] += jnp.dot(
                grads, only_head(q_aug, head == 0, half), preferred_element_type=f32
            )
            dq += tn_dot(grads, key_only[head])
        dq_ref[here, :] = dq * half**-0.5
        return 0

    lax.fori_loop(0, rows // block, step, 0)
    res, stat_t = norm_return(dk_ref[...], text_ref[...], gain_ref[2:3], half, None)
    dtext_ref[:, :LANES] = res
    dtext_ref[:, LANES:] = dv_ref[...].astype(bf16)
    stat_x = jnp.sum(grad_f * cross_ref[...], axis=0, keepdims=True)
    stat_ref[...] = jnp.concatenate([stat_t, stat_x, jnp.zeros((6, LANES), f32)], axis=0)


def self_back_kernel(
    half,
    block,
    query_ref,
    key_ref,
    val_ref,
    rawq_ref,
    rawk_ref,
    own_ref,
    lse_ref,
    dmix_ref,
    dqc_ref,
    cos_ref,
    sin_ref,
    gain_ref,
    dqkv_ref,
    stat_ref,
    qs_ref,
    os_ref,
    dq_ref,
    dk_ref,
    dv_ref,
):
    f32, bf16 = jnp.float32, jnp.bfloat16
    rows = query_ref.shape[0]
    grad = dmix_ref[...]
    delta = three_parts(
        -head_sums(grad.astype(f32) * own_ref[...], pair_matrix(False, half)), half
    )
    lse = three_parts(-lse_ref[...], half)
    query = query_ref[...] * jnp.asarray(half**-0.5, bf16)
    key, value = key_ref[...], val_ref[...]
    for head in range(2):
        qs_ref[head] = pick_head(query, lse, head == 0, half)
        os_ref[head] = pick_head(grad, delta, head == 0, half)
    key_aug = [with_ones(key, h == 0, half) for h in range(2)]
    val_aug = [with_ones(value, h == 0, half) for h in range(2)]
    key_only = [only_head(key, h == 0, half) for h in range(2)]
    dk_ref[...] = jnp.zeros_like(dk_ref)
    dv_ref[...] = jnp.zeros_like(dv_ref)

    def step(i, _):
        here = pl.ds(pl.multiple_of(i * block, block), block)
        dq = jnp.zeros((block, LANES), f32)
        for head in range(2):
            q_aug, o_aug = qs_ref[head, here], os_ref[head, here]
            probs, grads = score_grads(key_aug[head], val_aug[head], q_aug, o_aug, None)
            dv_ref[...] += jnp.dot(
                probs, only_head(o_aug, head == 0, half), preferred_element_type=f32
            )
            dk_ref[...] += jnp.dot(
                grads, only_head(q_aug, head == 0, half), preferred_element_type=f32
            )
            dq += tn_dot(grads, key_only[head])
        dq_ref[here, :] = dqc_ref[here, :] + dq * half**-0.5
        return 0

    lax.fori_loop(0, rows // block, step, 0)
    turn = (cos_ref, sin_ref)
    res, stat_q = norm_return(dq_ref[...], rawq_ref[...], gain_ref[0:1], half, turn)
    dqkv_ref[:, :LANES] = res
    res, stat_k = norm_return(dk_ref[...], rawk_ref[...], gain_ref[1:2], half, turn)
    dqkv_ref[:, LANES : 2 * LANES] = res
    dqkv_ref[:, 2 * LANES :] = dv_ref[...].astype(bf16)
    stat_ref[...] = jnp.concatenate([stat_q, stat_k, jnp.zeros((6, LANES), f32)], axis=0)


def lane_block(rows, scale, shift):
    return pl.BlockSpec((rows, LANES), lambda p: (0, scale * p + shift))


def fixed_block(rows):
    return pl.BlockSpec((rows, LANES), lambda p: (0, 0))


def cross_back(cap_len, query, tkv, text, cross, lse, dmix, tables, half):
    gains, tanh_lanes = tables[2], tables[3]
    rows, caps = query.shape[0], text.shape[0]
    width = dmix.shape[1]
    f32, bf16 = jnp.float32, jnp.bfloat16
    return pl.pallas_call(
        functools.partial(cross_back_kernel, half, min(512, rows)),
        grid=(width // LANES,),
        in_specs=[
            pl.BlockSpec(memory_space=pltpu.SMEM),
            lane_block(rows, 1, 0),
            pl.BlockSpec((caps, 2 * LANES), lambda p: (0, p)),
            lane_block(caps, 2, 0),
            lane_block(rows, 1, 0),
            lane_block(rows, 2, 1),
            lane_block(rows, 1, 0),
            fixed_block(8),
            lane_block(8, 1, 0),
        ],
        out_specs=[
            lane_block(rows, 1, 0),
            pl.BlockSpec((caps, 2 * LANES), lambda p: (0, p)),
            lane_block(8, 1, 0),
        ],
        out_shape=[
            jax.ShapeDtypeStruct((rows, width), f32),
            jax.ShapeDtypeStruct((caps, 2 * width), bf16),
            jax.ShapeDtypeStruct((8, width), f32),
        ],
        scratch_shapes=[pltpu.VMEM((2, rows, LANES), bf16)] * 2
        + [pltpu.VMEM((caps, LANES), f32)] * 2,
        compiler_params=pltpu.CompilerParams(vmem_limit_bytes=40 * 2**20),
        cost_estimate=LIGHT,
        name="cross_bwd",
    )(cap_len, query, tkv, text, cross, lse, dmix, gains, tanh_lanes)


def self_back(window, query, kv, raw, own, lse, dmix, dq_cross, tables, half):
    cosine, sine, gains, _ = tables
    first, pairs = window
    rows = raw.shape[0]
    width = pairs * LANES
    f32, bf16 = jnp.float32, jnp.bfloat16
    return pl.pallas_call(
        functools.partial(self_back_kernel, half, min(512, rows)),
        grid=(pairs,),
        in_specs=[
            lane_block(rows, 1, first),
            lane_block(rows, 2, 2 * first),
            lane_block(rows, 2, 2 * first + 1),
            lane_block(rows, 3, 3 * first),
            lane_block(rows, 3, 3 * first + 1),
            lane_block(rows, 1, first),
            lane_block(rows, 2, 2 * first),
            lane_block(rows, 1, first),
            lane_block(rows, 1, first),
            fixed_block(rows),
            fixed_block(rows),
            fixed_block(8),
        ],
        out_specs=[pl.BlockSpec((rows, 3 * LANES), lambda p: (0, p)), lane_block(8, 1, 0)],
        out_shape=[
            jax.ShapeDtypeStruct((rows, 3 * width), bf16),
            jax.ShapeDtypeStruct((8, width), f32),
        ],
        scratch_shapes=[pltpu.VMEM((2, rows, LANES), bf16)] * 2
        + [pltpu.VMEM((rows, LANES), f32)] * 3,
        compiler_params=pltpu.CompilerParams(vmem_limit_bytes=50 * 2**20),
        cost_estimate=LIGHT,
        name="self_bwd",
    )(query, kv, kv, raw, raw, own, lse, dmix, dq_cross, cosine, sine, gains)


def feed_kernel(x_ref, grad_ref, gate_ref, up_ref, down_ref, *refs):
    f32, bf16 = jnp.float32, jnp.bfloat16
    hidden_ref, both_ref = refs[-2:]
    gate = jnp.dot(x_ref[...], gate_ref[...], preferred_element_type=f32)
    up = jnp.dot(x_ref[...], up_ref[...], preferred_element_type=f32)
    dhidden = jnp.dot(grad_ref[...], down_ref[...], preferred_element_type=f32)
    sig = 1.0 / (1.0 + jnp.exp(-gate))
    act = gate * sig
    hidden_ref[...] = (act * up).astype(bf16)
    tile = gate_ref.shape[1]
    both_ref[:, :tile] = (dhidden * up * sig * (1.0 + gate * (1.0 - sig))).astype(bf16)
    both_ref[:, tile:] = (dhidden * act).astype(bf16)


def feed_forward(part, x, grad, weights, units, tile, kept=()):
    count, depth = x.shape
    rows = grad.shape[0]
    blocks = units // tile
    bf16 = jnp.bfloat16

    def cols(scale, shift):
        return pl.BlockSpec((depth, tile), lambda j: (0, scale * j + shift))

    return pl.pallas_call(
        feed_kernel,
        grid=(blocks,),
        in_specs=[
            pl.BlockSpec((count, depth), lambda j: (0, 0)),
            pl.BlockSpec((count, depth), lambda j: (part, 0)),
            cols(2, 0),
            cols(2, 1),
            cols(1, 2 * blocks),
        ]
        + [pl.BlockSpec(memory_space=pl.ANY)] * len(kept),
        out_specs=[
            pl.BlockSpec((count, tile), lambda j: (part, j)),
            pl.BlockSpec((count, 2 * tile), lambda j: (part, j)),
        ],
        out_shape=[
            jax.ShapeDtypeStruct((rows, units), bf16),
            jax.ShapeDtypeStruct((rows, 2 * units), bf16),
        ],
        input_output_aliases={5 + n: n for n in range(len(kept))},
        compiler_params=pltpu.CompilerParams(vmem_limit_bytes=58 * 2**20),
        cost_estimate=LIGHT,
        name="feed_forward",
    )(x, grad, weights, weights, weights, *kept)


def outer_kernel(size, bits, me_ref, left_ref, right_ref, keep_ref, away_ref, total_ref):
    total_ref[...] = tn_dot(left_ref[...], right_ref[...])
    rows = keep_ref.shape[0] // (size // 2)
    for place in range(size):
        slot = sum(((place >> (len(bits) - 1 - k)) & 1) << bit for k, bit in enumerate(bits))
        start = pl.multiple_of((me_ref[0] ^ slot) * rows, 16)
        block = total_ref[pl.ds(start, rows), :].astype(jnp.bfloat16)
        out_ref = keep_ref if place < size // 2 else away_ref
        spot = place % (size // 2)
        out_ref[spot * rows : (spot + 1) * rows, :] = block


def outer_grads(me, left, right, size, bits, tile):
    tokens, depth = left.shape
    cols = right.shape[1]
    half = jax.ShapeDtypeStruct((depth // 2, cols), jnp.bfloat16)
    return pl.pallas_call(
        functools.partial(outer_kernel, size, bits),
        grid=(cols // tile,),
        in_specs=[
            pl.BlockSpec(memory_space=pltpu.SMEM),
            pl.BlockSpec((tokens, depth), lambda j: (0, 0)),
            pl.BlockSpec((tokens, tile), lambda j: (0, j)),
        ],
        out_specs=[pl.BlockSpec((depth // 2, tile), lambda j: (0, j))] * 2,
        out_shape=[half, half],
        scratch_shapes=[pltpu.VMEM((depth, tile), jnp.float32)],
        compiler_params=pltpu.CompilerParams(vmem_limit_bytes=50 * 2**20),
        cost_estimate=LIGHT,
        name="outer_grads",
    )(me, left, right)


def product_kernel(turned, has_add, *refs):
    left_ref, right_ref = refs[:2]
    dot = nt_dot if turned else (lambda a, b: jnp.dot(a, b, preferred_element_type=jnp.float32))
    total = dot(left_ref[...], right_ref[...])
    if has_add:
        total = total + refs[2][...].astype(jnp.float32)
    refs[-1][...] = total.astype(refs[-1].dtype)


def product(left, right, cols, tile, dtype, turned=False, shift=0, add=None, part=(0, 1)):
    depth = left.shape[1]
    rows = left.shape[0] // part[1]
    if turned:
        right_block = pl.BlockSpec((tile, depth), lambda j: (j, shift))
    else:
        right_block = pl.BlockSpec((depth, tile), lambda j: (0, j + shift))
    in_specs = [pl.BlockSpec((rows, depth), lambda j: (part[0], 0)), right_block]
    if add is not None:
        in_specs.append(pl.BlockSpec((rows, tile), lambda j: (0, j)))
    return pl.pallas_call(
        functools.partial(product_kernel, turned, add is not None),
        grid=(cols // tile,),
        in_specs=in_specs,
        out_specs=pl.BlockSpec((rows, tile), lambda j: (0, j)),
        out_shape=jax.ShapeDtypeStruct((rows, cols), dtype),
        compiler_params=pltpu.CompilerParams(vmem_limit_bytes=58 * 2**20),
        cost_estimate=LIGHT,
        name="product",
    )(left, right, *([] if add is None else [add]))


def gated(value, *tokens):
    return lax.optimization_barrier((value,) + tokens)[0]


def flip_perm(size, bit):
    return [(i, i ^ bit) for i in range(size)]


class SmallScatter:
    def __init__(self, value, size):
        self.value, self.size, self.bit = value, size, 0

    def left(self):
        return self.value.shape[0] > 1

    def hop(self, *tokens):
        if not self.left():
            return None
        index = lax.axis_index("dp")
        value = gated(self.value, *tokens) if tokens else self.value
        pairs = value.reshape(value.shape[0] // 2, 2, value.shape[1])
        upper = (index >> self.bit) % 2 == 1
        away = jnp.where(upper, pairs[:, 0], pairs[:, 1])
        came = lax.ppermute(away, "dp", flip_perm(self.size, 1 << self.bit))
        self.value = jnp.where(upper, pairs[:, 1], pairs[:, 0]) + came
        self.bit += 1
        return came


class Halving:
    def __init__(self, size, bits, keep, away):
        self.size, self.bits, self.stage = size, bits, 0
        self.terms = [keep]
        self.whole = [keep]
        self.out = away

    def start(self):
        bit = self.bits[self.stage]
        self.came = lax.ppermute(self.out, "dp", flip_perm(self.size, 1 << bit))
        self.stage += 1

    def land(self, *tokens):
        self.came = gated(self.came, *tokens)
        return self.came

    def finish(self, *tokens):
        came = gated(self.came, *tokens) if tokens else self.came
        self.terms.append(came)
        self.whole.append(came)
        rows = self.terms[-1].shape[0]
        last = self.stage == len(self.bits)
        half = rows if last else rows // 2
        low = 0 if last else half
        total = sum(term[low : low + half].astype(jnp.float32) for term in self.terms)
        self.out = total if last else total.astype(jnp.bfloat16)
        self.terms = [term[:half] for term in self.terms]
        return self.out

    def drain(self, *tokens):
        while self.stage < len(self.bits):
            self.finish(*tokens)
            self.start()
            tokens = ()
        came = gated(self.came, *tokens) if tokens else self.came
        return self.whole + [came]


def swap_start(part, size, chunks):
    step = part.shape[0] // chunks
    own = [part[i * step : (i + 1) * step] for i in range(chunks)]
    if size == 2:
        return own, [lax.ppermute(o, "tensor", flip_perm(size, 1)) for o in own]
    return own, [lax.psum(o, "tensor") for o in own]


def swap_end(own, came, size):
    f32 = jnp.float32
    both = [o.astype(f32) + c.astype(f32) if size == 2 else c.astype(f32) for o, c in zip(own, came)]
    return jnp.concatenate(both, axis=0) if len(both) > 1 else both[0]


def small_gather(value, name, size, tokens=(), steps=None):
    index = lax.axis_index(name)
    for k in range(size.bit_length() - 1):
        bit = 1 << k
        if k < len(tokens):
            value = gated(value, tokens[k])
        came = lax.ppermute(value, name, flip_perm(size, bit))
        upper = (index // bit) % 2 == 1
        value = jnp.where(
            upper, jnp.concatenate([came, value], 0), jnp.concatenate([value, came], 0)
        )
        if steps is not None:
            steps.append(value)
    return value


def small_sum(value, name, size):
    bit = 1
    while bit < size:
        value = value + lax.ppermute(value, name, flip_perm(size, bit))
        bit *= 2
    return value


def tensor_scatter(part, size):
    if size == 2:
        index = lax.axis_index("tensor")
        width = part.shape[1] // 2
        away = lax.dynamic_slice_in_dim(part, (1 - index) * width, width, 1)
        kept = lax.dynamic_slice_in_dim(part, index * width, width, 1)
        came = lax.ppermute(away, "tensor", flip_perm(size, 1))
        return kept.astype(jnp.float32) + came.astype(jnp.float32)
    return lax.psum_scatter(part, "tensor", scatter_dimension=1, tiled=True).astype(jnp.float32)


def weave_kernel(tile, plan, *refs):
    out_ref = refs[-1]
    out_ref[...] = jnp.zeros_like(out_ref)
    for target, source, low, wide, turned in plan:
        if turned:
            out_ref[:, target : target + wide] = refs[source][low : low + wide, :].T
        else:
            out_ref[:, target : target + wide] = refs[source][:, low : low + wide]


def weave(arrays, tile, last=None):
    rows, cols = arrays[0].shape
    count = -(-cols // tile)
    plan = []
    target = 0
    for i in range(count):
        for source in range(len(arrays)):
            plan.append((target, source, i * tile, min(tile, cols - i * tile), False))
            target += tile
    operands = list(arrays)
    if last is not None:
        plan.append((target, len(arrays), 0, last.shape[0], True))
        target += last.shape[0] + -last.shape[0] % tile
        operands.append(last)
    return pl.pallas_call(
        functools.partial(weave_kernel, tile, plan),
        out_shape=jax.ShapeDtypeStruct((rows, target), arrays[0].dtype),
        compiler_params=pltpu.CompilerParams(vmem_limit_bytes=30 * 2**20),
        cost_estimate=LIGHT,
        name="weave",
    )(*operands)


def gather_sum_kernel(tile, sizes, count, *refs):
    outs = refs[-count:]
    cols = outs[0].shape[1]
    low = 0
    base = 0
    for size in sizes:
        total = refs[low][...].astype(jnp.float32)
        for ref in refs[low + 1 : low + size]:
            total = total + ref[...].astype(jnp.float32)
        low += size
        tiles = total.shape[1] // (tile * count)
        for i in range(tiles):
            start = base + i * tile
            wide = min(tile, cols - start)
            for n, out_ref in enumerate(outs):
                at = (i * count + n) * tile
                out_ref[:, start : start + wide] = total[:, at : at + wide]
        base += tiles * tile


def gather_sum(groups, tile, count, cols):
    rows = groups[0][-1].shape[0]
    terms = [term for group in groups for term in group]
    wide = sum(term.shape[1] for term in terms) * 2 + count * cols * 4
    block = rows
    while block * wide > 12 * 2**20 and block % 32 == 0:
        block //= 2
    return pl.pallas_call(
        functools.partial(gather_sum_kernel, tile, [len(group) for group in groups], count),
        grid=(rows // block,),
        in_specs=[pl.BlockSpec((block, term.shape[1]), lambda r: (r, 0)) for term in terms],
        out_specs=[pl.BlockSpec((block, cols), lambda r: (r, 0))] * count,
        out_shape=[jax.ShapeDtypeStruct((rows, cols), jnp.float32)] * count,
        compiler_params=pltpu.CompilerParams(vmem_limit_bytes=58 * 2**20),
        cost_estimate=LIGHT,
        name="gather_sum",
    )(*terms)


def fold_plan(rows, blocks, tall):
    plan = []
    for block in range(blocks):
        low = block * rows
        while low < (block + 1) * rows:
            high = min((block + 1) * rows, (low // tall + 1) * tall)
            plan.append((block, low - block * rows, low % tall, low // tall, high - low))
            low = high
    return plan


def pack_kernel(rows, tall, wide, plans, *refs):
    out_ref = refs[-1]
    out_ref[...] = jnp.zeros_like(out_ref)
    text_plan, rest_plan = plans
    for target, source, low, width, _ in text_plan:
        out_ref[:, target : target + width] = refs[source][:, low : low + width]
    for block, at, row, col, count in fold_plan(rows, len(rest_plan), tall):
        source, low, width, turned = rest_plan[block]
        if turned:
            piece = refs[source][low : low + width, :].T
        else:
            piece = refs[source][:, low : low + width]
        start = wide + col * LANES
        out_ref[row : row + count, start : start + width] = piece[at : at + count]


def pack_weights(text, attention, last):
    tall, cols = text[0].shape
    rows = attention[0].shape[0]
    tiles = -(-cols // LANES)
    text_plan = []
    rest_plan = []
    for i in range(tiles):
        width = min(LANES, cols - i * LANES)
        for n in range(len(text)):
            target = (i * len(text) + n) * LANES
            text_plan.append((target, n, i * LANES, width, False))
        for n in range(len(attention)):
            rest_plan.append((len(text) + n, i * LANES, width, False))
    for i in range(tiles):
        width = min(LANES, cols - i * LANES)
        rest_plan.append((len(text) + len(attention), i * LANES, width, True))
    wide = tiles * len(text) * LANES
    folded = len(rest_plan) * rows // tall * LANES
    return pl.pallas_call(
        functools.partial(pack_kernel, rows, tall, wide, (text_plan, rest_plan)),
        out_shape=jax.ShapeDtypeStruct((tall, wide + folded), text[0].dtype),
        compiler_params=pltpu.CompilerParams(vmem_limit_bytes=30 * 2**20),
        cost_estimate=LIGHT,
        name="pack_weights",
    )(*text, *attention, last)


def unfold_kernel(rows, tall, blocks, size, edge, left_ref, *refs):
    full_ref, raw_ref = refs[-2:]
    plan = fold_plan(rows, blocks, tall)

    def place(d, _):
        start = pl.multiple_of(d * rows, 16)
        for block, at, row, col, count in plan:
            full_ref[pl.ds(start + at, count), block * LANES : (block + 1) * LANES] = refs[col][
                d, row : row + count, :
            ]
        return 0

    lax.fori_loop(0, size, place, 0)
    last = pl.program_id(0) == pl.num_programs(0) - 1

    @pl.when(jnp.logical_not(last))
    def _():
        raw_ref[...] = jnp.dot(left_ref[...], full_ref[...], preferred_element_type=jnp.float32)

    @pl.when(last)
    def _():
        raw_ref[:, :edge] = jnp.dot(
            left_ref[...], full_ref[:, :edge], preferred_element_type=jnp.float32
        )


def unfold_product(left, packed, rows, tall, blocks, used, size):
    period = math.lcm(rows, tall)
    span, folds = period // rows, period // tall
    steps = blocks // span
    skip = packed.shape[1] // LANES - folds * steps
    tokens = left.shape[0]
    view = packed.reshape(size, tall, packed.shape[1])
    return pl.pallas_call(
        functools.partial(
            unfold_kernel, rows, tall, span, size, (used - (steps - 1) * span) * LANES
        ),
        grid=(steps,),
        in_specs=[pl.BlockSpec(left.shape, lambda j: (0, 0))]
        + [
            pl.BlockSpec((size, tall, LANES), lambda j, k=k: (0, 0, skip + folds * j + k))
            for k in range(folds)
        ],
        out_specs=[
            pl.BlockSpec((size * rows, span * LANES), lambda j: (0, j)),
            pl.BlockSpec((tokens, span * LANES), lambda j: (0, j)),
        ],
        out_shape=[
            jax.ShapeDtypeStruct((size * rows, blocks * LANES), packed.dtype),
            jax.ShapeDtypeStruct((tokens, blocks * LANES), jnp.float32),
        ],
        compiler_params=pltpu.CompilerParams(vmem_limit_bytes=58 * 2**20),
        cost_estimate=LIGHT,
        name="unfold_product",
    )(left, *[view] * folds)


def rotary_tables(row_pos, col_pos, quarter, repeat):
    frequency = jnp.exp(-math.log(10000.0) * jnp.arange(quarter, dtype=jnp.float32) / quarter)
    angles = jnp.concatenate(
        [
            row_pos.astype(jnp.float32)[:, None] * frequency,
            col_pos.astype(jnp.float32)[:, None] * frequency,
        ],
        axis=1,
    )
    sine = jnp.sin(angles)
    return jnp.tile(jnp.cos(angles), (1, 2 * repeat)), jnp.tile(
        jnp.concatenate([-sine, sine], axis=1), (1, repeat)
    )


def local(
    size,
    groups,
    latents,
    cotangent,
    caption,
    caption_lens,
    patch_row,
    patch_col,
    timestep,
    query_proj,
    key_proj,
    value_proj,
    output_proj,
    textkey_proj,
    textval_proj,
    gate_proj,
    up_proj,
    down_proj,
    modulation,
    attn_gain,
    ffn_gain,
    query_gain,
    key_gain,
    textkey_gain,
    cross_gate,
):
    f32, bf16 = jnp.float32, jnp.bfloat16
    rows_w, chan = query_proj.shape
    units = gate_proj.shape[1]
    head_part = query_gain.shape[0]
    head_dim = head_part * size
    heads_here = chan // head_dim
    model_dim = latents.shape[1]
    padded = chan + -chan % LANES
    pairs = padded // LANES
    dp_index = lax.axis_index("dp")
    tensor_index = lax.axis_index("tensor")

    small = jnp.concatenate(
        [
            attn_gain.astype(f32),
            ffn_gain.astype(f32),
            query_gain.astype(f32),
            key_gain.astype(f32),
            textkey_gain.astype(f32),
            timestep.astype(f32),
        ]
    )[None]
    steps = []
    small_all = small_gather(small, "dp", size, (), steps)
    packed = pack_weights(
        gated([textkey_proj, textval_proj], steps[0]), [query_proj, key_proj, value_proj], output_proj
    )
    packed_set = lax.all_gather(packed, "dp", axis=0, tiled=True)

    cuts = [rows_w, 2 * rows_w, 2 * rows_w + head_part]
    gain_one = small_all[:, : cuts[0]].reshape(-1)
    gain_two = small_all[:, cuts[0] : cuts[1]].reshape(-1)
    gain_query = small_all[:, cuts[1] : cuts[2]].reshape(-1)
    gain_key = small_all[:, cuts[2] : cuts[2] + head_part].reshape(-1)
    gain_text = small_all[:, cuts[2] + head_part : cuts[2] + 2 * head_part].reshape(-1)
    steps_all = small_all[:, cuts[2] + 2 * head_part :].reshape(-1)
    embed_rows = modulation.shape[0]
    embed_dim = embed_rows * size
    embed_all = time_embed(steps_all, embed_dim)
    cond_all = (embed_all * jax.nn.sigmoid(embed_all)).astype(bf16)
    cond_here = lax.dynamic_slice_in_dim(cond_all, dp_index * embed_rows, embed_rows, 1)
    mod_part = jnp.dot(cond_here, modulation, preferred_element_type=f32)
    mod_sums = SmallScatter(mod_part, size)
    while mod_sums.left():
        mod_sums.hop()
    mod_here = mod_sums.value
    mod_all = small_gather(mod_here, "tensor", groups).reshape(1, -1)
    tile = 256
    blocks = units // tile
    gate_l, up_l, down_l = gated((gate_proj, up_proj, down_proj), small_all)
    third = weave([gate_l, up_l], tile, down_l)
    ffn_set = lax.all_gather(gated(third, small_all), "dp", axis=0, tiled=True)
    scale_one = mod_all[:, 0:model_dim]
    gate_one = jnp.tanh(mod_all[:, model_dim : 2 * model_dim])
    scale_two = mod_all[:, 2 * model_dim : 3 * model_dim]
    gate_two = jnp.tanh(mod_all[:, 3 * model_dim : 4 * model_dim])
    tanh_cross = jnp.tanh(cross_gate.astype(f32))
    tanh_lanes = jnp.pad(jnp.repeat(tanh_cross, head_dim), (0, padded - chan))
    tanh_lanes = jnp.broadcast_to(tanh_lanes[None], (8, padded))
    per_tile = LANES // head_dim
    gain_lanes = jnp.pad(
        jnp.tile(jnp.stack([gain_query, gain_key, gain_text]), (1, per_tile)), ((0, 5), (0, 0))
    )
    cosine, sine = rotary_tables(patch_row[0], patch_col[0], head_dim // 4, per_tile)
    tables = (cosine, sine, gain_lanes, tanh_lanes)

    resid_in = latents.astype(f32)
    factor_one = inv_rms(resid_in)
    normed_one = resid_in * factor_one
    attn_in = (normed_one * gain_one * (1.0 + scale_one)).astype(bf16)
    grad_out = cotangent.astype(f32)
    grad_ffn = (gate_two * grad_out).astype(bf16)
    full_text = gated(packed_set, attn_in, grad_ffn)
    full_qkvo, qkv_raw = unfold_product(
        attn_in, full_text, rows_w, packed.shape[0], 4 * pairs, 3 * pairs, size
    )
    cap_in = caption[0]
    text_raw = product(gated(cap_in, qkv_raw), full_text, 2 * padded, 256, f32)
    mixed_a, query_bf, own_out, cross_out, lse, kv_bf, tkv_bf = attend_rows(
        0, caption_lens, qkv_raw, text_raw, tables, head_dim
    )
    part_a = product(mixed_a, full_qkvo, model_dim, 512, bf16, True, 3)
    own_a, came_a = swap_start(part_a, groups, 1)
    kept = gated((query_bf, own_out, cross_out, lse, kv_bf, tkv_bf), part_a)
    mixed_b, query_bf, own_out, cross_out, lse = attend_rows(
        1, caption_lens, qkv_raw, text_raw, tables, head_dim, kept
    )
    attn_part = product(mixed_b, full_qkvo, model_dim, 512, bf16, True, 3)
    mixed_heads = jnp.concatenate([mixed_a, mixed_b], axis=0)
    mod_set = lax.all_gather(gated(modulation, qkv_raw), "dp", axis=0, tiled=True)

    came_a = gated(came_a, attn_part)
    own_b, came_b = swap_start(gated(attn_part, came_a), groups, 1)
    half_rows = grad_ffn.shape[0] // 2
    full_ffn = gated(ffn_set, attn_part)
    gain_mul = gain_two * (1.0 + scale_two)

    def feed_input(resid, own, came):
        attn_sum = swap_end(own, came, groups)
        total = resid + gate_one * attn_sum
        factor = inv_rms(total)
        normed = total * factor
        return attn_sum, total, factor, normed, (normed * gain_mul).astype(bf16)

    resid_a, resid_b = resid_in[:half_rows], resid_in[half_rows:]
    attn_out_a, residual_a, factor_a, normed_a, feed_a = feed_input(resid_a, own_a, came_a)
    kept = feed_forward(0, feed_a, grad_ffn, full_ffn, units, tile)
    dffn_one = product(kept[1], full_ffn, model_dim, 512, bf16, True, 0, None, (0, 2))
    one_own, one_came = swap_start(dffn_one, groups, 1)
    came_b = gated(came_b, dffn_one)
    attn_out_b, residual_b, factor_b, normed_b, feed_b = feed_input(resid_b, own_b, came_b)
    hidden, dboth = feed_forward(
        1, feed_b, grad_ffn, full_ffn, units, tile, gated(kept, dffn_one)
    )
    dffn_two = product(dboth, full_ffn, model_dim, 512, bf16, True, 0, None, (1, 2))
    ffn_in = jnp.concatenate([feed_a, feed_b], axis=0)
    me = dp_index.astype(jnp.int32)[None]
    depth_bits = list(range(2, size.bit_length() - 1))
    side_first = [0, 1] + depth_bits
    line_first = [0, 2, 1] + depth_bits[1:]

    def staged(left, right, bits, tile_cols):
        return Halving(size, bits, *outer_grads(me, left, right, size, bits, tile_cols))

    down = staged(grad_ffn, gated(hidden, dffn_two), line_first, 512)
    down.start()
    one_came = gated(one_came, down.out)
    two_own, two_came = swap_start(gated(dffn_two, one_came), groups, 1)
    grown = staged(ffn_in, gated(dboth, down.out, one_came), side_first, 512)
    grown.start()
    ffn_part = product(gated(hidden, grown.out, mod_set), full_ffn, model_dim, 512, bf16, True, 2)
    grad_out_a, grad_out_b = grad_out[:half_rows], grad_out[half_rows:]

    def feed_back(grad, own, came, normed, factor, attn_sum):
        dffn = swap_end(own, came, groups)
        dres = grad + norm_back(dffn * gain_mul, normed, factor)
        sums_here = jnp.sum(dffn * normed, axis=0), jnp.sum(dres * attn_sum, axis=0)
        return dres, (gate_one * dres).astype(bf16), sums_here

    dres_a, grad_attn_a, sums_a = feed_back(
        grad_out_a, one_own, one_came, normed_a, factor_a, attn_out_a
    )
    dmix_a = product(
        gated(grad_attn_a, ffn_part), full_qkvo, padded, LANES, bf16, False, 3 * padded // LANES
    )
    two_came = gated(two_came, dmix_a)
    down.finish(two_came)
    down.start()
    grown.finish(down.out)
    grown.start()
    dres_b, grad_attn_b, sums_b = feed_back(
        grad_out_b, two_own, gated(two_came, grown.out), normed_b, factor_b, attn_out_b
    )
    dmix_b = product(grad_attn_b, full_qkvo, padded, LANES, bf16, False, 3 * padded // LANES)
    dmixed = jnp.concatenate([dmix_a, dmix_b], axis=0)
    grad_attn = jnp.concatenate([grad_attn_a, grad_attn_b], axis=0)
    weighed = sums_a[0] + sums_b[0]
    grad_gaintwo = weighed * (1.0 + scale_two[0])
    dscale_two = weighed * gain_two
    dgate_one = (sums_a[1] + sums_b[1]) * (1.0 - gate_one[0] ** 2)
    dresid = jnp.concatenate([dres_a, dres_b], axis=0)
    residual = jnp.concatenate([residual_a, residual_b], axis=0)
    ffn_own, ffn_came = swap_start(gated(ffn_part, dmixed), groups, 1)
    dq_cross, dtext, stats_c = cross_back(
        caption_lens, query_bf, tkv_bf, text_raw, cross_out, lse, dmixed, tables, head_dim
    )
    down.finish(dq_cross)
    down.start()
    grown.finish(down.out)
    grown.start()
    text = staged(cap_in, gated(dtext, grown.out), side_first, 256)
    text.start()
    split = pairs - pairs // 2
    windows = [(0, split), (split, pairs - split)]
    common = (query_bf, kv_bf, qkv_raw, own_out, lse)
    dmixed_a = gated(dmixed, text.out)
    dqkv_a, stats_a = self_back(windows[0], *common, dmixed_a, dq_cross, tables, head_dim)
    down.finish(dqkv_a)
    down.start()
    grown.finish(down.out)
    grown.start()
    text.finish(grown.out)
    text.start()
    first_qkv = staged(attn_in, gated(dqkv_a, text.out), side_first, 3 * LANES)
    first_qkv.start()
    outp = staged(gated(grad_attn, first_qkv.out), mixed_heads, side_first, padded)
    outp.start()
    edge = 3 * LANES * split
    even = pairs == 2 * split
    wide_a = full_qkvo if even else full_qkvo[:, :edge]
    wide_b = full_qkvo if even else full_qkvo[:, edge : 3 * padded]
    dattn_a = product(gated(dqkv_a, outp.out), wide_a, model_dim, 512, f32, True)
    dmixed_b = gated(dmixed, dattn_a)
    dqkv_b, stats_b = self_back(windows[1], *common, dmixed_b, dq_cross, tables, head_dim)
    landed = (down.land(dqkv_b), grown.land(dqkv_b), gated(ffn_came, dqkv_b))
    ffn_came = landed[2]
    dqkv_l = gated(dqkv_b, *landed)
    dattn_part = product(dqkv_l, wide_b, model_dim, 512, bf16, True, int(even), dattn_a)
    cut = dattn_part.shape[0] * 5 // 8
    high_own, high_came = swap_start(dattn_part[:cut], groups, 1)
    last_qkv = staged(attn_in, gated(dqkv_b, dattn_part), side_first, 3 * LANES)
    last_qkv.start()
    text.finish(last_qkv.out)
    text.start()
    first_qkv.finish(text.out)
    first_qkv.start()
    outp.finish(first_qkv.out)
    outp.start()
    last_qkv.finish(outp.out)
    last_qkv.start()
    caption_part = product(
        gated(dtext, last_qkv.out), full_text, cap_in.shape[1], 1024, bf16, True
    )
    grad_gate, grad_up = gather_sum([grown.drain(caption_part)], tile, 2, units)
    high_came = gated(high_came, grad_gate)
    base_own, base_came = swap_start(gated(dattn_part[cut:], high_came), groups, 1)
    last_qkv.finish(high_came)
    last_qkv.start()
    outp.finish(last_qkv.out)
    outp.start()
    down_t = sum(term[:rows_w].astype(f32) for term in down.drain(outp.out))
    ffn_out = swap_end(ffn_own, gated(ffn_came, down_t), groups)
    output = (residual + gate_two * ffn_out).astype(bf16)
    weighed_part = jnp.sum(gated(dattn_part, output).astype(f32) * normed_one, axis=0)
    gate_part = jnp.sum(grad_out * gated(ffn_part, weighed_part).astype(f32), axis=0)
    text.finish(gate_part)
    text.start()
    first_qkv.finish(text.out)
    first_qkv.start()
    last_qkv.finish(first_qkv.out)
    last_qkv.start()
    base_came = gated(base_came, last_qkv.out)
    stats = jnp.concatenate([stats_a, stats_b], axis=1)[:2]
    stat_sums = jnp.concatenate([stats, stats_c[:2]], axis=0)[:, :chan]
    stat_sums = jnp.sum(stat_sums.reshape(4, heads_here, head_dim), axis=(1,))
    xgate_rows = stats_c[1, :chan].reshape(heads_here, head_dim)
    xgate_here = jnp.sum(xgate_rows, axis=1) * (1.0 - tanh_cross**2)
    sums_part = jnp.concatenate([weighed_part, gate_part, stat_sums[:3].reshape(-1)])[None]
    sums = small_sum(gated(sums_part, base_came), "tensor", groups)[0]
    dattn_in = jnp.concatenate(
        [swap_end(high_own, high_came, groups), swap_end(base_own, base_came, groups)], axis=0
    )
    grad_latents = (
        dresid + norm_back(dattn_in * gain_one * (1.0 + scale_one), normed_one, factor_one)
    ).astype(bf16)
    outp.finish(grad_latents)
    outp.start()
    first_qkv.finish(outp.out)
    first_qkv.start()
    sums = gated(sums, first_qkv.out)
    weighed_one, head_gains = sums[:model_dim], sums[2 * model_dim :]
    dgate_two = sums[model_dim : 2 * model_dim] * (1.0 - gate_two[0] ** 2)
    grad_gainone = weighed_one * (1.0 + scale_one[0])
    dscale_one = weighed_one * gain_one
    dmod_all = jnp.concatenate([dscale_one, dgate_one, dscale_two, dgate_two])
    cols_here = modulation.shape[1]
    dmod_here = lax.dynamic_slice_in_dim(dmod_all, tensor_index * cols_here, cols_here, 0)
    row = jnp.concatenate([dmod_here, grad_gainone, grad_gaintwo, head_gains, xgate_here])
    row = row.astype(bf16).astype(f32)[None]
    dcaption = tensor_scatter(gated(caption_part, sums), groups)
    embed_row = jnp.einsum(
        "bc,tc->bt", row[:, :cols_here].astype(bf16), mod_set, preferred_element_type=f32
    )
    rows_set = small_gather(row, "dp", size)
    grad_textkey, grad_textval = gather_sum([text.drain(row)], LANES, 2, chan)
    dmod_set = rows_set[:, :cols_here].astype(bf16)
    gain_sums = jnp.sum(rows_set[:, cols_here:], axis=0)
    grad_modul = jnp.einsum("bt,bc->tc", cond_here, dmod_set, preferred_element_type=f32)
    embed_sum = small_sum(embed_row, "tensor", groups)
    embed_own = lax.dynamic_slice_in_dim(embed_all, dp_index, 1, 0)
    sig_own = jax.nn.sigmoid(embed_own)
    dembed_all = embed_sum * (sig_own * (1.0 + embed_own * (1.0 - sig_own)))
    width = embed_dim // groups
    dembed = lax.dynamic_slice_in_dim(dembed_all, tensor_index * width, width, 1)
    output_t = sum(term[:rows_w].astype(f32) for term in outp.drain(grad_textkey))
    parts = [last_qkv.drain(output_t), first_qkv.drain(output_t)][::-1]
    grad_query, grad_key, grad_value = gather_sum(parts, LANES, 3, chan)

    def own_part(start, width):
        return lax.dynamic_slice_in_dim(gain_sums, start + dp_index * width, width, 0)

    heads_at = 2 * model_dim
    gate_at = heads_at + 3 * head_dim
    return (
        output,
        grad_latents,
        dcaption.astype(bf16)[None],
        dembed,
        grad_query,
        grad_key,
        grad_value,
        output_t[:, :chan].T,
        grad_textkey,
        grad_textval,
        grad_gate,
        grad_up,
        down_t.T,
        grad_modul,
        own_part(0, rows_w),
        own_part(model_dim, rows_w),
        own_part(heads_at, head_part),
        own_part(heads_at + head_dim, head_part),
        own_part(heads_at + 2 * head_dim, head_part),
        gain_sums[gate_at:],
    )


def solution(mesh):
    in_specs = (
        P("dp", None),
        P("dp", None),
        P("dp", None, None),
        P("dp"),
        P("dp", None),
        P("dp", None),
        P("dp"),
        P("dp", "tensor"),
        P("dp", "tensor"),
        P("dp", "tensor"),
        P("tensor", "dp"),
        P("dp", "tensor"),
        P("dp", "tensor"),
        P("dp", "tensor"),
        P("dp", "tensor"),
        P("tensor", "dp"),
        P("dp", "tensor"),
        P("dp"),
        P("dp"),
        P("dp"),
        P("dp"),
        P("dp"),
        P("tensor"),
    )
    out_specs = (
        P("dp", None),
        P("dp", None),
        P("dp", None, "tensor"),
        P("dp", "tensor"),
        P("dp", "tensor"),
        P("dp", "tensor"),
        P("dp", "tensor"),
        P("tensor", "dp"),
        P("dp", "tensor"),
        P("dp", "tensor"),
        P("dp", "tensor"),
        P("dp", "tensor"),
        P("tensor", "dp"),
        P("dp", "tensor"),
        P("dp"),
        P("dp"),
        P("dp"),
        P("dp"),
        P("dp"),
        P("tensor"),
    )
    bound = functools.partial(local, mesh.shape["dp"], mesh.shape["tensor"])
    return jax.shard_map(bound, mesh=mesh, in_specs=in_specs, out_specs=out_specs, check_vma=False)
```

```python
import functools
import math

import jax
import jax.numpy as jnp
from jax import lax
from jax.experimental import pallas as pl
from jax.experimental.pallas import tpu as pltpu
from jax.sharding import PartitionSpec as P

EPSILON = 1e-06


def inv_rms(values):
    return lax.rsqrt(jnp.mean(values * values, axis=-1, keepdims=True) + EPSILON)


def time_embed(step_vals, embed_width):
    half_width = embed_width // 2
    frequency = jnp.exp(-math.log(10000.0) * jnp.arange(half_width, dtype=jnp.float32) / half_width)
    phases = step_vals.astype(jnp.float32)[:, None] * frequency
    return jnp.concatenate([jnp.cos(phases), jnp.sin(phases)], axis=1)


def norm_back(grad_hat, normed, factor):
    return factor * (grad_hat - normed * jnp.mean(grad_hat * normed, axis=-1, keepdims=True))


LANES = 128
LIGHT = pl.CostEstimate(flops=1, transcendentals=0, bytes_accessed=1)


def lane_ids(rows):
    return lax.broadcasted_iota(jnp.int32, (rows, LANES), 1)


def pair_matrix(same, half):
    row = lax.broadcasted_iota(jnp.int32, (LANES, LANES), 0) // half
    col = lax.broadcasted_iota(jnp.int32, (LANES, LANES), 1) // half
    return jnp.where((row == col) == same, 1.0, 0.0).astype(jnp.bfloat16)


def head_sums(values, matrix):
    high = values.astype(jnp.bfloat16)
    low = (values - high.astype(jnp.float32)).astype(jnp.bfloat16)
    return jnp.dot(high, matrix, preferred_element_type=jnp.float32) + jnp.dot(
        low, matrix, preferred_element_type=jnp.float32
    )


def swap_quarters(values, half):
    rows = values.shape[0]
    first = lane_ids(rows) % half < half // 2
    return jnp.where(
        first,
        pltpu.roll(values, LANES - half // 2, 1),
        pltpu.roll(values, half // 2, 1),
    )


def nt_dot(left, right):
    return lax.dot_general(
        left, right, (((1,), (1,)), ((), ())), preferred_element_type=jnp.float32
    )


def tn_dot(left, right):
    return lax.dot_general(
        left, right, (((0,), (0,)), ((), ())), preferred_element_type=jnp.float32
    )


def attend_kernel(half, block, fresh, *refs):
    f32, bf16 = jnp.float32, jnp.bfloat16
    matrix = pair_matrix(True, half)
    if fresh:
        len_ref, rawq_ref, rawk_ref, rawv_ref, text_ref, tval_ref = refs[:6]
        cos_ref, sin_ref, cosk_ref, sink_ref, gain_ref, tanh_ref = refs[6:12]
        mixed_ref, query_ref, own_ref, cross_ref, lse_ref, kv_ref, tkv_ref = refs[12:]
    else:
        len_ref, rawq_ref, kv_ref, tkv_ref, cos_ref, sin_ref, gain_ref, tanh_ref = refs[:8]
        mixed_ref, query_ref, own_ref, cross_ref, lse_ref = refs[12:]

    def hat(raw):
        return raw * lax.rsqrt(head_sums(raw * raw, matrix) * (1.0 / half) + EPSILON)

    def turned(raw, gain, cosine, sine):
        value = hat(raw) * gain
        return (value * cosine + swap_quarters(value, half) * sine).astype(bf16)

    query_ref[...] = turned(rawq_ref[...], gain_ref[0:1], cos_ref[...], sin_ref[...])
    if fresh:
        kv_ref[:, :LANES] = turned(rawk_ref[...], gain_ref[1:2], cosk_ref[...], sink_ref[...])
        kv_ref[:, LANES:] = rawv_ref[...].astype(bf16)
        tkv_ref[:, :LANES] = (hat(text_ref[...]) * gain_ref[2:3]).astype(bf16)
        tkv_ref[:, LANES:] = tval_ref[...].astype(bf16)
    key, value = kv_ref[:, :LANES], kv_ref[:, LANES:]
    tkey, tval = tkv_ref[:, :LANES], tkv_ref[:, LANES:]
    one = jnp.ones((), bf16)
    zero = jnp.zeros((), bf16)

    def pick(a, b):
        return jnp.where(lane_ids(a.shape[0]) < half, a, b)

    def fill(a, fillers, first):
        other = jnp.full(a.shape, fillers, bf16)
        return pick(a, other) if first else pick(other, a)

    value_ones = [fill(value, one, True), fill(value, one, False)]
    tval_ones = [fill(tval, one, True), fill(tval, one, False)]
    keep = lax.broadcasted_iota(jnp.int32, (block, tkey.shape[0]), 1) < len_ref[0]

    def step(i, _):
        here = pl.ds(pl.multiple_of(i * block, block), block)
        q_blk = query_ref[here, :] * jnp.asarray(half**-0.5, bf16)
        outs = []
        texts = []
        for head in range(2):
            q_one = fill(q_blk, zero, head == 0)
            e_self = jnp.exp(nt_dot(q_one, key)).astype(bf16)
            outs.append(jnp.dot(e_self, value_ones[head], preferred_element_type=f32))
            e_text = jnp.where(keep, jnp.exp(nt_dot(q_one, tkey)), 0.0).astype(bf16)
            texts.append(jnp.dot(e_text, tval_ones[head], preferred_element_type=f32))
        for n, (a, b) in enumerate((outs, texts)):
            total = pick(b, a)
            lse_ref[here, n * LANES : (n + 1) * LANES] = jnp.log(total)
            res = pick(a, b) / pltpu.roll(total, half, 1)
            if n == 0:
                own = res
                own_ref[here, :] = res
            else:
                cross_ref[here, :] = res
                mixed_ref[here, :] = (own + tanh_ref[0:1] * res).astype(bf16)
        return 0

    lax.fori_loop(0, query_ref.shape[0] // block, step, 0)


def attend_rows(part, cap_len, raw, text, tables, half, kept=None):
    cosine, sine, gains, tanh_lanes = tables
    rows, caps = raw.shape[0], text.shape[0]
    count = rows // 2
    width = tanh_lanes.shape[1]
    f32, bf16 = jnp.float32, jnp.bfloat16
    fresh = kept is None

    def piece(scale, shift, wide=1):
        return pl.BlockSpec((count, wide * LANES), lambda p: (part, scale * p + shift))

    table = pl.BlockSpec((count, LANES), lambda p: (part, 0))
    whole = pl.BlockSpec(memory_space=pl.ANY)
    smem = pl.BlockSpec(memory_space=pltpu.SMEM)
    kv_block = pl.BlockSpec((rows, 2 * LANES), lambda p: (0, p))
    tkv_block = pl.BlockSpec((caps, 2 * LANES), lambda p: (0, p))
    tail_specs = [fixed_block(8), lane_block(8, 1, 0)]
    out_specs = [
        pl.BlockSpec((count, LANES), lambda p: (0, p)),
        piece(1, 0),
        piece(1, 0),
        piece(1, 0),
        piece(1, 0, 2),
    ]
    out_shape = [
        jax.ShapeDtypeStruct((count, width), bf16),
        jax.ShapeDtypeStruct((rows, width), bf16),
        jax.ShapeDtypeStruct((rows, width), f32),
        jax.ShapeDtypeStruct((rows, width), f32),
        jax.ShapeDtypeStruct((rows, 2 * width), f32),
    ]
    if fresh:
        in_specs = [smem, piece(3, 0), lane_block(rows, 3, 1), lane_block(rows, 3, 2)]
        in_specs += [lane_block(caps, 2, 0), lane_block(caps, 2, 1)]
        in_specs += [table, table, fixed_block(rows), fixed_block(rows)] + tail_specs
        operands = (cap_len, raw, raw, raw, text, text, cosine, sine, cosine, sine)
        operands += (gains, tanh_lanes)
        out_specs += [kv_block, tkv_block]
        out_shape += [
            jax.ShapeDtypeStruct((rows, 2 * width), bf16),
            jax.ShapeDtypeStruct((caps, 2 * width), bf16),
        ]
        aliases = {}
    else:
        query, own, cross, lse, kv, tkv = kept
        in_specs = [smem, piece(3, 0), kv_block, tkv_block, table, table] + tail_specs
        in_specs += [whole] * 4
        operands = (cap_len, raw, kv, tkv, cosine, sine, gains, tanh_lanes)
        operands += (query, own, cross, lse)
        aliases = {8: 1, 9: 2, 10: 3, 11: 4}
    return pl.pallas_call(
        functools.partial(attend_kernel, half, min(256, count), fresh),
        grid=(width // LANES,),
        in_specs=in_specs,
        out_specs=out_specs,
        out_shape=out_shape,
        input_output_aliases=aliases,
        compiler_params=pltpu.CompilerParams(vmem_limit_bytes=50 * 2**20),
        cost_estimate=LIGHT,
        name="attend_fwd",
    )(*operands)


def pick_head(a, b, first, half):
    low = lane_ids(a.shape[0]) < half
    return jnp.where(low, a, b) if first else jnp.where(low, b, a)


def three_parts(value, half):
    spot = lane_ids(value.shape[0]) % half
    high = value.astype(jnp.bfloat16).astype(jnp.float32)
    rest = value - high
    mid = rest.astype(jnp.bfloat16).astype(jnp.float32)
    low = rest - mid
    parts = jnp.where(spot == 0, high, jnp.where(spot == 1, mid, jnp.where(spot == 2, low, 0.0)))
    return parts.astype(jnp.bfloat16)


def with_ones(value, first, half):
    ones = jnp.where(lane_ids(value.shape[0]) % half < 3, 1.0, 0.0).astype(jnp.bfloat16)
    return pick_head(value, ones, first, half)


def only_head(value, first, half):
    return pick_head(value, jnp.zeros(value.shape, jnp.bfloat16), first, half)


def norm_return(grad_in, raw, gain, half, turn):
    same = pair_matrix(True, half)
    inv = lax.rsqrt(head_sums(raw * raw, same) * (1.0 / half) + EPSILON)
    normed = raw * inv
    back = grad_in.astype(jnp.bfloat16).astype(jnp.float32)
    if turn is not None:
        back = back * turn[0][...] - swap_quarters(back, half) * turn[1][...]
    scaled = back * gain
    mean = head_sums(scaled * normed, same) * (1.0 / half)
    stat = jnp.sum(back * normed, axis=0, keepdims=True)
    return (inv * (scaled - normed * mean)).astype(jnp.bfloat16), stat


def score_grads(key_aug, val_aug, q_aug, o_aug, keep):
    probs = jnp.exp(nt_dot(key_aug, q_aug))
    if keep is not None:
        probs = jnp.where(keep, probs, 0.0)
    return probs.astype(jnp.bfloat16), (probs * nt_dot(val_aug, o_aug)).astype(jnp.bfloat16)


def cross_back_kernel(
    half,
    block,
    len_ref,
    query_ref,
    tkv_ref,
    text_ref,
    cross_ref,
    lse_ref,
    dmix_ref,
    gain_ref,
    tanh_ref,
    dq_ref,
    dtext_ref,
    stat_ref,
    qs_ref,
    os_ref,
    dk_ref,
    dv_ref,
):
    f32, bf16 = jnp.float32, jnp.bfloat16
    rows, caps = query_ref.shape[0], tkv_ref.shape[0]
    grad_f = dmix_ref[...].astype(f32)
    other = (grad_f * tanh_ref[0:1]).astype(bf16)
    delta = three_parts(
        -head_sums(other.astype(f32) * cross_ref[...], pair_matrix(False, half)), half
    )
    lse = three_parts(-lse_ref[...], half)
    query = query_ref[...] * jnp.asarray(half**-0.5, bf16)
    tkey, tval = tkv_ref[:, :LANES], tkv_ref[:, LANES:]
    for head in range(2):
        qs_ref[head] = pick_head(query, lse, head == 0, half)
        os_ref[head] = pick_head(other, delta, head == 0, half)
    key_aug = [with_ones(tkey, h == 0, half) for h in range(2)]
    val_aug = [with_ones(tval, h == 0, half) for h in range(2)]
    key_only = [only_head(tkey, h == 0, half) for h in range(2)]
    dk_ref[...] = jnp.zeros_like(dk_ref)
    dv_ref[...] = jnp.zeros_like(dv_ref)
    keep = lax.broadcasted_iota(jnp.int32, (caps, block), 0) < len_ref[0]

    def step(i, _):
        here = pl.ds(pl.multiple_of(i * block, block), block)
        dq = jnp.zeros((block, LANES), f32)
        for head in range(2):
            q_aug, o_aug = qs_ref[head, here], os_ref[head, here]
            probs, grads = score_grads(key_aug[head], val_aug[head], q_aug, o_aug, keep)
            dv_ref[...] += jnp.dot(
                probs, only_head(o_aug, head == 0, half), preferred_element_type=f32
            )
            dk_ref[...] += jnp.dot(
                grads, only_head(q_aug, head == 0, half), preferred_element_type=f32
            )
            dq += tn_dot(grads, key_only[head])
        dq_ref[here, :] = dq * half**-0.5
        return 0

    lax.fori_loop(0, rows // block, step, 0)
    res, stat_t = norm_return(dk_ref[...], text_ref[...], gain_ref[2:3], half, None)
    dtext_ref[:, :LANES] = res
    dtext_ref[:, LANES:] = dv_ref[...].astype(bf16)
    stat_x = jnp.sum(grad_f * cross_ref[...], axis=0, keepdims=True)
    stat_ref[...] = jnp.concatenate([stat_t, stat_x, jnp.zeros((6, LANES), f32)], axis=0)


def self_back_kernel(
    half,
    block,
    query_ref,
    key_ref,
    val_ref,
    rawq_ref,
    rawk_ref,
    own_ref,
    lse_ref,
    dmix_ref,
    dqc_ref,
    cos_ref,
    sin_ref,
    gain_ref,
    dqkv_ref,
    stat_ref,
    qs_ref,
    os_ref,
    dq_ref,
    dk_ref,
    dv_ref,
):
    f32, bf16 = jnp.float32, jnp.bfloat16
    rows = query_ref.shape[0]
    grad = dmix_ref[...]
    delta = three_parts(
        -head_sums(grad.astype(f32) * own_ref[...], pair_matrix(False, half)), half
    )
    lse = three_parts(-lse_ref[...], half)
    query = query_ref[...] * jnp.asarray(half**-0.5, bf16)
    key, value = key_ref[...], val_ref[...]
    for head in range(2):
        qs_ref[head] = pick_head(query, lse, head == 0, half)
        os_ref[head] = pick_head(grad, delta, head == 0, half)
    key_aug = [with_ones(key, h == 0, half) for h in range(2)]
    val_aug = [with_ones(value, h == 0, half) for h in range(2)]
    key_only = [only_head(key, h == 0, half) for h in range(2)]
    dk_ref[...] = jnp.zeros_like(dk_ref)
    dv_ref[...] = jnp.zeros_like(dv_ref)

    def step(i, _):
        here = pl.ds(pl.multiple_of(i * block, block), block)
        dq = jnp.zeros((block, LANES), f32)
        for head in range(2):
            q_aug, o_aug = qs_ref[head, here], os_ref[head, here]
            probs, grads = score_grads(key_aug[head], val_aug[head], q_aug, o_aug, None)
            dv_ref[...] += jnp.dot(
                probs, only_head(o_aug, head == 0, half), preferred_element_type=f32
            )
            dk_ref[...] += jnp.dot(
                grads, only_head(q_aug, head == 0, half), preferred_element_type=f32
            )
            dq += tn_dot(grads, key_only[head])
        dq_ref[here, :] = dqc_ref[here, :] + dq * half**-0.5
        return 0

    lax.fori_loop(0, rows // block, step, 0)
    turn = (cos_ref, sin_ref)
    res, stat_q = norm_return(dq_ref[...], rawq_ref[...], gain_ref[0:1], half, turn)
    dqkv_ref[:, :LANES] = res
    res, stat_k = norm_return(dk_ref[...], rawk_ref[...], gain_ref[1:2], half, turn)
    dqkv_ref[:, LANES : 2 * LANES] = res
    dqkv_ref[:, 2 * LANES :] = dv_ref[...].astype(bf16)
    stat_ref[...] = jnp.concatenate([stat_q, stat_k, jnp.zeros((6, LANES), f32)], axis=0)


def lane_block(rows, scale, shift):
    return pl.BlockSpec((rows, LANES), lambda p: (0, scale * p + shift))


def fixed_block(rows):
    return pl.BlockSpec((rows, LANES), lambda p: (0, 0))


def cross_back(cap_len, query, tkv, text, cross, lse, dmix, tables, half):
    gains, tanh_lanes = tables[2], tables[3]
    rows, caps = query.shape[0], text.shape[0]
    width = dmix.shape[1]
    f32, bf16 = jnp.float32, jnp.bfloat16
    return pl.pallas_call(
        functools.partial(cross_back_kernel, half, min(512, rows)),
        grid=(width // LANES,),
        in_specs=[
            pl.BlockSpec(memory_space=pltpu.SMEM),
            lane_block(rows, 1, 0),
            pl.BlockSpec((caps, 2 * LANES), lambda p: (0, p)),
            lane_block(caps, 2, 0),
            lane_block(rows, 1, 0),
            lane_block(rows, 2, 1),
            lane_block(rows, 1, 0),
            fixed_block(8),
            lane_block(8, 1, 0),
        ],
        out_specs=[
            lane_block(rows, 1, 0),
            pl.BlockSpec((caps, 2 * LANES), lambda p: (0, p)),
            lane_block(8, 1, 0),
        ],
        out_shape=[
            jax.ShapeDtypeStruct((rows, width), f32),
            jax.ShapeDtypeStruct((caps, 2 * width), bf16),
            jax.ShapeDtypeStruct((8, width), f32),
        ],
        scratch_shapes=[pltpu.VMEM((2, rows, LANES), bf16)] * 2
        + [pltpu.VMEM((caps, LANES), f32)] * 2,
        compiler_params=pltpu.CompilerParams(vmem_limit_bytes=40 * 2**20),
        cost_estimate=LIGHT,
        name="cross_bwd",
    )(cap_len, query, tkv, text, cross, lse, dmix, gains, tanh_lanes)


def self_back(window, query, kv, raw, own, lse, dmix, dq_cross, tables, half):
    cosine, sine, gains, _ = tables
    first, pairs = window
    rows = raw.shape[0]
    width = pairs * LANES
    f32, bf16 = jnp.float32, jnp.bfloat16
    return pl.pallas_call(
        functools.partial(self_back_kernel, half, min(512, rows)),
        grid=(pairs,),
        in_specs=[
            lane_block(rows, 1, first),
            lane_block(rows, 2, 2 * first),
            lane_block(rows, 2, 2 * first + 1),
            lane_block(rows, 3, 3 * first),
            lane_block(rows, 3, 3 * first + 1),
            lane_block(rows, 1, first),
            lane_block(rows, 2, 2 * first),
            lane_block(rows, 1, first),
            lane_block(rows, 1, first),
            fixed_block(rows),
            fixed_block(rows),
            fixed_block(8),
        ],
        out_specs=[pl.BlockSpec((rows, 3 * LANES), lambda p: (0, p)), lane_block(8, 1, 0)],
        out_shape=[
            jax.ShapeDtypeStruct((rows, 3 * width), bf16),
            jax.ShapeDtypeStruct((8, width), f32),
        ],
        scratch_shapes=[pltpu.VMEM((2, rows, LANES), bf16)] * 2
        + [pltpu.VMEM((rows, LANES), f32)] * 3,
        compiler_params=pltpu.CompilerParams(vmem_limit_bytes=50 * 2**20),
        cost_estimate=LIGHT,
        name="self_bwd",
    )(query, kv, kv, raw, raw, own, lse, dmix, dq_cross, cosine, sine, gains)


def feed_kernel(x_ref, grad_ref, gate_ref, up_ref, down_ref, *refs):
    f32, bf16 = jnp.float32, jnp.bfloat16
    hidden_ref, both_ref = refs[-2:]
    gate = jnp.dot(x_ref[...], gate_ref[...], preferred_element_type=f32)
    up = jnp.dot(x_ref[...], up_ref[...], preferred_element_type=f32)
    dhidden = jnp.dot(grad_ref[...], down_ref[...], preferred_element_type=f32)
    sig = 1.0 / (1.0 + jnp.exp(-gate))
    act = gate * sig
    hidden_ref[...] = (act * up).astype(bf16)
    tile = gate_ref.shape[1]
    both_ref[:, :tile] = (dhidden * up * sig * (1.0 + gate * (1.0 - sig))).astype(bf16)
    both_ref[:, tile:] = (dhidden * act).astype(bf16)


def feed_forward(part, x, grad, weights, units, tile, kept=()):
    count, depth = x.shape
    rows = grad.shape[0]
    blocks = units // tile
    bf16 = jnp.bfloat16

    def cols(scale, shift):
        return pl.BlockSpec((depth, tile), lambda j: (0, scale * j + shift))

    return pl.pallas_call(
        feed_kernel,
        grid=(blocks,),
        in_specs=[
            pl.BlockSpec((count, depth), lambda j: (0, 0)),
            pl.BlockSpec((count, depth), lambda j: (part, 0)),
            cols(2, 0),
            cols(2, 1),
            cols(1, 2 * blocks),
        ]
        + [pl.BlockSpec(memory_space=pl.ANY)] * len(kept),
        out_specs=[
            pl.BlockSpec((count, tile), lambda j: (part, j)),
            pl.BlockSpec((count, 2 * tile), lambda j: (part, j)),
        ],
        out_shape=[
            jax.ShapeDtypeStruct((rows, units), bf16),
            jax.ShapeDtypeStruct((rows, 2 * units), bf16),
        ],
        input_output_aliases={5 + n: n for n in range(len(kept))},
        compiler_params=pltpu.CompilerParams(vmem_limit_bytes=58 * 2**20),
        cost_estimate=LIGHT,
        name="feed_forward",
    )(x, grad, weights, weights, weights, *kept)


def outer_kernel(size, bits, me_ref, left_ref, right_ref, keep_ref, away_ref, total_ref):
    total_ref[...] = tn_dot(left_ref[...], right_ref[...])
    rows = keep_ref.shape[0] // (size // 2)
    for place in range(size):
        slot = sum(((place >> (len(bits) - 1 - k)) & 1) << bit for k, bit in enumerate(bits))
        start = pl.multiple_of((me_ref[0] ^ slot) * rows, 16)
        block = total_ref[pl.ds(start, rows), :].astype(jnp.bfloat16)
        out_ref = keep_ref if place < size // 2 else away_ref
        spot = place % (size // 2)
        out_ref[spot * rows : (spot + 1) * rows, :] = block


def outer_grads(me, left, right, size, bits, tile):
    tokens, depth = left.shape
    cols = right.shape[1]
    half = jax.ShapeDtypeStruct((depth // 2, cols), jnp.bfloat16)
    return pl.pallas_call(
        functools.partial(outer_kernel, size, bits),
        grid=(cols // tile,),
        in_specs=[
            pl.BlockSpec(memory_space=pltpu.SMEM),
            pl.BlockSpec((tokens, depth), lambda j: (0, 0)),
            pl.BlockSpec((tokens, tile), lambda j: (0, j)),
        ],
        out_specs=[pl.BlockSpec((depth // 2, tile), lambda j: (0, j))] * 2,
        out_shape=[half, half],
        scratch_shapes=[pltpu.VMEM((depth, tile), jnp.float32)],
        compiler_params=pltpu.CompilerParams(vmem_limit_bytes=50 * 2**20),
        cost_estimate=LIGHT,
        name="outer_grads",
    )(me, left, right)


def product_kernel(turned, has_add, *refs):
    left_ref, right_ref = refs[:2]
    dot = nt_dot if turned else (lambda a, b: jnp.dot(a, b, preferred_element_type=jnp.float32))
    total = dot(left_ref[...], right_ref[...])
    if has_add:
        total = total + refs[2][...].astype(jnp.float32)
    low = 0
    for out_ref in refs[2 + has_add :]:
        count = out_ref.shape[0]
        out_ref[...] = total[low : low + count].astype(out_ref.dtype)
        low += count


def product(left, right, cols, tile, dtype, turned=False, shift=0, add=None, part=(0, 1), cut=0):
    depth = left.shape[1]
    rows = left.shape[0] // part[1]
    counts = [cut, rows - cut] if cut else [rows]
    if turned:
        right_block = pl.BlockSpec((tile, depth), lambda j: (j, shift))
    else:
        right_block = pl.BlockSpec((depth, tile), lambda j: (0, j + shift))
    in_specs = [pl.BlockSpec((rows, depth), lambda j: (part[0], 0)), right_block]
    if add is not None:
        in_specs.append(pl.BlockSpec((rows, tile), lambda j: (0, j)))
    outs = pl.pallas_call(
        functools.partial(product_kernel, turned, add is not None),
        grid=(cols // tile,),
        in_specs=in_specs,
        out_specs=[pl.BlockSpec((count, tile), lambda j: (0, j)) for count in counts],
        out_shape=[jax.ShapeDtypeStruct((count, cols), dtype) for count in counts],
        compiler_params=pltpu.CompilerParams(vmem_limit_bytes=58 * 2**20),
        cost_estimate=LIGHT,
        name="product",
    )(left, right, *([] if add is None else [add]))
    return outs if cut else outs[0]


def gated(value, *tokens):
    return lax.optimization_barrier((value,) + tokens)[0]


def flip_perm(size, bit):
    return [(i, i ^ bit) for i in range(size)]


class SmallScatter:
    def __init__(self, value, size):
        self.value, self.size, self.bit = value, size, 0

    def left(self):
        return self.value.shape[0] > 1

    def hop(self, *tokens):
        if not self.left():
            return None
        index = lax.axis_index("dp")
        value = gated(self.value, *tokens) if tokens else self.value
        pairs = value.reshape(value.shape[0] // 2, 2, value.shape[1])
        upper = (index >> self.bit) % 2 == 1
        away = jnp.where(upper, pairs[:, 0], pairs[:, 1])
        came = lax.ppermute(away, "dp", flip_perm(self.size, 1 << self.bit))
        self.value = jnp.where(upper, pairs[:, 1], pairs[:, 0]) + came
        self.bit += 1
        return came


class Halving:
    def __init__(self, size, bits, keep, away):
        self.size, self.bits, self.stage = size, bits, 0
        self.terms = [keep]
        self.whole = [keep]
        self.out = away

    def start(self):
        bit = self.bits[self.stage]
        self.came = lax.ppermute(self.out, "dp", flip_perm(self.size, 1 << bit))
        self.stage += 1

    def land(self, *tokens):
        self.came = gated(self.came, *tokens)
        return self.came

    def finish(self, *tokens):
        came = gated(self.came, *tokens) if tokens else self.came
        self.terms.append(came)
        self.whole.append(came)
        rows = self.terms[-1].shape[0]
        last = self.stage == len(self.bits)
        half = rows if last else rows // 2
        low = 0 if last else half
        total = sum(term[low : low + half].astype(jnp.float32) for term in self.terms)
        self.out = total if last else total.astype(jnp.bfloat16)
        self.terms = [term[:half] for term in self.terms]
        return self.out

    def drain(self, *tokens):
        while self.stage < len(self.bits):
            self.finish(*tokens)
            self.start()
            tokens = ()
        came = gated(self.came, *tokens) if tokens else self.came
        return self.whole + [came]


def swap_start(part, size, chunks):
    step = part.shape[0] // chunks
    own = [part[i * step : (i + 1) * step] for i in range(chunks)]
    if size == 2:
        return own, [lax.ppermute(o, "tensor", flip_perm(size, 1)) for o in own]
    return own, [lax.psum(o, "tensor") for o in own]


def swap_end(own, came, size):
    f32 = jnp.float32
    both = [o.astype(f32) + c.astype(f32) if size == 2 else c.astype(f32) for o, c in zip(own, came)]
    return jnp.concatenate(both, axis=0) if len(both) > 1 else both[0]


def small_gather(value, name, size, tokens=(), steps=None):
    index = lax.axis_index(name)
    for k in range(size.bit_length() - 1):
        bit = 1 << k
        if k < len(tokens):
            value = gated(value, tokens[k])
        came = lax.ppermute(value, name, flip_perm(size, bit))
        upper = (index // bit) % 2 == 1
        value = jnp.where(
            upper, jnp.concatenate([came, value], 0), jnp.concatenate([value, came], 0)
        )
        if steps is not None:
            steps.append(value)
    return value


class Hops:
    def __init__(self, value, size):
        self.value, self.size, self.bit = value, size, 0

    def start(self, *tokens):
        if self.bit < self.size.bit_length() - 1:
            value = gated(self.value, *tokens) if tokens else self.value
            self.came = lax.ppermute(value, "dp", flip_perm(self.size, 1 << self.bit))

    def finish(self, *tokens):
        if self.bit < self.size.bit_length() - 1:
            came = gated(self.came, *tokens) if tokens else self.came
            upper = (lax.axis_index("dp") >> self.bit) % 2 == 1
            self.value = jnp.where(
                upper,
                jnp.concatenate([came, self.value], 0),
                jnp.concatenate([self.value, came], 0),
            )
            self.bit += 1
        return self.value

    def drain(self):
        while self.bit < self.size.bit_length() - 1:
            self.start()
            self.finish()
        return self.value


def small_sum(value, name, size):
    bit = 1
    while bit < size:
        value = value + lax.ppermute(value, name, flip_perm(size, bit))
        bit *= 2
    return value


def tensor_scatter(part, size):
    if size == 2:
        index = lax.axis_index("tensor")
        width = part.shape[1] // 2
        away = lax.dynamic_slice_in_dim(part, (1 - index) * width, width, 1)
        kept = lax.dynamic_slice_in_dim(part, index * width, width, 1)
        came = lax.ppermute(away, "tensor", flip_perm(size, 1))
        return kept.astype(jnp.float32) + came.astype(jnp.float32)
    return lax.psum_scatter(part, "tensor", scatter_dimension=1, tiled=True).astype(jnp.float32)


def weave_kernel(tile, plan, *refs):
    out_ref = refs[-1]
    out_ref[...] = jnp.zeros_like(out_ref)
    for target, source, low, wide, turned in plan:
        if turned:
            out_ref[:, target : target + wide] = refs[source][low : low + wide, :].T
        else:
            out_ref[:, target : target + wide] = refs[source][:, low : low + wide]


def weave(arrays, tile, last=None):
    rows, cols = arrays[0].shape
    count = -(-cols // tile)
    plan = []
    target = 0
    for i in range(count):
        for source in range(len(arrays)):
            plan.append((target, source, i * tile, min(tile, cols - i * tile), False))
            target += tile
    operands = list(arrays)
    if last is not None:
        plan.append((target, len(arrays), 0, last.shape[0], True))
        target += last.shape[0] + -last.shape[0] % tile
        operands.append(last)
    return pl.pallas_call(
        functools.partial(weave_kernel, tile, plan),
        out_shape=jax.ShapeDtypeStruct((rows, target), arrays[0].dtype),
        compiler_params=pltpu.CompilerParams(vmem_limit_bytes=30 * 2**20),
        cost_estimate=LIGHT,
        name="weave",
    )(*operands)


def gather_sum_kernel(tile, sizes, count, *refs):
    outs = refs[-count:]
    cols = outs[0].shape[1]
    low = 0
    base = 0
    for size in sizes:
        total = refs[low][...].astype(jnp.float32)
        for ref in refs[low + 1 : low + size]:
            total = total + ref[...].astype(jnp.float32)
        low += size
        tiles = total.shape[1] // (tile * count)
        for i in range(tiles):
            start = base + i * tile
            wide = min(tile, cols - start)
            for n, out_ref in enumerate(outs):
                at = (i * count + n) * tile
                out_ref[:, start : start + wide] = total[:, at : at + wide]
        base += tiles * tile


def gather_sum(groups, tile, count, cols):
    rows = groups[0][-1].shape[0]
    terms = [term for group in groups for term in group]
    wide = sum(term.shape[1] for term in terms) * 2 + count * cols * 4
    block = rows
    while block * wide > 12 * 2**20 and block % 32 == 0:
        block //= 2
    return pl.pallas_call(
        functools.partial(gather_sum_kernel, tile, [len(group) for group in groups], count),
        grid=(rows // block,),
        in_specs=[pl.BlockSpec((block, term.shape[1]), lambda r: (r, 0)) for term in terms],
        out_specs=[pl.BlockSpec((block, cols), lambda r: (r, 0))] * count,
        out_shape=[jax.ShapeDtypeStruct((rows, cols), jnp.float32)] * count,
        compiler_params=pltpu.CompilerParams(vmem_limit_bytes=58 * 2**20),
        cost_estimate=LIGHT,
        name="gather_sum",
    )(*terms)


def fold_plan(rows, blocks, tall):
    plan = []
    for block in range(blocks):
        low = block * rows
        while low < (block + 1) * rows:
            high = min((block + 1) * rows, (low // tall + 1) * tall)
            plan.append((block, low - block * rows, low % tall, low // tall, high - low))
            low = high
    return plan


def pack_kernel(rows, tall, wide, plans, *refs):
    out_ref = refs[-1]
    out_ref[...] = jnp.zeros_like(out_ref)
    text_plan, rest_plan = plans
    for target, source, low, width, _ in text_plan:
        out_ref[:, target : target + width] = refs[source][:, low : low + width]
    for block, at, row, col, count in fold_plan(rows, len(rest_plan), tall):
        source, low, width, turned = rest_plan[block]
        if turned:
            piece = refs[source][low : low + width, :].T
        else:
            piece = refs[source][:, low : low + width]
        start = wide + col * LANES
        out_ref[row : row + count, start : start + width] = piece[at : at + count]


def pack_weights(text, attention, last):
    tall, cols = text[0].shape
    rows = attention[0].shape[0]
    tiles = -(-cols // LANES)
    text_plan = []
    rest_plan = []
    for i in range(tiles):
        width = min(LANES, cols - i * LANES)
        for n in range(len(text)):
            target = (i * len(text) + n) * LANES
            text_plan.append((target, n, i * LANES, width, False))
        for n in range(len(attention)):
            rest_plan.append((len(text) + n, i * LANES, width, False))
    for i in range(tiles):
        width = min(LANES, cols - i * LANES)
        rest_plan.append((len(text) + len(attention), i * LANES, width, True))
    wide = tiles * len(text) * LANES
    folded = len(rest_plan) * rows // tall * LANES
    return pl.pallas_call(
        functools.partial(pack_kernel, rows, tall, wide, (text_plan, rest_plan)),
        out_shape=jax.ShapeDtypeStruct((tall, wide + folded), text[0].dtype),
        compiler_params=pltpu.CompilerParams(vmem_limit_bytes=30 * 2**20),
        cost_estimate=LIGHT,
        name="pack_weights",
    )(*text, *attention, last)


def unfold_kernel(rows, tall, blocks, size, edge, left_ref, *refs):
    full_ref, raw_ref = refs[-2:]
    plan = fold_plan(rows, blocks, tall)

    def place(d, _):
        start = pl.multiple_of(d * rows, 16)
        for block, at, row, col, count in plan:
            full_ref[pl.ds(start + at, count), block * LANES : (block + 1) * LANES] = refs[col][
                d, row : row + count, :
            ]
        return 0

    lax.fori_loop(0, size, place, 0)
    last = pl.program_id(0) == pl.num_programs(0) - 1

    @pl.when(jnp.logical_not(last))
    def _():
        raw_ref[...] = jnp.dot(left_ref[...], full_ref[...], preferred_element_type=jnp.float32)

    @pl.when(last)
    def _():
        raw_ref[:, :edge] = jnp.dot(
            left_ref[...], full_ref[:, :edge], preferred_element_type=jnp.float32
        )


def unfold_product(left, packed, rows, tall, blocks, used, size):
    period = math.lcm(rows, tall)
    span, folds = period // rows, period // tall
    steps = blocks // span
    skip = packed.shape[1] // LANES - folds * steps
    tokens = left.shape[0]
    view = packed.reshape(size, tall, packed.shape[1])
    return pl.pallas_call(
        functools.partial(
            unfold_kernel, rows, tall, span, size, (used - (steps - 1) * span) * LANES
        ),
        grid=(steps,),
        in_specs=[pl.BlockSpec(left.shape, lambda j: (0, 0))]
        + [
            pl.BlockSpec((size, tall, LANES), lambda j, k=k: (0, 0, skip + folds * j + k))
            for k in range(folds)
        ],
        out_specs=[
            pl.BlockSpec((size * rows, span * LANES), lambda j: (0, j)),
            pl.BlockSpec((tokens, span * LANES), lambda j: (0, j)),
        ],
        out_shape=[
            jax.ShapeDtypeStruct((size * rows, blocks * LANES), packed.dtype),
            jax.ShapeDtypeStruct((tokens, blocks * LANES), jnp.float32),
        ],
        compiler_params=pltpu.CompilerParams(vmem_limit_bytes=58 * 2**20),
        cost_estimate=LIGHT,
        name="unfold_product",
    )(left, *[view] * folds)


def rotary_tables(row_pos, col_pos, quarter, repeat):
    frequency = jnp.exp(-math.log(10000.0) * jnp.arange(quarter, dtype=jnp.float32) / quarter)
    angles = jnp.concatenate(
        [
            row_pos.astype(jnp.float32)[:, None] * frequency,
            col_pos.astype(jnp.float32)[:, None] * frequency,
        ],
        axis=1,
    )
    sine = jnp.sin(angles)
    return jnp.tile(jnp.cos(angles), (1, 2 * repeat)), jnp.tile(
        jnp.concatenate([-sine, sine], axis=1), (1, repeat)
    )


def local(
    size,
    groups,
    latents,
    cotangent,
    caption,
    caption_lens,
    patch_row,
    patch_col,
    timestep,
    query_proj,
    key_proj,
    value_proj,
    output_proj,
    textkey_proj,
    textval_proj,
    gate_proj,
    up_proj,
    down_proj,
    modulation,
    attn_gain,
    ffn_gain,
    query_gain,
    key_gain,
    textkey_gain,
    cross_gate,
):
    f32, bf16 = jnp.float32, jnp.bfloat16
    rows_w, chan = query_proj.shape
    units = gate_proj.shape[1]
    head_part = query_gain.shape[0]
    head_dim = head_part * size
    heads_here = chan // head_dim
    model_dim = latents.shape[1]
    padded = chan + -chan % LANES
    pairs = padded // LANES
    dp_index = lax.axis_index("dp")
    tensor_index = lax.axis_index("tensor")

    small = jnp.concatenate(
        [
            attn_gain.astype(f32),
            ffn_gain.astype(f32),
            query_gain.astype(f32),
            key_gain.astype(f32),
            textkey_gain.astype(f32),
            timestep.astype(f32),
        ]
    )[None]
    steps = []
    small_all = small_gather(small, "dp", size, (), steps)
    packed = pack_weights(
        [textkey_proj, textval_proj], [query_proj, key_proj, value_proj], output_proj
    )
    packed_set = lax.all_gather(packed, "dp", axis=0, tiled=True)

    cuts = [rows_w, 2 * rows_w, 2 * rows_w + head_part]
    gain_one = small_all[:, : cuts[0]].reshape(-1)
    gain_two = small_all[:, cuts[0] : cuts[1]].reshape(-1)
    gain_query = small_all[:, cuts[1] : cuts[2]].reshape(-1)
    gain_key = small_all[:, cuts[2] : cuts[2] + head_part].reshape(-1)
    gain_text = small_all[:, cuts[2] + head_part : cuts[2] + 2 * head_part].reshape(-1)
    steps_all = small_all[:, cuts[2] + 2 * head_part :].reshape(-1)
    embed_rows = modulation.shape[0]
    embed_dim = embed_rows * size
    embed_all = time_embed(steps_all, embed_dim)
    cond_all = (embed_all * jax.nn.sigmoid(embed_all)).astype(bf16)
    cond_here = lax.dynamic_slice_in_dim(cond_all, dp_index * embed_rows, embed_rows, 1)
    mod_part = jnp.dot(cond_here, modulation, preferred_element_type=f32)
    mod_sums = SmallScatter(mod_part, size)
    while mod_sums.left():
        mod_sums.hop()
    mod_here = mod_sums.value
    mod_all = small_gather(mod_here, "tensor", groups).reshape(1, -1)
    tile = 256
    blocks = units // tile
    gate_l, up_l, down_l = gated((gate_proj, up_proj, down_proj), small_all)
    third = weave([gate_l, up_l], tile, down_l)
    ffn_set = lax.all_gather(gated(third, small_all), "dp", axis=0, tiled=True)
    scale_one = mod_all[:, 0:model_dim]
    gate_one = jnp.tanh(mod_all[:, model_dim : 2 * model_dim])
    scale_two = mod_all[:, 2 * model_dim : 3 * model_dim]
    gate_two = jnp.tanh(mod_all[:, 3 * model_dim : 4 * model_dim])
    tanh_cross = jnp.tanh(cross_gate.astype(f32))
    tanh_lanes = jnp.pad(jnp.repeat(tanh_cross, head_dim), (0, padded - chan))
    tanh_lanes = jnp.broadcast_to(tanh_lanes[None], (8, padded))
    per_tile = LANES // head_dim
    gain_lanes = jnp.pad(
        jnp.tile(jnp.stack([gain_query, gain_key, gain_text]), (1, per_tile)), ((0, 5), (0, 0))
    )
    cosine, sine = rotary_tables(patch_row[0], patch_col[0], head_dim // 4, per_tile)
    tables = (cosine, sine, gain_lanes, tanh_lanes)

    resid_in = latents.astype(f32)
    factor_one = inv_rms(resid_in)
    normed_one = resid_in * factor_one
    attn_in = (normed_one * gain_one * (1.0 + scale_one)).astype(bf16)
    grad_out = cotangent.astype(f32)
    grad_ffn = (gate_two * grad_out).astype(bf16)
    full_text = gated(packed_set, attn_in, grad_ffn)
    full_qkvo, qkv_raw = unfold_product(
        attn_in, full_text, rows_w, packed.shape[0], 4 * pairs, 3 * pairs, size
    )
    cap_in = caption[0]
    text_raw = product(gated(cap_in, qkv_raw), full_text, 2 * padded, 256, f32)
    mixed_a, query_bf, own_out, cross_out, lse, kv_bf, tkv_bf = attend_rows(
        0, caption_lens, qkv_raw, text_raw, tables, head_dim
    )
    part_a = product(mixed_a, full_qkvo, model_dim, 512, bf16, True, 3)
    own_a, came_a = swap_start(part_a, groups, 1)
    kept = gated((query_bf, own_out, cross_out, lse, kv_bf, tkv_bf), part_a)
    mixed_b, query_bf, own_out, cross_out, lse = attend_rows(
        1, caption_lens, qkv_raw, text_raw, tables, head_dim, kept
    )
    attn_part = product(mixed_b, full_qkvo, model_dim, 512, bf16, True, 3)
    mixed_heads = jnp.concatenate([mixed_a, mixed_b], axis=0)
    mod_set = lax.all_gather(gated(modulation, qkv_raw), "dp", axis=0, tiled=True)

    came_a = gated(came_a, attn_part)
    own_b, came_b = swap_start(gated(attn_part, came_a), groups, 1)
    half_rows = grad_ffn.shape[0] // 2
    full_ffn = gated(ffn_set, attn_part)
    gain_mul = gain_two * (1.0 + scale_two)

    def feed_input(resid, own, came):
        attn_sum = swap_end(own, came, groups)
        total = resid + gate_one * attn_sum
        factor = inv_rms(total)
        normed = total * factor
        return attn_sum, total, factor, normed, (normed * gain_mul).astype(bf16)

    resid_a, resid_b = resid_in[:half_rows], resid_in[half_rows:]
    attn_out_a, residual_a, factor_a, normed_a, feed_a = feed_input(resid_a, own_a, came_a)
    kept = feed_forward(0, feed_a, grad_ffn, full_ffn, units, tile)
    dffn_one = product(kept[1], full_ffn, model_dim, 512, bf16, True, 0, None, (0, 2))
    one_own, one_came = swap_start(dffn_one, groups, 1)
    came_b = gated(came_b, dffn_one)
    attn_out_b, residual_b, factor_b, normed_b, feed_b = feed_input(resid_b, own_b, came_b)
    hidden, dboth = feed_forward(
        1, feed_b, grad_ffn, full_ffn, units, tile, gated(kept, dffn_one)
    )
    dffn_two = product(dboth, full_ffn, model_dim, 512, bf16, True, 0, None, (1, 2))
    ffn_in = jnp.concatenate([feed_a, feed_b], axis=0)
    me = dp_index.astype(jnp.int32)[None]
    depth_bits = list(range(2, size.bit_length() - 1))
    side_first = [0, 1] + depth_bits
    line_first = [0, 2, 1] + depth_bits[1:]

    def staged(left, right, bits, tile_cols):
        return Halving(size, bits, *outer_grads(me, left, right, size, bits, tile_cols))

    down = staged(grad_ffn, gated(hidden, dffn_two), line_first, 512)
    down.start()
    one_came = gated(one_came, down.out)
    two_own, two_came = swap_start(gated(dffn_two, one_came), groups, 1)
    grown = staged(ffn_in, gated(dboth, down.out, one_came), side_first, 512)
    grown.start()
    ffn_part = product(gated(hidden, grown.out, mod_set), full_ffn, model_dim, 512, bf16, True, 2)
    grad_out_a, grad_out_b = grad_out[:half_rows], grad_out[half_rows:]

    def feed_back(grad, own, came, normed, factor, attn_sum):
        dffn = swap_end(own, came, groups)
        dres = grad + norm_back(dffn * gain_mul, normed, factor)
        sums_here = jnp.sum(dffn * normed, axis=0), jnp.sum(dres * attn_sum, axis=0)
        return dres, (gate_one * dres).astype(bf16), sums_here

    dres_a, grad_attn_a, sums_a = feed_back(
        grad_out_a, one_own, one_came, normed_a, factor_a, attn_out_a
    )
    dmix_a = product(
        gated(grad_attn_a, ffn_part), full_qkvo, padded, LANES, bf16, False, 3 * padded // LANES
    )
    two_came = gated(two_came, dmix_a)
    down.finish(two_came)
    down.start()
    grown.finish(down.out)
    grown.start()
    dres_b, grad_attn_b, sums_b = feed_back(
        grad_out_b, two_own, gated(two_came, grown.out), normed_b, factor_b, attn_out_b
    )
    dmix_b = product(grad_attn_b, full_qkvo, padded, LANES, bf16, False, 3 * padded // LANES)
    dmixed = jnp.concatenate([dmix_a, dmix_b], axis=0)
    grad_attn = jnp.concatenate([grad_attn_a, grad_attn_b], axis=0)
    weighed = sums_a[0] + sums_b[0]
    grad_gaintwo = weighed * (1.0 + scale_two[0])
    dscale_two = weighed * gain_two
    dgate_one = (sums_a[1] + sums_b[1]) * (1.0 - gate_one[0] ** 2)
    dresid = jnp.concatenate([dres_a, dres_b], axis=0)
    residual = jnp.concatenate([residual_a, residual_b], axis=0)
    ffn_own, ffn_came = swap_start(gated(ffn_part, dmixed), groups, 1)
    dq_cross, dtext, stats_c = cross_back(
        caption_lens, query_bf, tkv_bf, text_raw, cross_out, lse, dmixed, tables, head_dim
    )
    down.finish(dq_cross)
    down.start()
    text = staged(cap_in, gated(dtext, down.out), side_first, 256)
    grown.finish(text.out)
    grown.start()
    text.out = gated(text.out, grown.out)
    text.start()
    split = pairs - pairs // 2
    windows = [(0, split), (split, pairs - split)]
    common = (query_bf, kv_bf, qkv_raw, own_out, lse)
    dmixed_a = gated(dmixed, text.out)
    dqkv_a, stats_a = self_back(windows[0], *common, dmixed_a, dq_cross, tables, head_dim)
    down.finish(dqkv_a)
    down.start()
    grown.finish(down.out)
    grown.start()
    text.finish(grown.out)
    text.start()
    outp = staged(gated(grad_attn, text.out), mixed_heads, side_first, padded)
    outp.start()
    first_qkv = staged(attn_in, gated(dqkv_a, outp.out), side_first, 3 * LANES)
    edge = 3 * LANES * split
    even = pairs == 2 * split
    wide_a = full_qkvo if even else full_qkvo[:, :edge]
    wide_b = full_qkvo if even else full_qkvo[:, edge : 3 * padded]
    dattn_a = product(gated(dqkv_a, first_qkv.out), wide_a, model_dim, 512, f32, True)
    outp.finish(dattn_a)
    outp.start()
    dmixed_b = gated(dmixed, outp.out)
    dqkv_b, stats_b = self_back(windows[1], *common, dmixed_b, dq_cross, tables, head_dim)
    landed = (down.land(dqkv_b), grown.land(dqkv_b), gated(ffn_came, dqkv_b))
    ffn_came = landed[2]
    dqkv_l = gated(dqkv_b, *landed)
    cut = latents.shape[0] * 5 // 8
    top, low = product(
        dqkv_l, wide_b, model_dim, 512, bf16, True, int(even), dattn_a, (0, 1), cut
    )
    high_own, high_came = swap_start(top, groups, 1)
    first_qkv.out = gated(first_qkv.out, low)
    first_qkv.start()
    last_qkv = staged(attn_in, gated(dqkv_b, low), side_first, 3 * LANES)
    last_qkv.start()
    text.finish(last_qkv.out)
    text.start()
    first_qkv.finish(text.out)
    first_qkv.start()
    outp.finish(first_qkv.out)
    outp.start()
    last_qkv.finish(outp.out)
    last_qkv.start()
    caption_part = product(
        gated(dtext, last_qkv.out), full_text, cap_in.shape[1], 1024, bf16, True
    )
    grad_gate, grad_up = gather_sum([grown.drain(caption_part)], tile, 2, units)
    top_l, low_l, ffn_l = gated((top, low, ffn_part), grad_gate)
    weighed_part = jnp.sum(top_l.astype(f32) * normed_one[:cut], axis=0)
    weighed_part = weighed_part + jnp.sum(low_l.astype(f32) * normed_one[cut:], axis=0)
    gate_part = jnp.sum(grad_out * ffn_l.astype(f32), axis=0)
    stats = jnp.concatenate([stats_a, stats_b], axis=1)[:2]
    stat_sums = jnp.concatenate([stats, stats_c[:2]], axis=0)[:, :chan]
    stat_sums = jnp.sum(stat_sums.reshape(4, heads_here, head_dim), axis=(1,))
    xgate_rows = stats_c[1, :chan].reshape(heads_here, head_dim)
    xgate_here = jnp.sum(xgate_rows, axis=1) * (1.0 - tanh_cross**2)
    sums_part = jnp.concatenate([weighed_part, gate_part, stat_sums[:3].reshape(-1)])[None]
    sums = small_sum(sums_part, "tensor", groups)[0]
    high_came = gated(high_came, sums_part)
    base_own, base_came = swap_start(gated(low, high_came), groups, 1)
    sums = gated(sums, high_came)
    weighed_one, head_gains = sums[:model_dim], sums[2 * model_dim :]
    dgate_two = sums[model_dim : 2 * model_dim] * (1.0 - gate_two[0] ** 2)
    grad_gainone = weighed_one * (1.0 + scale_one[0])
    dscale_one = weighed_one * gain_one
    dmod_all = jnp.concatenate([dscale_one, dgate_one, dscale_two, dgate_two])
    cols_here = modulation.shape[1]
    dmod_here = lax.dynamic_slice_in_dim(dmod_all, tensor_index * cols_here, cols_here, 0)
    row = jnp.concatenate([dmod_here, grad_gainone, grad_gaintwo, head_gains, xgate_here])
    row = row.astype(bf16).astype(f32)[None]
    hops = Hops(row, size)
    hops.start()
    text.finish(row)
    text.start()
    first_qkv.finish(text.out)
    first_qkv.start()
    last_qkv.finish(first_qkv.out)
    last_qkv.start()
    hops.finish(last_qkv.out)
    hops.start()
    outp.finish(hops.value)
    outp.start()
    down_t = sum(term[:rows_w].astype(f32) for term in down.drain(outp.out))
    hops.finish(down_t)
    hops.start()
    ffn_out = swap_end(ffn_own, gated(ffn_came, hops.value), groups)
    output = (residual + gate_two * ffn_out).astype(bf16)
    first_qkv.finish(output)
    first_qkv.start()
    last_qkv.finish(first_qkv.out)
    last_qkv.start()
    hops.finish(last_qkv.out)
    hops.start()
    base_came = gated(base_came, hops.value)
    dcaption = tensor_scatter(gated(caption_part, base_came), groups)
    dattn_in = jnp.concatenate(
        [swap_end(high_own, high_came, groups), swap_end(base_own, base_came, groups)], axis=0
    )
    grad_latents = (
        dresid + norm_back(dattn_in * gain_one * (1.0 + scale_one), normed_one, factor_one)
    ).astype(bf16)
    embed_row = jnp.einsum(
        "bc,tc->bt", row[:, :cols_here].astype(bf16), mod_set, preferred_element_type=f32
    )
    grad_textkey, grad_textval = gather_sum([text.drain(grad_latents)], LANES, 2, chan)
    hops.finish(grad_textkey)
    rows_set = hops.drain()
    dmod_set = rows_set[:, :cols_here].astype(bf16)
    gain_sums = jnp.sum(rows_set[:, cols_here:], axis=0)
    grad_modul = jnp.einsum("bt,bc->tc", cond_here, dmod_set, preferred_element_type=f32)
    embed_sum = small_sum(embed_row, "tensor", groups)
    embed_own = lax.dynamic_slice_in_dim(embed_all, dp_index, 1, 0)
    sig_own = jax.nn.sigmoid(embed_own)
    dembed_all = embed_sum * (sig_own * (1.0 + embed_own * (1.0 - sig_own)))
    width = embed_dim // groups
    dembed = lax.dynamic_slice_in_dim(dembed_all, tensor_index * width, width, 1)
    output_t = sum(term[:rows_w].astype(f32) for term in outp.drain(grad_textkey))
    parts = [last_qkv.drain(output_t), first_qkv.drain(output_t)][::-1]
    grad_query, grad_key, grad_value = gather_sum(parts, LANES, 3, chan)

    def own_part(start, width):
        return lax.dynamic_slice_in_dim(gain_sums, start + dp_index * width, width, 0)

    heads_at = 2 * model_dim
    gate_at = heads_at + 3 * head_dim
    return (
        output,
        grad_latents,
        dcaption.astype(bf16)[None],
        dembed,
        grad_query,
        grad_key,
        grad_value,
        output_t[:, :chan].T,
        grad_textkey,
        grad_textval,
        grad_gate,
        grad_up,
        down_t.T,
        grad_modul,
        own_part(0, rows_w),
        own_part(model_dim, rows_w),
        own_part(heads_at, head_part),
        own_part(heads_at + head_dim, head_part),
        own_part(heads_at + 2 * head_dim, head_part),
        gain_sums[gate_at:],
    )


def solution(mesh):
    in_specs = (
        P("dp", None),
        P("dp", None),
        P("dp", None, None),
        P("dp"),
        P("dp", None),
        P("dp", None),
        P("dp"),
        P("dp", "tensor"),
        P("dp", "tensor"),
        P("dp", "tensor"),
        P("tensor", "dp"),
        P("dp", "tensor"),
        P("dp", "tensor"),
        P("dp", "tensor"),
        P("dp", "tensor"),
        P("tensor", "dp"),
        P("dp", "tensor"),
        P("dp"),
        P("dp"),
        P("dp"),
        P("dp"),
        P("dp"),
        P("tensor"),
    )
    out_specs = (
        P("dp", None),
        P("dp", None),
        P("dp", None, "tensor"),
        P("dp", "tensor"),
        P("dp", "tensor"),
        P("dp", "tensor"),
        P("dp", "tensor"),
        P("tensor", "dp"),
        P("dp", "tensor"),
        P("dp", "tensor"),
        P("dp", "tensor"),
        P("dp", "tensor"),
        P("tensor", "dp"),
        P("dp", "tensor"),
        P("dp"),
        P("dp"),
        P("dp"),
        P("dp"),
        P("dp"),
        P("tensor"),
    )
    bound = functools.partial(local, mesh.shape["dp"], mesh.shape["tensor"])
    return jax.shard_map(bound, mesh=mesh, in_specs=in_specs, out_specs=out_specs, check_vma=False)
```

```python
import functools
import math

import jax
import jax.numpy as jnp
from jax import lax
from jax.experimental import pallas as pl
from jax.experimental.pallas import tpu as pltpu
from jax.sharding import PartitionSpec as P

EPSILON = 1e-06


def inv_rms(values):
    return lax.rsqrt(jnp.mean(values * values, axis=-1, keepdims=True) + EPSILON)


def time_embed(step_vals, embed_width):
    half_width = embed_width // 2
    frequency = jnp.exp(-math.log(10000.0) * jnp.arange(half_width, dtype=jnp.float32) / half_width)
    phases = step_vals.astype(jnp.float32)[:, None] * frequency
    return jnp.concatenate([jnp.cos(phases), jnp.sin(phases)], axis=1)


def norm_back(grad_hat, normed, factor):
    return factor * (grad_hat - normed * jnp.mean(grad_hat * normed, axis=-1, keepdims=True))


LANES = 128
LIGHT = pl.CostEstimate(flops=1, transcendentals=0, bytes_accessed=1)


def lane_ids(rows):
    return lax.broadcasted_iota(jnp.int32, (rows, LANES), 1)


def pair_matrix(same, half):
    row = lax.broadcasted_iota(jnp.int32, (LANES, LANES), 0) // half
    col = lax.broadcasted_iota(jnp.int32, (LANES, LANES), 1) // half
    return jnp.where((row == col) == same, 1.0, 0.0).astype(jnp.bfloat16)


def head_sums(values, matrix):
    high = values.astype(jnp.bfloat16)
    low = (values - high.astype(jnp.float32)).astype(jnp.bfloat16)
    return jnp.dot(high, matrix, preferred_element_type=jnp.float32) + jnp.dot(
        low, matrix, preferred_element_type=jnp.float32
    )


def swap_quarters(values, half):
    rows = values.shape[0]
    first = lane_ids(rows) % half < half // 2
    return jnp.where(
        first,
        pltpu.roll(values, LANES - half // 2, 1),
        pltpu.roll(values, half // 2, 1),
    )


def nt_dot(left, right):
    return lax.dot_general(
        left, right, (((1,), (1,)), ((), ())), preferred_element_type=jnp.float32
    )


def tn_dot(left, right):
    return lax.dot_general(
        left, right, (((0,), (0,)), ((), ())), preferred_element_type=jnp.float32
    )


def attend_kernel(half, block, fresh, *refs):
    f32, bf16 = jnp.float32, jnp.bfloat16
    matrix = pair_matrix(True, half)
    if fresh:
        len_ref, rawq_ref, rawk_ref, rawv_ref, text_ref, tval_ref = refs[:6]
        cos_ref, sin_ref, cosk_ref, sink_ref, gain_ref, tanh_ref = refs[6:12]
        mixed_ref, query_ref, own_ref, cross_ref, lse_ref, kv_ref, tkv_ref = refs[12:]
    else:
        len_ref, rawq_ref, kv_ref, tkv_ref, cos_ref, sin_ref, gain_ref, tanh_ref = refs[:8]
        mixed_ref, query_ref, own_ref, cross_ref, lse_ref = refs[12:]

    def hat(raw):
        return raw * lax.rsqrt(head_sums(raw * raw, matrix) * (1.0 / half) + EPSILON)

    def turned(raw, gain, cosine, sine):
        value = hat(raw) * gain
        return (value * cosine + swap_quarters(value, half) * sine).astype(bf16)

    query_ref[...] = turned(rawq_ref[...], gain_ref[0:1], cos_ref[...], sin_ref[...])
    if fresh:
        kv_ref[:, :LANES] = turned(rawk_ref[...], gain_ref[1:2], cosk_ref[...], sink_ref[...])
        kv_ref[:, LANES:] = rawv_ref[...].astype(bf16)
        tkv_ref[:, :LANES] = (hat(text_ref[...]) * gain_ref[2:3]).astype(bf16)
        tkv_ref[:, LANES:] = tval_ref[...].astype(bf16)
    key, value = kv_ref[:, :LANES], kv_ref[:, LANES:]
    tkey, tval = tkv_ref[:, :LANES], tkv_ref[:, LANES:]
    one = jnp.ones((), bf16)
    zero = jnp.zeros((), bf16)

    def pick(a, b):
        return jnp.where(lane_ids(a.shape[0]) < half, a, b)

    def fill(a, fillers, first):
        other = jnp.full(a.shape, fillers, bf16)
        return pick(a, other) if first else pick(other, a)

    value_ones = [fill(value, one, True), fill(value, one, False)]
    tval_ones = [fill(tval, one, True), fill(tval, one, False)]
    keep = lax.broadcasted_iota(jnp.int32, (block, tkey.shape[0]), 1) < len_ref[0]

    def step(i, _):
        here = pl.ds(pl.multiple_of(i * block, block), block)
        q_blk = query_ref[here, :] * jnp.asarray(half**-0.5, bf16)
        outs = []
        texts = []
        for head in range(2):
            q_one = fill(q_blk, zero, head == 0)
            e_self = jnp.exp(nt_dot(q_one, key)).astype(bf16)
            outs.append(jnp.dot(e_self, value_ones[head], preferred_element_type=f32))
            e_text = jnp.where(keep, jnp.exp(nt_dot(q_one, tkey)), 0.0).astype(bf16)
            texts.append(jnp.dot(e_text, tval_ones[head], preferred_element_type=f32))
        for n, (a, b) in enumerate((outs, texts)):
            total = pick(b, a)
            lse_ref[here, n * LANES : (n + 1) * LANES] = jnp.log(total)
            res = pick(a, b) / pltpu.roll(total, half, 1)
            if n == 0:
                own = res
                own_ref[here, :] = res
            else:
                cross_ref[here, :] = res
                mixed_ref[here, :] = (own + tanh_ref[0:1] * res).astype(bf16)
        return 0

    lax.fori_loop(0, query_ref.shape[0] // block, step, 0)


def attend_rows(part, cap_len, raw, text, tables, half, kept=None):
    cosine, sine, gains, tanh_lanes = tables
    rows, caps = raw.shape[0], text.shape[0]
    count = rows // 2
    width = tanh_lanes.shape[1]
    f32, bf16 = jnp.float32, jnp.bfloat16
    fresh = kept is None

    def piece(scale, shift, wide=1):
        return pl.BlockSpec((count, wide * LANES), lambda p: (part, scale * p + shift))

    table = pl.BlockSpec((count, LANES), lambda p: (part, 0))
    whole = pl.BlockSpec(memory_space=pl.ANY)
    smem = pl.BlockSpec(memory_space=pltpu.SMEM)
    kv_block = pl.BlockSpec((rows, 2 * LANES), lambda p: (0, p))
    tkv_block = pl.BlockSpec((caps, 2 * LANES), lambda p: (0, p))
    tail_specs = [fixed_block(8), lane_block(8, 1, 0)]
    out_specs = [
        pl.BlockSpec((count, LANES), lambda p: (0, p)),
        piece(1, 0),
        piece(1, 0),
        piece(1, 0),
        piece(1, 0, 2),
    ]
    out_shape = [
        jax.ShapeDtypeStruct((count, width), bf16),
        jax.ShapeDtypeStruct((rows, width), bf16),
        jax.ShapeDtypeStruct((rows, width), f32),
        jax.ShapeDtypeStruct((rows, width), f32),
        jax.ShapeDtypeStruct((rows, 2 * width), f32),
    ]
    if fresh:
        in_specs = [smem, piece(3, 0), lane_block(rows, 3, 1), lane_block(rows, 3, 2)]
        in_specs += [lane_block(caps, 2, 0), lane_block(caps, 2, 1)]
        in_specs += [table, table, fixed_block(rows), fixed_block(rows)] + tail_specs
        operands = (cap_len, raw, raw, raw, text, text, cosine, sine, cosine, sine)
        operands += (gains, tanh_lanes)
        out_specs += [kv_block, tkv_block]
        out_shape += [
            jax.ShapeDtypeStruct((rows, 2 * width), bf16),
            jax.ShapeDtypeStruct((caps, 2 * width), bf16),
        ]
        aliases = {}
    else:
        query, own, cross, lse, kv, tkv = kept
        in_specs = [smem, piece(3, 0), kv_block, tkv_block, table, table] + tail_specs
        in_specs += [whole] * 4
        operands = (cap_len, raw, kv, tkv, cosine, sine, gains, tanh_lanes)
        operands += (query, own, cross, lse)
        aliases = {8: 1, 9: 2, 10: 3, 11: 4}
    return pl.pallas_call(
        functools.partial(attend_kernel, half, min(256, count), fresh),
        grid=(width // LANES,),
        in_specs=in_specs,
        out_specs=out_specs,
        out_shape=out_shape,
        input_output_aliases=aliases,
        compiler_params=pltpu.CompilerParams(vmem_limit_bytes=50 * 2**20),
        cost_estimate=LIGHT,
        name="attend_fwd",
    )(*operands)


def pick_head(a, b, first, half):
    low = lane_ids(a.shape[0]) < half
    return jnp.where(low, a, b) if first else jnp.where(low, b, a)


def three_parts(value, half):
    spot = lane_ids(value.shape[0]) % half
    high = value.astype(jnp.bfloat16).astype(jnp.float32)
    rest = value - high
    mid = rest.astype(jnp.bfloat16).astype(jnp.float32)
    low = rest - mid
    parts = jnp.where(spot == 0, high, jnp.where(spot == 1, mid, jnp.where(spot == 2, low, 0.0)))
    return parts.astype(jnp.bfloat16)


def with_ones(value, first, half):
    ones = jnp.where(lane_ids(value.shape[0]) % half < 3, 1.0, 0.0).astype(jnp.bfloat16)
    return pick_head(value, ones, first, half)


def only_head(value, first, half):
    return pick_head(value, jnp.zeros(value.shape, jnp.bfloat16), first, half)


def norm_return(grad_in, raw, gain, half, turn):
    same = pair_matrix(True, half)
    inv = lax.rsqrt(head_sums(raw * raw, same) * (1.0 / half) + EPSILON)
    normed = raw * inv
    back = grad_in.astype(jnp.bfloat16).astype(jnp.float32)
    if turn is not None:
        back = back * turn[0][...] - swap_quarters(back, half) * turn[1][...]
    scaled = back * gain
    mean = head_sums(scaled * normed, same) * (1.0 / half)
    stat = jnp.sum(back * normed, axis=0, keepdims=True)
    return (inv * (scaled - normed * mean)).astype(jnp.bfloat16), stat


def score_grads(key_aug, val_aug, q_aug, o_aug, keep):
    probs = jnp.exp(nt_dot(key_aug, q_aug))
    if keep is not None:
        probs = jnp.where(keep, probs, 0.0)
    return probs.astype(jnp.bfloat16), (probs * nt_dot(val_aug, o_aug)).astype(jnp.bfloat16)


def cross_back_kernel(
    half,
    block,
    len_ref,
    query_ref,
    tkv_ref,
    text_ref,
    cross_ref,
    lse_ref,
    dmix_ref,
    gain_ref,
    tanh_ref,
    dq_ref,
    dtext_ref,
    stat_ref,
    qs_ref,
    os_ref,
    dk_ref,
    dv_ref,
):
    f32, bf16 = jnp.float32, jnp.bfloat16
    rows, caps = query_ref.shape[0], tkv_ref.shape[0]
    grad_f = dmix_ref[...].astype(f32)
    other = (grad_f * tanh_ref[0:1]).astype(bf16)
    delta = three_parts(
        -head_sums(other.astype(f32) * cross_ref[...], pair_matrix(False, half)), half
    )
    lse = three_parts(-lse_ref[...], half)
    query = query_ref[...] * jnp.asarray(half**-0.5, bf16)
    tkey, tval = tkv_ref[:, :LANES], tkv_ref[:, LANES:]
    for head in range(2):
        qs_ref[head] = pick_head(query, lse, head == 0, half)
        os_ref[head] = pick_head(other, delta, head == 0, half)
    key_aug = [with_ones(tkey, h == 0, half) for h in range(2)]
    val_aug = [with_ones(tval, h == 0, half) for h in range(2)]
    key_only = [only_head(tkey, h == 0, half) for h in range(2)]
    dk_ref[...] = jnp.zeros_like(dk_ref)
    dv_ref[...] = jnp.zeros_like(dv_ref)
    keep = lax.broadcasted_iota(jnp.int32, (caps, block), 0) < len_ref[0]

    def step(i, _):
        here = pl.ds(pl.multiple_of(i * block, block), block)
        dq = jnp.zeros((block, LANES), f32)
        for head in range(2):
            q_aug, o_aug = qs_ref[head, here], os_ref[head, here]
            probs, grads = score_grads(key_aug[head], val_aug[head], q_aug, o_aug, keep)
            dv_ref[...] += jnp.dot(
                probs, only_head(o_aug, head == 0, half), preferred_element_type=f32
            )
            dk_ref[...] += jnp.dot(
                grads, only_head(q_aug, head == 0, half), preferred_element_type=f32
            )
            dq += tn_dot(grads, key_only[head])
        dq_ref[here, :] = dq * half**-0.5
        return 0

    lax.fori_loop(0, rows // block, step, 0)
    res, stat_t = norm_return(dk_ref[...], text_ref[...], gain_ref[2:3], half, None)
    dtext_ref[:, :LANES] = res
    dtext_ref[:, LANES:] = dv_ref[...].astype(bf16)
    stat_x = jnp.sum(grad_f * cross_ref[...], axis=0, keepdims=True)
    stat_ref[...] = jnp.concatenate([stat_t, stat_x, jnp.zeros((6, LANES), f32)], axis=0)


def self_back_kernel(
    half,
    block,
    query_ref,
    key_ref,
    val_ref,
    rawq_ref,
    rawk_ref,
    own_ref,
    lse_ref,
    dmix_ref,
    dqc_ref,
    cos_ref,
    sin_ref,
    gain_ref,
    dqkv_ref,
    stat_ref,
    qs_ref,
    os_ref,
    dq_ref,
    dk_ref,
    dv_ref,
):
    f32, bf16 = jnp.float32, jnp.bfloat16
    rows = query_ref.shape[0]
    grad = dmix_ref[...]
    delta = three_parts(
        -head_sums(grad.astype(f32) * own_ref[...], pair_matrix(False, half)), half
    )
    lse = three_parts(-lse_ref[...], half)
    query = query_ref[...] * jnp.asarray(half**-0.5, bf16)
    key, value = key_ref[...], val_ref[...]
    for head in range(2):
        qs_ref[head] = pick_head(query, lse, head == 0, half)
        os_ref[head] = pick_head(grad, delta, head == 0, half)
    key_aug = [with_ones(key, h == 0, half) for h in range(2)]
    val_aug = [with_ones(value, h == 0, half) for h in range(2)]
    key_only = [only_head(key, h == 0, half) for h in range(2)]
    dk_ref[...] = jnp.zeros_like(dk_ref)
    dv_ref[...] = jnp.zeros_like(dv_ref)

    def step(i, _):
        here = pl.ds(pl.multiple_of(i * block, block), block)
        dq = jnp.zeros((block, LANES), f32)
        for head in range(2):
            q_aug, o_aug = qs_ref[head, here], os_ref[head, here]
            probs, grads = score_grads(key_aug[head], val_aug[head], q_aug, o_aug, None)
            dv_ref[...] += jnp.dot(
                probs, only_head(o_aug, head == 0, half), preferred_element_type=f32
            )
            dk_ref[...] += jnp.dot(
                grads, only_head(q_aug, head == 0, half), preferred_element_type=f32
            )
            dq += tn_dot(grads, key_only[head])
        dq_ref[here, :] = dqc_ref[here, :] + dq * half**-0.5
        return 0

    lax.fori_loop(0, rows // block, step, 0)
    turn = (cos_ref, sin_ref)
    res, stat_q = norm_return(dq_ref[...], rawq_ref[...], gain_ref[0:1], half, turn)
    dqkv_ref[:, :LANES] = res
    res, stat_k = norm_return(dk_ref[...], rawk_ref[...], gain_ref[1:2], half, turn)
    dqkv_ref[:, LANES : 2 * LANES] = res
    dqkv_ref[:, 2 * LANES :] = dv_ref[...].astype(bf16)
    stat_ref[...] = jnp.concatenate([stat_q, stat_k, jnp.zeros((6, LANES), f32)], axis=0)


def lane_block(rows, scale, shift):
    return pl.BlockSpec((rows, LANES), lambda p: (0, scale * p + shift))


def fixed_block(rows):
    return pl.BlockSpec((rows, LANES), lambda p: (0, 0))


def cross_back(cap_len, query, tkv, text, cross, lse, dmix, tables, half):
    gains, tanh_lanes = tables[2], tables[3]
    rows, caps = query.shape[0], text.shape[0]
    width = dmix.shape[1]
    f32, bf16 = jnp.float32, jnp.bfloat16
    return pl.pallas_call(
        functools.partial(cross_back_kernel, half, min(512, rows)),
        grid=(width // LANES,),
        in_specs=[
            pl.BlockSpec(memory_space=pltpu.SMEM),
            lane_block(rows, 1, 0),
            pl.BlockSpec((caps, 2 * LANES), lambda p: (0, p)),
            lane_block(caps, 2, 0),
            lane_block(rows, 1, 0),
            lane_block(rows, 2, 1),
            lane_block(rows, 1, 0),
            fixed_block(8),
            lane_block(8, 1, 0),
        ],
        out_specs=[
            lane_block(rows, 1, 0),
            pl.BlockSpec((caps, 2 * LANES), lambda p: (0, p)),
            lane_block(8, 1, 0),
        ],
        out_shape=[
            jax.ShapeDtypeStruct((rows, width), f32),
            jax.ShapeDtypeStruct((caps, 2 * width), bf16),
            jax.ShapeDtypeStruct((8, width), f32),
        ],
        scratch_shapes=[pltpu.VMEM((2, rows, LANES), bf16)] * 2
        + [pltpu.VMEM((caps, LANES), f32)] * 2,
        compiler_params=pltpu.CompilerParams(vmem_limit_bytes=40 * 2**20),
        cost_estimate=LIGHT,
        name="cross_bwd",
    )(cap_len, query, tkv, text, cross, lse, dmix, gains, tanh_lanes)


def self_back(window, query, kv, raw, own, lse, dmix, dq_cross, tables, half):
    cosine, sine, gains, _ = tables
    first, pairs = window
    rows = raw.shape[0]
    width = pairs * LANES
    f32, bf16 = jnp.float32, jnp.bfloat16
    return pl.pallas_call(
        functools.partial(self_back_kernel, half, min(512, rows)),
        grid=(pairs,),
        in_specs=[
            lane_block(rows, 1, first),
            lane_block(rows, 2, 2 * first),
            lane_block(rows, 2, 2 * first + 1),
            lane_block(rows, 3, 3 * first),
            lane_block(rows, 3, 3 * first + 1),
            lane_block(rows, 1, first),
            lane_block(rows, 2, 2 * first),
            lane_block(rows, 1, first),
            lane_block(rows, 1, first),
            fixed_block(rows),
            fixed_block(rows),
            fixed_block(8),
        ],
        out_specs=[pl.BlockSpec((rows, 3 * LANES), lambda p: (0, p)), lane_block(8, 1, 0)],
        out_shape=[
            jax.ShapeDtypeStruct((rows, 3 * width), bf16),
            jax.ShapeDtypeStruct((8, width), f32),
        ],
        scratch_shapes=[pltpu.VMEM((2, rows, LANES), bf16)] * 2
        + [pltpu.VMEM((rows, LANES), f32)] * 3,
        compiler_params=pltpu.CompilerParams(vmem_limit_bytes=50 * 2**20),
        cost_estimate=LIGHT,
        name="self_bwd",
    )(query, kv, kv, raw, raw, own, lse, dmix, dq_cross, cosine, sine, gains)


def feed_kernel(x_ref, grad_ref, gate_ref, up_ref, down_ref, *refs):
    f32, bf16 = jnp.float32, jnp.bfloat16
    hidden_ref, both_ref = refs[-2:]
    gate = jnp.dot(x_ref[...], gate_ref[...], preferred_element_type=f32)
    up = jnp.dot(x_ref[...], up_ref[...], preferred_element_type=f32)
    dhidden = jnp.dot(grad_ref[...], down_ref[...], preferred_element_type=f32)
    sig = 1.0 / (1.0 + jnp.exp(-gate))
    act = gate * sig
    hidden_ref[...] = (act * up).astype(bf16)
    tile = gate_ref.shape[1]
    both_ref[:, :tile] = (dhidden * up * sig * (1.0 + gate * (1.0 - sig))).astype(bf16)
    both_ref[:, tile:] = (dhidden * act).astype(bf16)


def feed_forward(part, x, grad, weights, units, tile, kept=()):
    count, depth = x.shape
    rows = grad.shape[0]
    blocks = units // tile
    bf16 = jnp.bfloat16

    def cols(scale, shift):
        return pl.BlockSpec((depth, tile), lambda j: (0, scale * j + shift))

    return pl.pallas_call(
        feed_kernel,
        grid=(blocks,),
        in_specs=[
            pl.BlockSpec((count, depth), lambda j: (0, 0)),
            pl.BlockSpec((count, depth), lambda j: (part, 0)),
            cols(2, 0),
            cols(2, 1),
            cols(1, 2 * blocks),
        ]
        + [pl.BlockSpec(memory_space=pl.ANY)] * len(kept),
        out_specs=[
            pl.BlockSpec((count, tile), lambda j: (part, j)),
            pl.BlockSpec((count, 2 * tile), lambda j: (part, j)),
        ],
        out_shape=[
            jax.ShapeDtypeStruct((rows, units), bf16),
            jax.ShapeDtypeStruct((rows, 2 * units), bf16),
        ],
        input_output_aliases={5 + n: n for n in range(len(kept))},
        compiler_params=pltpu.CompilerParams(vmem_limit_bytes=58 * 2**20),
        cost_estimate=LIGHT,
        name="feed_forward",
    )(x, grad, weights, weights, weights, *kept)


def outer_kernel(size, bits, me_ref, left_ref, right_ref, keep_ref, away_ref, total_ref):
    total_ref[...] = tn_dot(left_ref[...], right_ref[...])
    rows = keep_ref.shape[0] // (size // 2)
    for place in range(size):
        slot = sum(((place >> (len(bits) - 1 - k)) & 1) << bit for k, bit in enumerate(bits))
        start = pl.multiple_of((me_ref[0] ^ slot) * rows, 16)
        block = total_ref[pl.ds(start, rows), :].astype(jnp.bfloat16)
        out_ref = keep_ref if place < size // 2 else away_ref
        spot = place % (size // 2)
        out_ref[spot * rows : (spot + 1) * rows, :] = block


def outer_grads(me, left, right, size, bits, tile):
    tokens, depth = left.shape
    cols = right.shape[1]
    half = jax.ShapeDtypeStruct((depth // 2, cols), jnp.bfloat16)
    return pl.pallas_call(
        functools.partial(outer_kernel, size, bits),
        grid=(cols // tile,),
        in_specs=[
            pl.BlockSpec(memory_space=pltpu.SMEM),
            pl.BlockSpec((tokens, depth), lambda j: (0, 0)),
            pl.BlockSpec((tokens, tile), lambda j: (0, j)),
        ],
        out_specs=[pl.BlockSpec((depth // 2, tile), lambda j: (0, j))] * 2,
        out_shape=[half, half],
        scratch_shapes=[pltpu.VMEM((depth, tile), jnp.float32)],
        compiler_params=pltpu.CompilerParams(vmem_limit_bytes=50 * 2**20),
        cost_estimate=LIGHT,
        name="outer_grads",
    )(me, left, right)


def product_kernel(turned, has_add, *refs):
    left_ref, right_ref = refs[:2]
    dot = nt_dot if turned else (lambda a, b: jnp.dot(a, b, preferred_element_type=jnp.float32))
    total = dot(left_ref[...], right_ref[...])
    if has_add:
        total = total + refs[2][...].astype(jnp.float32)
    low = 0
    for out_ref in refs[2 + has_add :]:
        count = out_ref.shape[0]
        out_ref[...] = total[low : low + count].astype(out_ref.dtype)
        low += count


def product(left, right, cols, tile, dtype, turned=False, shift=0, add=None, part=(0, 1), cut=0):
    depth = left.shape[1]
    rows = left.shape[0] // part[1]
    counts = [cut, rows - cut] if cut else [rows]
    if turned:
        right_block = pl.BlockSpec((tile, depth), lambda j: (j, shift))
    else:
        right_block = pl.BlockSpec((depth, tile), lambda j: (0, j + shift))
    in_specs = [pl.BlockSpec((rows, depth), lambda j: (part[0], 0)), right_block]
    if add is not None:
        in_specs.append(pl.BlockSpec((rows, tile), lambda j: (0, j)))
    outs = pl.pallas_call(
        functools.partial(product_kernel, turned, add is not None),
        grid=(cols // tile,),
        in_specs=in_specs,
        out_specs=[pl.BlockSpec((count, tile), lambda j: (0, j)) for count in counts],
        out_shape=[jax.ShapeDtypeStruct((count, cols), dtype) for count in counts],
        compiler_params=pltpu.CompilerParams(vmem_limit_bytes=58 * 2**20),
        cost_estimate=LIGHT,
        name="product",
    )(left, right, *([] if add is None else [add]))
    return outs if cut else outs[0]


def gated(value, *tokens):
    return lax.optimization_barrier((value,) + tokens)[0]


def flip_perm(size, bit):
    return [(i, i ^ bit) for i in range(size)]


class SmallScatter:
    def __init__(self, value, size):
        self.value, self.size, self.bit = value, size, 0

    def left(self):
        return self.value.shape[0] > 1

    def hop(self, *tokens):
        if not self.left():
            return None
        index = lax.axis_index("dp")
        value = gated(self.value, *tokens) if tokens else self.value
        pairs = value.reshape(value.shape[0] // 2, 2, value.shape[1])
        upper = (index >> self.bit) % 2 == 1
        away = jnp.where(upper, pairs[:, 0], pairs[:, 1])
        came = lax.ppermute(away, "dp", flip_perm(self.size, 1 << self.bit))
        self.value = jnp.where(upper, pairs[:, 1], pairs[:, 0]) + came
        self.bit += 1
        return came


class Halving:
    def __init__(self, size, bits, keep, away):
        self.size, self.bits, self.stage = size, bits, 0
        self.terms = [keep]
        self.whole = [keep]
        self.out = away

    def start(self):
        bit = self.bits[self.stage]
        self.came = lax.ppermute(self.out, "dp", flip_perm(self.size, 1 << bit))
        self.stage += 1

    def land(self, *tokens):
        self.came = gated(self.came, *tokens)
        return self.came

    def finish(self, *tokens):
        came = gated(self.came, *tokens) if tokens else self.came
        self.terms.append(came)
        self.whole.append(came)
        rows = self.terms[-1].shape[0]
        last = self.stage == len(self.bits)
        half = rows if last else rows // 2
        low = 0 if last else half
        total = sum(term[low : low + half].astype(jnp.float32) for term in self.terms)
        self.out = total if last else total.astype(jnp.bfloat16)
        self.terms = [term[:half] for term in self.terms]
        return self.out

    def drain(self, *tokens):
        while self.stage < len(self.bits):
            self.finish(*tokens)
            self.start()
            tokens = ()
        came = gated(self.came, *tokens) if tokens else self.came
        return self.whole + [came]


def swap_start(part, size, chunks):
    step = part.shape[0] // chunks
    own = [part[i * step : (i + 1) * step] for i in range(chunks)]
    if size == 2:
        return own, [lax.ppermute(o, "tensor", flip_perm(size, 1)) for o in own]
    return own, [lax.psum(o, "tensor") for o in own]


def swap_end(own, came, size):
    f32 = jnp.float32
    both = [o.astype(f32) + c.astype(f32) if size == 2 else c.astype(f32) for o, c in zip(own, came)]
    return jnp.concatenate(both, axis=0) if len(both) > 1 else both[0]


def small_gather(value, name, size, tokens=(), steps=None):
    index = lax.axis_index(name)
    for k in range(size.bit_length() - 1):
        bit = 1 << k
        if k < len(tokens):
            value = gated(value, tokens[k])
        came = lax.ppermute(value, name, flip_perm(size, bit))
        upper = (index // bit) % 2 == 1
        value = jnp.where(
            upper, jnp.concatenate([came, value], 0), jnp.concatenate([value, came], 0)
        )
        if steps is not None:
            steps.append(value)
    return value


class Hops:
    def __init__(self, value, size):
        self.value, self.size, self.bit = value, size, 0

    def start(self, *tokens):
        if self.bit < self.size.bit_length() - 1:
            value = gated(self.value, *tokens) if tokens else self.value
            self.came = lax.ppermute(value, "dp", flip_perm(self.size, 1 << self.bit))

    def finish(self, *tokens):
        if self.bit < self.size.bit_length() - 1:
            came = gated(self.came, *tokens) if tokens else self.came
            upper = (lax.axis_index("dp") >> self.bit) % 2 == 1
            self.value = jnp.where(
                upper,
                jnp.concatenate([came, self.value], 0),
                jnp.concatenate([self.value, came], 0),
            )
            self.bit += 1
        return self.value

    def drain(self):
        while self.bit < self.size.bit_length() - 1:
            self.start()
            self.finish()
        return self.value


def small_sum(value, name, size):
    bit = 1
    while bit < size:
        value = value + lax.ppermute(value, name, flip_perm(size, bit))
        bit *= 2
    return value


def tensor_scatter(part, size):
    if size == 2:
        index = lax.axis_index("tensor")
        width = part.shape[1] // 2
        away = lax.dynamic_slice_in_dim(part, (1 - index) * width, width, 1)
        kept = lax.dynamic_slice_in_dim(part, index * width, width, 1)
        came = lax.ppermute(away, "tensor", flip_perm(size, 1))
        return kept.astype(jnp.float32) + came.astype(jnp.float32)
    return lax.psum_scatter(part, "tensor", scatter_dimension=1, tiled=True).astype(jnp.float32)


def weave_kernel(tile, plan, *refs):
    out_ref = refs[-1]
    out_ref[...] = jnp.zeros_like(out_ref)
    for target, source, low, wide, turned in plan:
        if turned:
            out_ref[:, target : target + wide] = refs[source][low : low + wide, :].T
        else:
            out_ref[:, target : target + wide] = refs[source][:, low : low + wide]


def weave(arrays, tile, last=None):
    rows, cols = arrays[0].shape
    count = -(-cols // tile)
    plan = []
    target = 0
    for i in range(count):
        for source in range(len(arrays)):
            plan.append((target, source, i * tile, min(tile, cols - i * tile), False))
            target += tile
    operands = list(arrays)
    if last is not None:
        plan.append((target, len(arrays), 0, last.shape[0], True))
        target += last.shape[0] + -last.shape[0] % tile
        operands.append(last)
    return pl.pallas_call(
        functools.partial(weave_kernel, tile, plan),
        out_shape=jax.ShapeDtypeStruct((rows, target), arrays[0].dtype),
        compiler_params=pltpu.CompilerParams(vmem_limit_bytes=30 * 2**20),
        cost_estimate=LIGHT,
        name="weave",
    )(*operands)


def gather_sum_kernel(tile, sizes, count, *refs):
    outs = refs[-count:]
    cols = outs[0].shape[1]
    low = 0
    base = 0
    for size in sizes:
        total = refs[low][...].astype(jnp.float32)
        for ref in refs[low + 1 : low + size]:
            total = total + ref[...].astype(jnp.float32)
        low += size
        tiles = total.shape[1] // (tile * count)
        for i in range(tiles):
            start = base + i * tile
            wide = min(tile, cols - start)
            for n, out_ref in enumerate(outs):
                at = (i * count + n) * tile
                out_ref[:, start : start + wide] = total[:, at : at + wide]
        base += tiles * tile


def gather_sum(groups, tile, count, cols):
    rows = groups[0][-1].shape[0]
    terms = [term for group in groups for term in group]
    wide = sum(term.shape[1] for term in terms) * 2 + count * cols * 4
    block = rows
    while block * wide > 12 * 2**20 and block % 32 == 0:
        block //= 2
    return pl.pallas_call(
        functools.partial(gather_sum_kernel, tile, [len(group) for group in groups], count),
        grid=(rows // block,),
        in_specs=[pl.BlockSpec((block, term.shape[1]), lambda r: (r, 0)) for term in terms],
        out_specs=[pl.BlockSpec((block, cols), lambda r: (r, 0))] * count,
        out_shape=[jax.ShapeDtypeStruct((rows, cols), jnp.float32)] * count,
        compiler_params=pltpu.CompilerParams(vmem_limit_bytes=58 * 2**20),
        cost_estimate=LIGHT,
        name="gather_sum",
    )(*terms)


def fold_plan(rows, blocks, tall):
    plan = []
    for block in range(blocks):
        low = block * rows
        while low < (block + 1) * rows:
            high = min((block + 1) * rows, (low // tall + 1) * tall)
            plan.append((block, low - block * rows, low % tall, low // tall, high - low))
            low = high
    return plan


def pack_kernel(rows, tall, wide, plans, *refs):
    out_ref = refs[-1]
    out_ref[...] = jnp.zeros_like(out_ref)
    text_plan, rest_plan = plans
    for target, source, low, width, _ in text_plan:
        out_ref[:, target : target + width] = refs[source][:, low : low + width]
    for block, at, row, col, count in fold_plan(rows, len(rest_plan), tall):
        source, low, width, turned = rest_plan[block]
        if turned:
            piece = refs[source][low : low + width, :].T
        else:
            piece = refs[source][:, low : low + width]
        start = wide + col * LANES
        out_ref[row : row + count, start : start + width] = piece[at : at + count]


def pack_weights(text, attention, last):
    tall, cols = text[0].shape
    rows = attention[0].shape[0]
    tiles = -(-cols // LANES)
    text_plan = []
    rest_plan = []
    for i in range(tiles):
        width = min(LANES, cols - i * LANES)
        for n in range(len(text)):
            target = (i * len(text) + n) * LANES
            text_plan.append((target, n, i * LANES, width, False))
        for n in range(len(attention)):
            rest_plan.append((len(text) + n, i * LANES, width, False))
    for i in range(tiles):
        width = min(LANES, cols - i * LANES)
        rest_plan.append((len(text) + len(attention), i * LANES, width, True))
    wide = tiles * len(text) * LANES
    folded = len(rest_plan) * rows // tall * LANES
    return pl.pallas_call(
        functools.partial(pack_kernel, rows, tall, wide, (text_plan, rest_plan)),
        out_shape=jax.ShapeDtypeStruct((tall, wide + folded), text[0].dtype),
        compiler_params=pltpu.CompilerParams(vmem_limit_bytes=30 * 2**20),
        cost_estimate=LIGHT,
        name="pack_weights",
    )(*text, *attention, last)


def unfold_kernel(rows, tall, blocks, size, edge, left_ref, *refs):
    full_ref, raw_ref = refs[-2:]
    plan = fold_plan(rows, blocks, tall)

    def place(d, _):
        start = pl.multiple_of(d * rows, 16)
        for block, at, row, col, count in plan:
            full_ref[pl.ds(start + at, count), block * LANES : (block + 1) * LANES] = refs[col][
                d, row : row + count, :
            ]
        return 0

    lax.fori_loop(0, size, place, 0)
    last = pl.program_id(0) == pl.num_programs(0) - 1

    @pl.when(jnp.logical_not(last))
    def _():
        raw_ref[...] = jnp.dot(left_ref[...], full_ref[...], preferred_element_type=jnp.float32)

    @pl.when(last)
    def _():
        raw_ref[:, :edge] = jnp.dot(
            left_ref[...], full_ref[:, :edge], preferred_element_type=jnp.float32
        )


def unfold_product(left, packed, rows, tall, blocks, used, size):
    period = math.lcm(rows, tall)
    span, folds = period // rows, period // tall
    steps = blocks // span
    skip = packed.shape[1] // LANES - folds * steps
    tokens = left.shape[0]
    view = packed.reshape(size, tall, packed.shape[1])
    return pl.pallas_call(
        functools.partial(
            unfold_kernel, rows, tall, span, size, (used - (steps - 1) * span) * LANES
        ),
        grid=(steps,),
        in_specs=[pl.BlockSpec(left.shape, lambda j: (0, 0))]
        + [
            pl.BlockSpec((size, tall, LANES), lambda j, k=k: (0, 0, skip + folds * j + k))
            for k in range(folds)
        ],
        out_specs=[
            pl.BlockSpec((size * rows, span * LANES), lambda j: (0, j)),
            pl.BlockSpec((tokens, span * LANES), lambda j: (0, j)),
        ],
        out_shape=[
            jax.ShapeDtypeStruct((size * rows, blocks * LANES), packed.dtype),
            jax.ShapeDtypeStruct((tokens, blocks * LANES), jnp.float32),
        ],
        compiler_params=pltpu.CompilerParams(vmem_limit_bytes=58 * 2**20),
        cost_estimate=LIGHT,
        name="unfold_product",
    )(left, *[view] * folds)


def rotary_tables(row_pos, col_pos, quarter, repeat):
    frequency = jnp.exp(-math.log(10000.0) * jnp.arange(quarter, dtype=jnp.float32) / quarter)
    angles = jnp.concatenate(
        [
            row_pos.astype(jnp.float32)[:, None] * frequency,
            col_pos.astype(jnp.float32)[:, None] * frequency,
        ],
        axis=1,
    )
    sine = jnp.sin(angles)
    return jnp.tile(jnp.cos(angles), (1, 2 * repeat)), jnp.tile(
        jnp.concatenate([-sine, sine], axis=1), (1, repeat)
    )


def local(
    size,
    groups,
    latents,
    cotangent,
    caption,
    caption_lens,
    patch_row,
    patch_col,
    timestep,
    query_proj,
    key_proj,
    value_proj,
    output_proj,
    textkey_proj,
    textval_proj,
    gate_proj,
    up_proj,
    down_proj,
    modulation,
    attn_gain,
    ffn_gain,
    query_gain,
    key_gain,
    textkey_gain,
    cross_gate,
):
    f32, bf16 = jnp.float32, jnp.bfloat16
    rows_w, chan = query_proj.shape
    units = gate_proj.shape[1]
    head_part = query_gain.shape[0]
    head_dim = head_part * size
    heads_here = chan // head_dim
    model_dim = latents.shape[1]
    padded = chan + -chan % LANES
    pairs = padded // LANES
    dp_index = lax.axis_index("dp")
    tensor_index = lax.axis_index("tensor")

    small = jnp.concatenate(
        [
            attn_gain.astype(f32),
            ffn_gain.astype(f32),
            query_gain.astype(f32),
            key_gain.astype(f32),
            textkey_gain.astype(f32),
            timestep.astype(f32),
        ]
    )[None]
    steps = []
    small_all = small_gather(small, "dp", size, (), steps)
    packed = pack_weights(
        [textkey_proj, textval_proj], [query_proj, key_proj, value_proj], output_proj
    )
    packed_set = lax.all_gather(packed, "dp", axis=0, tiled=True)

    cuts = [rows_w, 2 * rows_w, 2 * rows_w + head_part]
    gain_one = small_all[:, : cuts[0]].reshape(-1)
    gain_two = small_all[:, cuts[0] : cuts[1]].reshape(-1)
    gain_query = small_all[:, cuts[1] : cuts[2]].reshape(-1)
    gain_key = small_all[:, cuts[2] : cuts[2] + head_part].reshape(-1)
    gain_text = small_all[:, cuts[2] + head_part : cuts[2] + 2 * head_part].reshape(-1)
    steps_all = small_all[:, cuts[2] + 2 * head_part :].reshape(-1)
    embed_rows = modulation.shape[0]
    embed_dim = embed_rows * size
    embed_all = time_embed(steps_all, embed_dim)
    cond_all = (embed_all * jax.nn.sigmoid(embed_all)).astype(bf16)
    cond_here = lax.dynamic_slice_in_dim(cond_all, dp_index * embed_rows, embed_rows, 1)
    mod_part = jnp.dot(cond_here, modulation, preferred_element_type=f32)
    mod_sums = SmallScatter(mod_part, size)
    while mod_sums.left():
        mod_sums.hop()
    mod_here = mod_sums.value
    mod_all = small_gather(mod_here, "tensor", groups).reshape(1, -1)
    tile = 256
    blocks = units // tile
    gate_l, up_l, down_l = gated((gate_proj, up_proj, down_proj), small_all)
    third = weave([gate_l, up_l], tile, down_l)
    ffn_set = lax.all_gather(gated(third, small_all), "dp", axis=0, tiled=True)
    scale_one = mod_all[:, 0:model_dim]
    gate_one = jnp.tanh(mod_all[:, model_dim : 2 * model_dim])
    scale_two = mod_all[:, 2 * model_dim : 3 * model_dim]
    gate_two = jnp.tanh(mod_all[:, 3 * model_dim : 4 * model_dim])
    tanh_cross = jnp.tanh(cross_gate.astype(f32))
    tanh_lanes = jnp.pad(jnp.repeat(tanh_cross, head_dim), (0, padded - chan))
    tanh_lanes = jnp.broadcast_to(tanh_lanes[None], (8, padded))
    per_tile = LANES // head_dim
    gain_lanes = jnp.pad(
        jnp.tile(jnp.stack([gain_query, gain_key, gain_text]), (1, per_tile)), ((0, 5), (0, 0))
    )
    cosine, sine = rotary_tables(patch_row[0], patch_col[0], head_dim // 4, per_tile)
    tables = (cosine, sine, gain_lanes, tanh_lanes)

    resid_in = latents.astype(f32)
    factor_one = inv_rms(resid_in)
    normed_one = resid_in * factor_one
    attn_in = (normed_one * gain_one * (1.0 + scale_one)).astype(bf16)
    grad_out = cotangent.astype(f32)
    grad_ffn = (gate_two * grad_out).astype(bf16)
    full_text = gated(packed_set, attn_in, grad_ffn)
    full_qkvo, qkv_raw = unfold_product(
        attn_in, full_text, rows_w, packed.shape[0], 4 * pairs, 3 * pairs, size
    )
    cap_in = caption[0]
    text_raw = product(gated(cap_in, qkv_raw), full_text, 2 * padded, 256, f32)
    mixed_a, query_bf, own_out, cross_out, lse, kv_bf, tkv_bf = attend_rows(
        0, caption_lens, qkv_raw, text_raw, tables, head_dim
    )
    part_a = product(mixed_a, full_qkvo, model_dim, 512, bf16, True, 3)
    own_a, came_a = swap_start(part_a, groups, 1)
    kept = gated((query_bf, own_out, cross_out, lse, kv_bf, tkv_bf), part_a)
    mixed_b, query_bf, own_out, cross_out, lse = attend_rows(
        1, caption_lens, qkv_raw, text_raw, tables, head_dim, kept
    )
    attn_part = product(mixed_b, full_qkvo, model_dim, 512, bf16, True, 3)
    mixed_heads = jnp.concatenate([mixed_a, mixed_b], axis=0)
    mod_set = lax.all_gather(gated(modulation, qkv_raw), "dp", axis=0, tiled=True)

    came_a = gated(came_a, attn_part)
    own_b, came_b = swap_start(gated(attn_part, came_a), groups, 1)
    half_rows = grad_ffn.shape[0] // 2
    full_ffn = gated(ffn_set, attn_part)
    gain_mul = gain_two * (1.0 + scale_two)

    def feed_input(resid, own, came):
        attn_sum = swap_end(own, came, groups)
        total = resid + gate_one * attn_sum
        factor = inv_rms(total)
        normed = total * factor
        return attn_sum, total, factor, normed, (normed * gain_mul).astype(bf16)

    resid_a, resid_b = resid_in[:half_rows], resid_in[half_rows:]
    attn_out_a, residual_a, factor_a, normed_a, feed_a = feed_input(resid_a, own_a, came_a)
    kept = feed_forward(0, feed_a, grad_ffn, full_ffn, units, tile)
    dffn_one = product(kept[1], full_ffn, model_dim, 512, bf16, True, 0, None, (0, 2))
    one_own, one_came = swap_start(dffn_one, groups, 1)
    came_b = gated(came_b, dffn_one)
    attn_out_b, residual_b, factor_b, normed_b, feed_b = feed_input(resid_b, own_b, came_b)
    hidden, dboth = feed_forward(
        1, feed_b, grad_ffn, full_ffn, units, tile, gated(kept, dffn_one)
    )
    dffn_two = product(dboth, full_ffn, model_dim, 512, bf16, True, 0, None, (1, 2))
    ffn_in = jnp.concatenate([feed_a, feed_b], axis=0)
    me = dp_index.astype(jnp.int32)[None]
    depth_bits = list(range(2, size.bit_length() - 1))
    side_first = [0, 1] + depth_bits
    line_first = [0, 2, 1] + depth_bits[1:]

    def staged(left, right, bits, tile_cols):
        return Halving(size, bits, *outer_grads(me, left, right, size, bits, tile_cols))

    down = staged(grad_ffn, gated(hidden, dffn_two), line_first, 512)
    down.start()
    one_came = gated(one_came, down.out)
    two_own, two_came = swap_start(gated(dffn_two, one_came), groups, 1)
    grown = staged(ffn_in, gated(dboth, down.out, one_came), side_first, 512)
    grown.start()
    ffn_part = product(gated(hidden, grown.out, mod_set), full_ffn, model_dim, 512, bf16, True, 2)
    grad_out_a, grad_out_b = grad_out[:half_rows], grad_out[half_rows:]

    def feed_back(grad, own, came, normed, factor, attn_sum):
        dffn = swap_end(own, came, groups)
        dres = grad + norm_back(dffn * gain_mul, normed, factor)
        sums_here = jnp.sum(dffn * normed, axis=0), jnp.sum(dres * attn_sum, axis=0)
        return dres, (gate_one * dres).astype(bf16), sums_here

    dres_a, grad_attn_a, sums_a = feed_back(
        grad_out_a, one_own, one_came, normed_a, factor_a, attn_out_a
    )
    dmix_a = product(
        gated(grad_attn_a, ffn_part), full_qkvo, padded, LANES, bf16, False, 3 * padded // LANES
    )
    two_came = gated(two_came, dmix_a)
    down.finish(two_came)
    down.start()
    grown.finish(down.out)
    grown.start()
    dres_b, grad_attn_b, sums_b = feed_back(
        grad_out_b, two_own, gated(two_came, grown.out), normed_b, factor_b, attn_out_b
    )
    dmix_b = product(grad_attn_b, full_qkvo, padded, LANES, bf16, False, 3 * padded // LANES)
    dmixed = jnp.concatenate([dmix_a, dmix_b], axis=0)
    grad_attn = jnp.concatenate([grad_attn_a, grad_attn_b], axis=0)
    weighed = sums_a[0] + sums_b[0]
    grad_gaintwo = weighed * (1.0 + scale_two[0])
    dscale_two = weighed * gain_two
    dgate_one = (sums_a[1] + sums_b[1]) * (1.0 - gate_one[0] ** 2)
    dresid = jnp.concatenate([dres_a, dres_b], axis=0)
    residual = jnp.concatenate([residual_a, residual_b], axis=0)
    ffn_own, ffn_came = swap_start(gated(ffn_part, dmixed), groups, 1)
    dq_cross, dtext, stats_c = cross_back(
        caption_lens, query_bf, tkv_bf, text_raw, cross_out, lse, dmixed, tables, head_dim
    )
    down.finish(dq_cross)
    down.start()
    text = staged(cap_in, gated(dtext, down.out), side_first, 256)
    grown.finish(text.out)
    grown.start()
    text.out = gated(text.out, grown.out)
    text.start()
    split = pairs - pairs // 2
    windows = [(0, split), (split, pairs - split)]
    common = (query_bf, kv_bf, qkv_raw, own_out, lse)
    dmixed_a = gated(dmixed, text.out)
    dqkv_a, stats_a = self_back(windows[0], *common, dmixed_a, dq_cross, tables, head_dim)
    down.finish(dqkv_a)
    down.start()
    grown.finish(down.out)
    grown.start()
    text.finish(grown.out)
    text.start()
    outp = staged(gated(grad_attn, text.out), mixed_heads, side_first, padded)
    outp.start()
    first_qkv = staged(attn_in, gated(dqkv_a, outp.out), side_first, 3 * LANES)
    edge = 3 * LANES * split
    even = pairs == 2 * split
    wide_a = full_qkvo if even else full_qkvo[:, :edge]
    wide_b = full_qkvo if even else full_qkvo[:, edge : 3 * padded]
    dattn_a = product(gated(dqkv_a, first_qkv.out), wide_a, model_dim, 512, f32, True)
    outp.finish(dattn_a)
    outp.start()
    dmixed_b = gated(dmixed, outp.out)
    dqkv_b, stats_b = self_back(windows[1], *common, dmixed_b, dq_cross, tables, head_dim)
    landed = (down.land(dqkv_b), grown.land(dqkv_b), gated(ffn_came, dqkv_b))
    ffn_came = landed[2]
    dqkv_l = gated(dqkv_b, *landed)
    cut = latents.shape[0] * 5 // 8
    top, low = product(
        dqkv_l, wide_b, model_dim, 512, bf16, True, int(even), dattn_a, (0, 1), cut
    )
    high_own, high_came = swap_start(top, groups, 1)
    first_qkv.out = gated(first_qkv.out, low)
    first_qkv.start()
    last_qkv = staged(attn_in, gated(dqkv_b, low), side_first, 3 * LANES)
    last_qkv.start()
    text.finish(last_qkv.out)
    text.start()
    first_qkv.finish(text.out)
    first_qkv.start()
    outp.finish(first_qkv.out)
    outp.start()
    last_qkv.finish(outp.out)
    last_qkv.start()
    caption_part = product(
        gated(dtext, last_qkv.out), full_text, cap_in.shape[1], 1024, bf16, True
    )
    grad_gate, grad_up = gather_sum([grown.drain(caption_part)], tile, 2, units)
    top_l, low_l, ffn_l = gated((top, low, ffn_part), grad_gate)
    weighed_part = jnp.sum(top_l.astype(f32) * normed_one[:cut], axis=0)
    weighed_part = weighed_part + jnp.sum(low_l.astype(f32) * normed_one[cut:], axis=0)
    gate_part = jnp.sum(grad_out * ffn_l.astype(f32), axis=0)
    stats = jnp.concatenate([stats_a, stats_b], axis=1)[:2]
    stat_sums = jnp.concatenate([stats, stats_c[:2]], axis=0)[:, :chan]
    stat_sums = jnp.sum(stat_sums.reshape(4, heads_here, head_dim), axis=(1,))
    xgate_rows = stats_c[1, :chan].reshape(heads_here, head_dim)
    xgate_here = jnp.sum(xgate_rows, axis=1) * (1.0 - tanh_cross**2)
    sums_part = jnp.concatenate([weighed_part, gate_part, stat_sums[:3].reshape(-1)])[None]
    sums = small_sum(sums_part, "tensor", groups)[0]
    high_came = gated(high_came, sums_part)
    base_own, base_came = swap_start(gated(low, high_came), groups, 1)
    sums = gated(sums, high_came)
    weighed_one, head_gains = sums[:model_dim], sums[2 * model_dim :]
    dgate_two = sums[model_dim : 2 * model_dim] * (1.0 - gate_two[0] ** 2)
    grad_gainone = weighed_one * (1.0 + scale_one[0])
    dscale_one = weighed_one * gain_one
    dmod_all = jnp.concatenate([dscale_one, dgate_one, dscale_two, dgate_two])
    cols_here = modulation.shape[1]
    dmod_here = lax.dynamic_slice_in_dim(dmod_all, tensor_index * cols_here, cols_here, 0)
    row = jnp.concatenate([dmod_here, grad_gainone, grad_gaintwo, head_gains, xgate_here])
    row = row.astype(bf16).astype(f32)[None]
    hops = Hops(row, size)
    hops.start()
    first_qkv.finish(row)
    first_qkv.start()
    last_qkv.finish(first_qkv.out)
    last_qkv.start()
    text.finish(last_qkv.out)
    text.start()
    hops.finish(text.out)
    hops.start()
    outp.finish(hops.value)
    outp.start()
    down_t = sum(term[:rows_w].astype(f32) for term in down.drain(outp.out))
    hops.finish(down_t)
    hops.start()
    ffn_out = swap_end(ffn_own, gated(ffn_came, hops.value), groups)
    output = (residual + gate_two * ffn_out).astype(bf16)
    first_qkv.finish(output)
    first_qkv.start()
    last_qkv.finish(first_qkv.out)
    last_qkv.start()
    hops.finish(last_qkv.out)
    hops.start()
    base_came = gated(base_came, hops.value)
    dcaption = tensor_scatter(gated(caption_part, base_came), groups)
    dattn_in = jnp.concatenate(
        [swap_end(high_own, high_came, groups), swap_end(base_own, base_came, groups)], axis=0
    )
    grad_latents = (
        dresid + norm_back(dattn_in * gain_one * (1.0 + scale_one), normed_one, factor_one)
    ).astype(bf16)
    embed_row = jnp.einsum(
        "bc,tc->bt", row[:, :cols_here].astype(bf16), mod_set, preferred_element_type=f32
    )
    grad_textkey, grad_textval = gather_sum([text.drain(grad_latents)], LANES, 2, chan)
    embed_sum = small_sum(embed_row, "tensor", groups)
    embed_own = lax.dynamic_slice_in_dim(embed_all, dp_index, 1, 0)
    sig_own = jax.nn.sigmoid(embed_own)
    dembed_all = embed_sum * (sig_own * (1.0 + embed_own * (1.0 - sig_own)))
    width = embed_dim // groups
    dembed = lax.dynamic_slice_in_dim(dembed_all, tensor_index * width, width, 1)
    output_t = sum(term[:rows_w].astype(f32) for term in outp.drain(grad_textkey))
    parts = [last_qkv.drain(output_t), first_qkv.drain(output_t)][::-1]
    grad_query, grad_key, grad_value = gather_sum(parts, LANES, 3, chan)

    hops.finish(grad_query)
    rows_set = hops.drain()
    dmod_set = rows_set[:, :cols_here].astype(bf16)
    gain_sums = jnp.sum(rows_set[:, cols_here:], axis=0)
    grad_modul = jnp.einsum("bt,bc->tc", cond_here, dmod_set, preferred_element_type=f32)

    def own_part(start, width):
        return lax.dynamic_slice_in_dim(gain_sums, start + dp_index * width, width, 0)

    heads_at = 2 * model_dim
    gate_at = heads_at + 3 * head_dim
    return (
        output,
        grad_latents,
        dcaption.astype(bf16)[None],
        dembed,
        grad_query,
        grad_key,
        grad_value,
        output_t[:, :chan].T,
        grad_textkey,
        grad_textval,
        grad_gate,
        grad_up,
        down_t.T,
        grad_modul,
        own_part(0, rows_w),
        own_part(model_dim, rows_w),
        own_part(heads_at, head_part),
        own_part(heads_at + head_dim, head_part),
        own_part(heads_at + 2 * head_dim, head_part),
        gain_sums[gate_at:],
    )


def solution(mesh):
    in_specs = (
        P("dp", None),
        P("dp", None),
        P("dp", None, None),
        P("dp"),
        P("dp", None),
        P("dp", None),
        P("dp"),
        P("dp", "tensor"),
        P("dp", "tensor"),
        P("dp", "tensor"),
        P("tensor", "dp"),
        P("dp", "tensor"),
        P("dp", "tensor"),
        P("dp", "tensor"),
        P("dp", "tensor"),
        P("tensor", "dp"),
        P("dp", "tensor"),
        P("dp"),
        P("dp"),
        P("dp"),
        P("dp"),
        P("dp"),
        P("tensor"),
    )
    out_specs = (
        P("dp", None),
        P("dp", None),
        P("dp", None, "tensor"),
        P("dp", "tensor"),
        P("dp", "tensor"),
        P("dp", "tensor"),
        P("dp", "tensor"),
        P("tensor", "dp"),
        P("dp", "tensor"),
        P("dp", "tensor"),
        P("dp", "tensor"),
        P("dp", "tensor"),
        P("tensor", "dp"),
        P("dp", "tensor"),
        P("dp"),
        P("dp"),
        P("dp"),
        P("dp"),
        P("dp"),
        P("tensor"),
    )
    bound = functools.partial(local, mesh.shape["dp"], mesh.shape["tensor"])
    return jax.shard_map(bound, mesh=mesh, in_specs=in_specs, out_specs=out_specs, check_vma=False)
```
